32 devices in a mesh: stream: 4 (over z), girth: 2 (over x), wall: 4 (over y, core).
Axes of the slice: x: 2, y: 2, z: 4, core: 2. Of those that a mesh axis runs over, the one named last changes fastest.
Arguments:
- state: float32 [6, 32, 32, 512], P(None, 'stream', 'girth', 'wall'), may hold values from -6 to 6
- advect: float32 [2, 32, 32], P(None, 'stream', 'girth'), may hold values from -5 to 5
- dtau: float32 [32, 32, 512], P('stream', 'girth', 'wall'), may hold values from 10 to 200
- viscosity: float32 [32, 32, 512], P('stream', 'girth', 'wall'), may hold values from 0.05 to 0.5
- mode_speed: float32 [6], replicated, may hold values from -2 to 2
- left_modes: float32 [6, 6], replicated, may hold values from -2.5 to 2.5
- right_modes: float32 [6, 6], replicated, may hold values from -2.5 to 2.5
- source_jac: float32 [6, 6], replicated, may hold values from -2.5 to 2.5
- elem_owner: int32 [64, 1], P(('stream', 'girth')), may hold values from 0 to 7; in each aligned block of 8 rows (0 to 7, 8 to 15, ...) at most 2 rows name the same one
- elem_tile: int32 [64], P(('stream', 'girth')), may hold values from 0 to 1
- elem_offset: float32 [64, 2], P(('stream', 'girth')), may hold values from 0 to 8
- elem_height: float32 [64], P(('stream', 'girth')), may hold values from 0 to 512
- elem_force: float32 [64, 3], P(('stream', 'girth')), may hold values from -180 to 180
- elem_width: float32 [64], P(('stream', 'girth')), may hold values from 1.5 to 4
Outputs:
- increment: float32 [6, 32, 32, 512], P(None, 'stream', 'girth', 'wall')
The draws below stay inside these ranges and needn't reach their ends.
Inputs may be any that keep to these rules, and one draw needn't show every extreme that they name: `elem_owner`: among the elements of one device, no owner block is named by more than 2 of them; some owner block is named by exactly 2.
All inputs are finite; a program needn't handle non-finite values.
Results may differ from the reference program's by a relative error of at most 0.00011.
Values sent between devices are 32-bit elements; how exact they have to be, the bound alone decides.
No kernel may reach another device: no remote copies, remote signals or barrier semaphores. Data moves between devices by JAX's collectives and lax.ppermute only.
A program may use at most 64 MiB of HBM per device.

```python
import math
import jax
import jax.numpy as jnp
import numpy as np
from jax import lax

EQ = 6
NW = 512
TILE = 8
CAP = 2
CS = 8
CG = 16
NE_DEV = 8
NS = 32
NG = 32
BLOCKS = 8
NE = 64
TILES = 2
N_GIRTH = 2


def place_ends(drawn, key, smallest, top_value):
    place = [jax.random.randint(jax.random.fold_in(key, axis), (), 0, length) for axis, length in enumerate(drawn.shape)]
    widest = drawn.shape.index(max(drawn.shape))
    beside = place[:widest] + [(place[widest] + 1) % drawn.shape[widest]] + place[widest + 1:]
    return drawn.at[tuple(place)].set(smallest).at[tuple(beside)].set(top_value)


def levels(own_key, extent, split, smallest, largest):
    level, own = 1.0, jax.random.fold_in(own_key, 6)
    for axis_at, parts in split:
        draws = jnp.exp(jax.random.uniform(jax.random.fold_in(own, axis_at), (parts,), jnp.float32, smallest / len(split), largest / len(split)))
        level = level * jnp.repeat(draws, extent[axis_at] // parts).reshape([-1 if axis == axis_at else 1 for axis in range(len(extent))])
    return level


def assign_block(stream_key, own, number, rows, amount, top, limit, lean):
    sequence = jax.random.permutation(stream_key, amount)
    heavy_load, common = portions_of(amount, rows * top, limit, lean, True), portions_of(amount, rows * top, limit, lean, False)
    places = jnp.arange(amount)

    def named(tallies, offset_by):
        used = int((tallies > 0).sum())
        fixed = max(1, used // 4)
        shifted = fixed + (places - fixed + offset_by * (used - fixed)) % max(1, amount - fixed)
        return jnp.zeros((amount,), jnp.int32).at[sequence[jnp.where(places < fixed, places, shifted)]].set(jnp.asarray(tallies, jnp.int32))

    tallies = jnp.where(number % 4 == 0, named(heavy_load, number // 4), named(common, number - number // 4 - 1))
    mixed = jax.random.permutation(jax.random.fold_in(own, 3), amount)
    donor, sink = mixed[0:amount // 2 * 2:2], mixed[1:amount // 2 * 2:2]
    slack = jnp.minimum(tallies[donor] - 1, limit - tallies[sink]) // 2
    slack = jnp.where((donor == sequence[0]) | (sink == sequence[0]) | (tallies[sink] == 0), 0, jnp.maximum(slack, 0))
    shifted = jax.random.randint(jax.random.fold_in(own, 4), (amount // 2,), 0, 1 << 20) % (slack + 1)
    tallies = tallies.at[donor].add(-shifted).at[sink].add(shifted)
    labels = jnp.searchsorted(jnp.cumsum(tallies), jnp.arange(rows * top), side="right").astype(jnp.int32)
    grid = labels.reshape(top, rows).T
    grid = grid[jax.random.permutation(jax.random.fold_in(own, 1), rows)]
    offset_by = jax.random.randint(jax.random.fold_in(own, 2), (rows, 1), 0, top)
    return jnp.take_along_axis(grid, (jnp.arange(top)[None, :] + offset_by) % top, axis=1)


def portions_of(count, total, reach, skew, full):
    portions = [(1 << 20) // math.isqrt(rank ** skew) + 1 for rank in range(1, count + 1)]
    largest = reach if full else min(reach, max(-(-total // count), total * portions[0] // sum(portions)))
    least = 1 if total - largest >= count - 1 else 0
    counts, surplus = [largest] + [least] * (count - 1), total - largest - least * (count - 1)
    while surplus > 0:
        movable = [i for i in range(1, count) if counts[i] < largest] or [i for i in range(1, count) if counts[i] < reach]
        whole, remaining = sum([portions[i] for i in movable]), surplus
        for i in movable:
            extra = min(reach - counts[i], max(1, remaining * portions[i] // whole), surplus)
            counts[i] = counts[i] + extra
            surplus = surplus - extra
    return np.array(counts)


def centred(rng, extent, scale, reach, pieces=(), kind=jnp.bfloat16):
    values = scale * jax.random.normal(rng, extent, jnp.float32)
    if pieces:
        values = values * levels(rng, extent, pieces, -0.22, 0.18)
    return jnp.clip(values, -reach, reach).astype(kind)


def setup_inputs(seed: int = 0) -> dict:
    splits = jax.random.split(jax.random.key(seed), 15)
    state = centred(splits[0], (EQ, NS, NG, NW), 1.0, 6.0, ((1, 4), (2, 2), (3, 4)), jnp.float32)
    advect = centred(splits[1], (2, NS, NG), 1.0, 5.0, ((1, 4), (2, 2)), jnp.float32)
    dtau = jnp.clip(jnp.exp(math.log(200.0) - 2.9957323 * jax.random.uniform(splits[2], (NS, NG, NW), jnp.float32) ** levels(splits[2], (NS, NG, NW), ((0, 4), (1, 2), (2, 4)), -0.2, 0.2)), 10.0, 200.0)
    viscosity = jnp.clip(jnp.exp(math.log(0.5) - 2.3025851 * jax.random.uniform(splits[3], (NS, NG, NW), jnp.float32) ** levels(splits[3], (NS, NG, NW), ((0, 4), (1, 2), (2, 4)), -0.2, 0.2)), 0.05, 0.5)
    mode_speed = jnp.clip(jax.random.uniform(splits[4], (EQ,), jnp.float32, -2.0, 2.0), -2.0, 2.0)
    left_modes = centred(splits[5], (EQ, EQ), EQ ** -0.5, 2.5, (), jnp.float32)
    right_modes = centred(splits[6], (EQ, EQ), EQ ** -0.5, 2.5, (), jnp.float32)
    source_jac = centred(splits[7], (EQ, EQ), EQ ** -0.5, 2.5, (), jnp.float32)
    elem_owner_keys = jax.random.split(jax.random.fold_in(splits[8], 1), NE // NE_DEV)
    elem_owner_turns = jax.random.permutation(jax.random.fold_in(splits[8], 3), NE // NE_DEV)
    elem_owner = jax.vmap(lambda own, number: assign_block(jax.random.fold_in(splits[8], 2), own, number, NE_DEV, BLOCKS, 1, CAP, 2))(elem_owner_keys, elem_owner_turns).reshape((NE, 1))
    elem_tile = place_ends(jax.random.randint(splits[9], (NE,), 0, TILES), jax.random.fold_in(splits[9], 1), 0, TILES - 1).astype(jnp.int32)
    elem_offset = jnp.clip(8.0 * jax.random.uniform(splits[10], (NE, 2), jnp.float32) ** levels(splits[10], (NE, 2), ((0, 8),), -0.2, 0.2), 0.0, 8.0)
    elem_height = jnp.clip(512.0 * jax.random.uniform(splits[11], (NE,), jnp.float32) ** levels(splits[11], (NE,), ((0, 8),), -0.2, 0.2), 0.0, 512.0)
    elem_force = centred(splits[12], (NE, 3), 30.0, 180.0, ((0, 8),), jnp.float32)
    elem_width = jnp.clip(jnp.exp(math.log(4.0) - 0.98082925 * jax.random.uniform(splits[13], (NE,), jnp.float32) ** levels(splits[13], (NE,), ((0, 8),), -0.2, 0.2)), 1.5, 4.0)
    return dict(state=state, advect=advect, dtau=dtau, viscosity=viscosity, mode_speed=mode_speed, left_modes=left_modes, right_modes=right_modes, source_jac=source_jac, elem_owner=elem_owner, elem_tile=elem_tile, elem_offset=elem_offset, elem_height=elem_height, elem_force=elem_force, elem_width=elem_width)


def spread_all(elem_owner, elem_tile, elem_offset, elem_height, elem_force, elem_width, dtype):
    tiles_g = CG // TILE
    field = jnp.zeros((3, NS, NG, NW), dtype)
    s_cells = jnp.arange(CS).astype(dtype) + 0.5
    g_cells = jnp.arange(CG).astype(dtype) + 0.5
    w_cells = jnp.arange(NW).astype(dtype) + 0.5

    def add_one(index, field):
        owner = elem_owner[index, 0]
        tile = elem_tile[index]
        pos_s = (tile // tiles_g).astype(dtype) * TILE + elem_offset[index, 0]
        pos_g = (tile % tiles_g).astype(dtype) * TILE + elem_offset[index, 1]
        pos_w = elem_height[index]
        width = elem_width[index]
        sharp = 1.0 / (width * width)
        amplitude = 1.0 / (width * width * width * math.pi ** 1.5)
        prof_s = jnp.exp(-sharp * (s_cells - pos_s) ** 2)
        prof_g = jnp.exp(-sharp * (g_cells - pos_g) ** 2)
        prof_w = jnp.exp(-sharp * (w_cells - pos_w) ** 2)
        push = elem_force[index] * amplitude
        piece = push[:, None, None, None] * prof_s[None, :, None, None] * prof_g[None, None, :, None] * prof_w[None, None, None, :]
        start_s = ((owner // N_GIRTH) * CS).astype(jnp.int32)
        start_g = ((owner % N_GIRTH) * CG).astype(jnp.int32)
        zero = jnp.array(0, jnp.int32)
        current = lax.dynamic_slice(field, (zero, start_s, start_g, zero), (3, CS, CG, NW))
        return lax.dynamic_update_slice(field, current + piece, (zero, start_s, start_g, zero))

    return lax.fori_loop(0, NE, add_one, field)


def reference(state, advect, dtau, viscosity, mode_speed, left_modes, right_modes, source_jac, elem_owner, elem_tile, elem_offset, elem_height, elem_force, elem_width):
    highest = lax.Precision.HIGHEST
    dtype = state.dtype
    force_field = spread_all(elem_owner, elem_tile, elem_offset, elem_height, elem_force, elem_width, dtype)
    side = jnp.pad(state, ((0, 0), (2, 2), (2, 2), (0, 0)))
    walls = jnp.pad(state, ((0, 0), (0, 0), (0, 0), (1, 1)))

    def along_s(shift):
        return side[:, 2 + shift:2 + shift + NS, 2:2 + NG, :]

    def along_g(shift):
        return side[:, 2:2 + NS, 2 + shift:2 + shift + NG, :]

    deriv_s = (8.0 * (along_s(1) - along_s(-1)) - (along_s(2) - along_s(-2))) / 12.0
    deriv_g = (8.0 * (along_g(1) - along_g(-1)) - (along_g(2) - along_g(-2))) / 12.0
    fourth_s = along_s(2) - 4.0 * along_s(1) + 6.0 * state - 4.0 * along_s(-1) + along_s(-2)
    fourth_g = along_g(2) - 4.0 * along_g(1) + 6.0 * state - 4.0 * along_g(-1) + along_g(-2)
    lap_w = walls[:, :, :, 2:] - 2.0 * state + walls[:, :, :, :-2]
    zeros_one = jnp.zeros((1, NS, NG, NW), dtype)
    forcing = jnp.concatenate([zeros_one, force_field, zeros_one, zeros_one], axis=0)
    mixing = jnp.einsum("ef,fsgw->esgw", source_jac, state, precision=highest)
    residual = (-(advect[0][None, :, :, None] * deriv_s + advect[1][None, :, :, None] * deriv_g)
                - (fourth_s + fourth_g) / 32.0 + viscosity[None] * lap_w + mixing + forcing)
    rhs = dtau[None] * jnp.einsum("me,esgw->msgw", left_modes, residual, precision=highest)
    speeds = mode_speed[:, None, None, None]
    up_coef = dtau[None] * (jnp.maximum(speeds, 0.0) + viscosity[None])
    down_coef = dtau[None] * (jnp.maximum(-speeds, 0.0) + viscosity[None])

    def step(carry, inputs):
        coef, source = inputs
        value = (source + coef * carry) / (1.0 + coef)
        return value, value

    start = jnp.zeros((EQ, NS, NG), dtype)
    sweep = lax.scan(step, start, (jnp.moveaxis(up_coef, 3, 0), jnp.moveaxis(rhs, 3, 0)))[1]
    modal = lax.scan(step, start, (jnp.moveaxis(down_coef, 3, 0), sweep), reverse=True)[1]
    modal = jnp.moveaxis(modal, 0, 3)
    return jnp.einsum("em,msgw->esgw", right_modes, modal, precision=highest)
```

```python
import functools
import math

import jax
import jax.numpy as jnp
from jax import lax
from jax.experimental import pallas as pl
from jax.experimental.pallas import tpu as pltpu
from jax.sharding import PartitionSpec as P

TILE = 8
EQ = 6
LANES = 128
STEPS = 16
HIGHEST = lax.Precision.HIGHEST
NT = (((1,), (1,)), ((), ()))
PN, PD0, G0, C0, C1, D1, LSF, LSL, UP, DOWN = range(10)
MAP_ROWS = 64
COEF_ROWS = 48


def call(kernel, outs, *args, scratch=(), cost=0):
    shapes = [jax.ShapeDtypeStruct(shape, jnp.float32) for shape in outs]
    return pl.pallas_call(
        kernel,
        out_shape=shapes,
        in_specs=[pl.BlockSpec(memory_space=pltpu.VMEM)] * len(args),
        out_specs=[pl.BlockSpec(memory_space=pltpu.VMEM)] * len(outs),
        scratch_shapes=[pltpu.VMEM(shape, jnp.float32) for shape in scratch],
        compiler_params=pltpu.CompilerParams(vmem_limit_bytes=16 << 20),
        cost_estimate=pl.CostEstimate(flops=cost, bytes_accessed=cost, transcendentals=0),
    )(*args)


def sub_iota(shape=(8, LANES)):
    return lax.broadcasted_iota(jnp.int32, shape, 0)


def up_entry(factor, offset):
    row = sub_iota()
    for reach in (1, 2, 4):
        inside = row >= reach
        offset = jnp.where(inside, factor * pltpu.roll(offset, reach, 0) + offset, offset)
        factor = jnp.where(inside, factor * pltpu.roll(factor, reach, 0), factor)
    return jnp.where(row >= 1, pltpu.roll(offset, 1, 0), 0.0), jnp.where(row >= 1, pltpu.roll(factor, 1, 0), 1.0)


def down_entry(factor, offset):
    row = sub_iota()
    for reach in (1, 2, 4):
        inside = row < 8 - reach
        offset = jnp.where(inside, factor * pltpu.roll(offset, 8 - reach, 0) + offset, offset)
        factor = jnp.where(inside, factor * pltpu.roll(factor, 8 - reach, 0), factor)
    return jnp.where(row < 7, pltpu.roll(offset, 7, 0), 0.0), jnp.where(row < 7, pltpu.roll(factor, 7, 0), 1.0)


def pack_kernel(
    cells, where, state_ref, owner_ref, tile_ref, offset_ref, height_ref, force_ref, width_ref,
    *refs,
):
    cells_s, cells_g = cells
    (out_s, out_g, pay_ref, col_ref) = (refs[:2], refs[2:-2], refs[-2], refs[-1])
    held = owner_ref.shape[0]
    col_ref[...] = jnp.zeros_like(col_ref)
    col_ref[:held, 0:2] = offset_ref[...]
    col_ref[:held, 2:5] = force_ref[...]
    col_ref[:held, 5:6] = owner_ref[...].astype(jnp.float32)
    pick = (sub_iota((8, LANES)) == lax.broadcasted_iota(jnp.int32, (8, LANES), 1)).astype(jnp.float32)
    rows = lax.dot_general(pick, col_ref[...], NT, precision=HIGHEST, preferred_element_type=jnp.float32)
    rows = rows[:, :held]
    tiles_g = cells_g // TILE
    tile = tile_ref[...].astype(jnp.float32)
    tile_s = jnp.floor(tile * (1.0 / tiles_g))
    tile_g = tile - tile_s * tiles_g
    width = width_ref[...]
    amplitude = 1.0 / (width * width * width * math.pi**1.5)
    pay_ref[...] = jnp.zeros_like(pay_ref)
    pay_ref[0:1, :held] = tile_s * TILE + rows[0:1]
    pay_ref[1:2, :held] = tile_g * TILE + rows[1:2]
    pay_ref[2:3, :held] = height_ref[...]
    pay_ref[3:4, :held] = 1.0 / (width * width)
    pay_ref[4:7, :held] = rows[2:5] * amplitude
    pay_ref[7:8, :held] = rows[5:6]
    columns = cells_s * cells_g
    odd_s = lax.rem(lax.axis_index("stream"), 2)
    odd_g = lax.rem(lax.axis_index("girth"), 2)
    for side, out_ref in enumerate(out_s):
        low = odd_s if side == 0 else 1 - odd_s
        start = (cells_s - 2) * cells_g * (1 - low)
        for q in range(EQ):
            at = pl.multiple_of(q * columns + start, 8)
            out_ref[q * 2 * cells_g : (q + 1) * 2 * cells_g, :] = state_ref[pl.ds(at, 2 * cells_g), :]
        if out_ref.shape[0] > EQ * 2 * cells_g:
            out_ref[EQ * 2 * cells_g :, :] = pay_ref[...]
    for side, out_ref in enumerate(out_g):
        low = odd_g if side == 0 else 1 - odd_g
        start = (cells_g - 2) * (1 - low)
        for r in range(2):
            for q in range(EQ):
                out_ref[(r * EQ + q) * cells_s : (r * EQ + q + 1) * cells_s, :] = state_ref[
                    pl.ds(q * columns + start + r, cells_s, stride=cells_g), :
                ]
        if out_ref.shape[0] > 2 * EQ * cells_s:
            out_ref[2 * EQ * cells_s :, :] = pay_ref[...]


def coef_kernel(
    cells, state_ref, advect_ref, dtau_ref, visc_ref, speed_ref, left_ref, right_ref, source_ref,
    r0_ref, adv_ref, lb_ref, rb_ref, fu_ref, gu_ref, fd_ref, gd_ref, dru_ref, rd_ref, gf_ref, pd_ref,
    crow_ref, turned, speeds,
):
    cells_s, cells_g = cells
    columns = cells_s * cells_g
    tiles = columns // 8
    for m in range(EQ):
        speeds[m] = jnp.broadcast_to(speed_ref[0:1, m : m + 1], (8, LANES))
        for q in range(EQ):
            lb_ref[m * EQ + q] = jnp.broadcast_to(left_ref[m : m + 1, q : q + 1], (8, LANES))
            rb_ref[m * EQ + q] = jnp.broadcast_to(right_ref[m : m + 1, q : q + 1], (8, LANES))
    on = sub_iota((cells_g, cells_g)) == lax.broadcasted_iota(jnp.int32, (cells_g, cells_g), 1)
    for d in range(2):
        for s in range(cells_s):
            line = jnp.broadcast_to(advect_ref[d, s : s + 1, :], (cells_g, cells_g))
            line = jnp.sum(jnp.where(on, line, 0.0), axis=1, keepdims=True)
            adv_ref[d, s * cells_g : (s + 1) * cells_g, :] = jnp.broadcast_to(line, (cells_g, LANES))
    girth = sub_iota((cells_g, LANES))
    lane = lax.broadcasted_iota(jnp.int32, (cells_g, LANES), 1)
    for s in range(cells_s):
        rows = slice(s * cells_g, (s + 1) * cells_g)
        speed_s, speed_g, visc = adv_ref[0, rows], adv_ref[1, rows], visc_ref[rows]
        state = [state_ref[q * columns + s * cells_g : q * columns + (s + 1) * cells_g] for q in range(EQ)]
        near_up, near_down = 0.125 - speed_s * (2.0 / 3.0), 0.125 + speed_s * (2.0 / 3.0)
        far_up, far_down = speed_s * (1.0 / 12.0) - 0.03125, -0.03125 - speed_s * (1.0 / 12.0)
        right1 = jnp.where(girth < cells_g - 1, 0.125 - speed_g * (2.0 / 3.0), 0.0)
        left1 = jnp.where(girth >= 1, 0.125 + speed_g * (2.0 / 3.0), 0.0)
        right2 = jnp.where(girth < cells_g - 2, speed_g * (1.0 / 12.0) - 0.03125, 0.0)
        left2 = jnp.where(girth >= 2, -0.03125 - speed_g * (1.0 / 12.0), 0.0)
        above = jnp.where(lane < LANES - 1, visc, 0.0)
        below = jnp.where(lane >= 1, visc, 0.0)
        centre = -0.375 - 2.0 * visc
        for q in range(EQ):
            here = state[q]
            total = centre * here
            for shift, weight in ((1, near_up), (-1, near_down), (2, far_up), (-2, far_down)):
                if 0 <= s + shift < cells_s:
                    at = q * columns + (s + shift) * cells_g
                    total = total + weight * state_ref[at : at + cells_g]
            total = total + right1 * pltpu.roll(here, cells_g - 1, 0) + left1 * pltpu.roll(here, 1, 0)
            total = total + right2 * pltpu.roll(here, cells_g - 2, 0) + left2 * pltpu.roll(here, 2, 0)
            total = total + above * pltpu.roll(here, LANES - 1, 1) + below * pltpu.roll(here, 1, 1)
            for f in range(EQ):
                total = total + jnp.broadcast_to(source_ref[q : q + 1, f : f + 1], (cells_g, LANES)) * state[f]
            r0_ref[q * columns + s * cells_g : q * columns + (s + 1) * cells_g] = total
    sub, lanes = sub_iota(), lax.broadcasted_iota(jnp.int32, (8, LANES), 1)
    ends = ((sub == 0) & (lanes == 0)) | ((sub == 1) & (lanes == LANES - 1))
    ends = jnp.where(ends, 1.0, 0.0)
    edge = [
        lax.dot_general(
            ends, state_ref[q * columns : (q + 1) * columns], NT, precision=HIGHEST,
            preferred_element_type=jnp.float32,
        )
        for q in range(EQ)
    ]
    for m in range(EQ):
        mixed = lb_ref[m * EQ] * edge[0]
        for q in range(1, EQ):
            mixed = mixed + lb_ref[m * EQ + q] * edge[q]
        crow_ref[LSF * EQ + m : LSF * EQ + m + 1] = mixed[0:1]
        crow_ref[LSL * EQ + m : LSL * EQ + m + 1] = mixed[1:2]
    turned[0] = jnp.transpose(dtau_ref[...])
    turned[1] = jnp.transpose(visc_ref[...])

    def mode(m, carry):
        ahead = jnp.maximum(speeds[m], 0.0)
        back = jnp.maximum(-speeds[m], 0.0)
        step = [turned[0, pl.ds(j, 8, stride=STEPS), :] for j in range(STEPS)]
        visc = [turned[1, pl.ds(j, 8, stride=STEPS), :] for j in range(STEPS)]
        product, ups = None, []
        for j in range(STEPS):
            a = step[j] * (ahead + visc[j])
            ru = 1.0 / (1.0 + a)
            fu = a * ru
            product = fu if product is None else fu * product
            fu_ref[m, j], gu_ref[m, j], dru_ref[m, j] = fu, product, step[j] * ru
            ups.append(product)
        last_ru = ru[7:8]
        last_dru = (step[-1] * ru)[7:8]
        _, outer = up_entry(product, jnp.zeros_like(product))
        ups = [p * outer for p in ups]
        product, value, downs, values = None, None, [None] * STEPS, [None] * STEPS
        for j in reversed(range(STEPS)):
            b = step[j] * (back + visc[j])
            rd = 1.0 / (1.0 + b)
            fd = b * rd
            source = ups[j] * rd
            product = fd if product is None else fd * product
            value = source if value is None else fd * value + source
            fd_ref[m, j], gd_ref[m, j], rd_ref[m, j] = fd, product, rd
            downs[j], values[j] = product, value
        entry, outer = down_entry(product, value)
        for j in range(STEPS):
            gf_ref[m, j] = values[j] + downs[j] * entry
            pd_ref[m, j] = downs[j] * outer
        rows = (
            (PN, ups[-1][7:8]),
            (PD0, (downs[0] * outer)[0:1]),
            (G0, (values[0] + downs[0] * entry)[0:1]),
            (C0, (visc[0] / (ahead + visc[0]))[0:1]),
            (C1, last_ru * (visc[-1] / (back + visc[-1]))[7:8]),
            (D1, last_dru * visc[-1][7:8]),
        )
        for kind, row in rows:
            crow_ref[pl.ds(kind * EQ + m, 1), :] = row
        return carry

    lax.fori_loop(0, EQ, mode, 0)


def pair_kernel(cells, pay_ref, a_ref, b_ref, g_ref, first_ref, second_ref):
    cells_s, cells_g = cells
    at_s, at_g = EQ * 2 * cells_g, EQ * 2 * cells_s
    first_ref[...] = pay_ref[...] + pltpu.roll(g_ref[at_g : at_g + 8], 8, 1)
    second_ref[...] = a_ref[at_s : at_s + 8] + pltpu.roll(b_ref[at_s : at_s + 8], 8, 1)


def sweep_kernel(cells, counts, shared, *refs):
    cells_s, cells_g = cells
    count_s, count_g = counts
    columns = cells_s * cells_g
    (
        a_ref, b_ref, ga_ref, gb_ref, r0_ref, adv_ref, lb_ref, fu_ref, gu_ref, fd_ref, gd_ref,
        dru_ref, rd_ref, crow_ref,
    ) = refs[:14]
    elems = refs[14:-5]
    h_ref, map_ref, res_ref, turned, field_ref = refs[-5:]
    at_s, at_g, at_w = (lax.axis_index(name) for name in ("stream", "girth", "wall"))
    mine = (at_s * count_g + at_g).astype(jnp.float32)
    base_s = sub_iota((cells_s, LANES)).astype(jnp.float32) + 0.5
    base_g = sub_iota((cells_g, LANES)).astype(jnp.float32) + 0.5
    base_w = (sub_iota((LANES, LANES)) + at_w * LANES).astype(jnp.float32) + 0.5

    def spread(pay):
        sharp = -pay[3:4]
        prof_s = jnp.exp(sharp * (base_s - pay[0:1]) ** 2)
        prof_g = jnp.exp(sharp * (base_g - pay[1:2]) ** 2)
        prof_w = jnp.exp(sharp * (base_w - pay[2:3]) ** 2)
        push = jnp.where(pay[7:8] == mine, pay[4:7], 0.0)
        plane = jnp.concatenate([prof_g * prof_s[s : s + 1] for s in range(cells_s)], axis=0)
        weights = jnp.concatenate([plane * push[c : c + 1] for c in range(3)], axis=0)
        return lax.dot_general(weights, prof_w, NT, precision=HIGHEST, preferred_element_type=jnp.float32)

    if shared:
        first, second, third, fourth = (ref[...] for ref in elems)
        pay = first + pltpu.roll(second, 16, 1) + pltpu.roll(third, 32, 1) + pltpu.roll(fourth, 48, 1)
        field_ref[...] = spread(pay)
    else:
        field_ref[...] = jnp.zeros_like(field_ref)

        def chunk(i, carry):
            field_ref[...] += spread(elems[0][i])
            return carry

        lax.fori_loop(0, elems[0].shape[0], chunk, 0)
    odd_s, odd_g = lax.rem(at_s, 2) == 1, lax.rem(at_g, 2) == 1
    low_s = jnp.where(at_s > 0, 1.0, 0.0)
    high_s = jnp.where(at_s < count_s - 1, 1.0, 0.0)
    low_g = jnp.where(at_g > 0, 1.0, 0.0)
    high_g = jnp.where(at_g < count_g - 1, 1.0, 0.0)
    speed = [adv_ref[0, s * cells_g : (s + 1) * cells_g] for s in range(cells_s)]
    sub = sub_iota()
    zero = jnp.zeros((8, LANES), jnp.float32)
    turn = []
    for s in range(cells_s):
        lead = adv_ref[1, s * cells_g : s * cells_g + 8]
        tail = adv_ref[1, (s + 1) * cells_g - 8 : (s + 1) * cells_g]
        near, far = low_g * (0.125 + lead * (2.0 / 3.0)), low_g * (-0.03125 - lead * (1.0 / 12.0))
        near_low = jnp.where(sub == 0, near, jnp.where(sub == 1, far, zero))
        far_low = jnp.where(sub == 0, far, zero)
        near, far = high_g * (0.125 - tail * (2.0 / 3.0)), high_g * (tail * (1.0 / 12.0) - 0.03125)
        near_high = jnp.where(sub == 7, near, jnp.where(sub == 6, far, zero))
        far_high = jnp.where(sub == 7, far, zero)
        turn.append((near_low, far_low, near_high, far_high))
    wide = cells_g
    for q in range(EQ):
        slab = slice(q * 2 * wide, (q + 1) * 2 * wide)
        slab_a, slab_b = a_ref[slab], b_ref[slab]
        low, high = jnp.where(odd_s, slab_a, slab_b), jnp.where(odd_s, slab_b, slab_a)
        for s in range(cells_s):
            rows = slice(q * columns + s * wide, q * columns + (s + 1) * wide)
            total = r0_ref[rows]
            if s == 0:
                total = total + low_s * (0.125 + speed[s] * (2.0 / 3.0)) * low[wide:]
                total = total + low_s * (-0.03125 - speed[s] * (1.0 / 12.0)) * low[:wide]
            if s == 1:
                total = total + low_s * (-0.03125 - speed[s] * (1.0 / 12.0)) * low[wide:]
            if s == cells_s - 2:
                total = total + high_s * (speed[s] * (1.0 / 12.0) - 0.03125) * high[:wide]
            if s == cells_s - 1:
                total = total + high_s * (0.125 - speed[s] * (2.0 / 3.0)) * high[:wide]
                total = total + high_s * (speed[s] * (1.0 / 12.0) - 0.03125) * high[wide:]
            if 1 <= q <= 3:
                total = total + field_ref[(q - 1) * columns + s * wide : (q - 1) * columns + (s + 1) * wide]
            near_low, far_low, near_high, far_high = turn[s]
            at = (q * cells_s + s, (EQ + q) * cells_s + s)
            part = [jnp.broadcast_to(ga_ref[i : i + 1], (8, LANES)) for i in at]
            if gb_ref is not ga_ref:
                other = [jnp.broadcast_to(gb_ref[i : i + 1], (8, LANES)) for i in at]
                part_low = [jnp.where(odd_g, x, y) for x, y in zip(part, other)]
                part_high = [jnp.where(odd_g, y, x) for x, y in zip(part, other)]
            else:
                part_low = part_high = part
            res_ref[rows] = total
            lead = slice(rows.start, rows.start + 8)
            tail = slice(rows.stop - 8, rows.stop)
            res_ref[lead] = total[:8] + near_low * part_low[1] + far_low * part_low[0]
            res_ref[tail] = total[wide - 8 :] + near_high * part_high[0] + far_high * part_high[1]
    tiles = columns // 8
    for m in range(EQ):
        total = None
        for q in range(EQ):
            part = lb_ref[m * EQ + q][None] * res_ref[q * columns : (q + 1) * columns].reshape(tiles, 8, LANES)
            total = part if total is None else total + part
        turned[m] = jnp.transpose(total.reshape(columns, LANES))
    map_ref[:COEF_ROWS] = crow_ref[...]
    map_ref[COEF_ROWS:] = jnp.zeros((MAP_ROWS - COEF_ROWS, LANES), jnp.float32)
    for m in range(EQ):
        value, values = None, []
        for j in range(STEPS):
            source = turned[m, pl.ds(j, 8, stride=STEPS), :] * dru_ref[m, j]
            value = source if value is None else fu_ref[m, j] * value + source
            values.append(value)
        entry, _ = up_entry(gu_ref[m, STEPS - 1], value)
        values = [v + gu_ref[m, j] * entry for j, v in enumerate(values)]
        map_ref[UP * EQ + m : UP * EQ + m + 1] = values[-1][7:8]
        value = None
        for j in reversed(range(STEPS)):
            source = values[j] * rd_ref[m, j]
            value = source if value is None else fd_ref[m, j] * value + source
            values[j] = value
        entry, _ = down_entry(gd_ref[m, 0], value)
        for j in range(STEPS):
            values[j] = values[j] + gd_ref[m, j] * entry
            h_ref[m, j] = values[j]
        map_ref[DOWN * EQ + m : DOWN * EQ + m + 1] = values[0][0:1]


def close_kernel(cells, count, *refs):
    maps = refs[:count]
    h_ref, gf_ref, pd_ref, rb_ref, out_ref, all_ref, turned = refs[count:]
    columns = cells[0] * cells[1]
    here = lax.axis_index("wall")
    for r, ref in enumerate(maps):
        all_ref[lax.rem(here + count - r, count)] = ref[...]

    def get(j, kind):
        return all_ref[j, kind * EQ : (kind + 1) * EQ]

    zero = jnp.zeros((EQ, LANES), jnp.float32)
    entry, entries, mine_up = zero, [], zero
    for j in range(count):
        if j > 0:
            entry = entry + get(j, C0) * get(j - 1, LSL)
        entries.append(entry)
        mine_up = jnp.where(here == j, entry, mine_up)
        entry = get(j, PN) * entry + get(j, UP)
        if j < count - 1:
            entry = entry + get(j, D1) * get(j + 1, LSF)
    above, mine_down = zero, zero
    for j in reversed(range(count)):
        if j < count - 1:
            above = above + get(j, C1) * get(j + 1, LSF)
        mine_down = jnp.where(here == j, above, mine_down)
        above = get(j, PD0) * above + get(j, G0) * entries[j] + get(j, DOWN)
    ups = [jnp.broadcast_to(mine_up[m : m + 1], (8, LANES)) for m in range(EQ)]
    downs = [jnp.broadcast_to(mine_down[m : m + 1], (8, LANES)) for m in range(EQ)]
    for j in range(STEPS):
        modal = [h_ref[m, j] + gf_ref[m, j] * ups[m] + pd_ref[m, j] * downs[m] for m in range(EQ)]
        for q in range(EQ):
            total = rb_ref[q * EQ] * modal[0]
            for m in range(1, EQ):
                total = total + rb_ref[q * EQ + m] * modal[m]
            turned[q, pl.ds(j, 8, stride=STEPS), :] = total
    for q in range(EQ):
        out_ref[q * columns : (q + 1) * columns] = jnp.transpose(turned[q])


def swaps(count, side):
    if side == 0:
        return [(i, i ^ 1) for i in range(count)]
    return [(i, (i + (1 if i % 2 else -1)) % count) for i in range(count)]


def local(
    state,
    advect,
    dtau,
    viscosity,
    mode_speed,
    left_modes,
    right_modes,
    source_jac,
    elem_owner,
    elem_tile,
    elem_offset,
    elem_height,
    elem_force,
    elem_width,
):
    cells = (state.shape[1], state.shape[2])
    cells_s, cells_g = cells
    columns = cells_s * cells_g
    count_s, count_g, count_w = (lax.axis_size(name) for name in ("stream", "girth", "wall"))
    held = elem_owner.shape[0]
    shared = count_s == 4 and count_g == 2 and held <= 8
    flat = state.reshape(EQ * columns, LANES)
    sides_g = 1 if count_g == 2 else 2
    extra = 8 if shared else 0
    outs = [(EQ * 2 * cells_g + extra, LANES)] * 2
    outs += [(EQ * 2 * cells_s + extra, LANES)] * sides_g + [(8, LANES)]
    *packed, pay = call(
        functools.partial(pack_kernel, cells, None),
        outs,
        flat,
        elem_owner,
        elem_tile.reshape(1, held),
        elem_offset,
        elem_height.reshape(1, held),
        elem_force,
        elem_width.reshape(1, held),
        scratch=[(max(8, held), LANES)],
    )
    halo_a = lax.ppermute(packed[0], "stream", swaps(count_s, 0))
    halo_b = lax.ppermute(packed[1], "stream", swaps(count_s, 1))
    halo_g = [lax.ppermute(packed[2 + i], "girth", swaps(count_g, i)) for i in range(sides_g)]
    wide = (EQ, STEPS, 8, LANES)
    r0, adv, lb, rb, fu, gu, fd, gd, dru, rd, gf, pd, crow = call(
        functools.partial(coef_kernel, cells),
        [(EQ * columns, LANES), (2, columns, LANES), (EQ * EQ, 8, LANES), (EQ * EQ, 8, LANES)]
        + [wide] * 8
        + [(COEF_ROWS, LANES)],
        flat,
        advect,
        dtau.reshape(columns, LANES),
        viscosity.reshape(columns, LANES),
        mode_speed.reshape(1, EQ),
        left_modes,
        right_modes,
        source_jac,
        scratch=[(2, LANES, columns), (EQ, 8, LANES)],
        cost=4 << 20,
    )
    if shared:
        first, second = call(
            functools.partial(pair_kernel, cells), [(8, LANES)] * 2, pay, halo_a, halo_b, halo_g[0]
        )
        both = ("stream", "girth")
        across = [(i, i ^ 4) for i in range(8)]
        third = lax.ppermute(first, both, across)
        fourth = lax.ppermute(second, "girth", swaps(2, 0))
        elems = (first, second, third, fourth)
    else:
        elems = (lax.all_gather(pay, ("stream", "girth")),)
    h, block_map = call(
        functools.partial(sweep_kernel, cells, (count_s, count_g), shared),
        [wide, (MAP_ROWS, LANES)],
        halo_a, halo_b, halo_g[0], halo_g[-1], r0, adv, lb, fu, gu, fd, gd, dru, rd, crow, *elems,
        scratch=[(EQ * columns, LANES), (EQ, LANES, columns), (3 * columns, LANES)],
        cost=1 << 20,
    )
    maps = [block_map]
    for r in range(1, count_w):
        maps.append(lax.ppermute(block_map, "wall", [(i, (i + r) % count_w) for i in range(count_w)]))
    (out,) = call(
        functools.partial(close_kernel, cells, count_w),
        [(EQ * columns, LANES)],
        *maps, h, gf, pd, rb,
        scratch=[(count_w, MAP_ROWS, LANES), (EQ, LANES, columns)],
        cost=1 << 20,
    )
    return out.reshape(state.shape)


def solution(mesh):
    in_specs = (
        P(None, "stream", "girth", "wall"),
        P(None, "stream", "girth"),
        P("stream", "girth", "wall"),
        P("stream", "girth", "wall"),
        P(),
        P(),
        P(),
        P(),
        P(("stream", "girth"), None),
        P(("stream", "girth")),
        P(("stream", "girth"), None),
        P(("stream", "girth")),
        P(("stream", "girth"), None),
        P(("stream", "girth")),
    )
    out_specs = P(None, "stream", "girth", "wall")
    return jax.shard_map(local, mesh=mesh, in_specs=in_specs, out_specs=out_specs, check_vma=False)
```

```python
import functools
import math

import jax
import jax.numpy as jnp
from jax import lax
from jax.experimental import pallas as pl
from jax.experimental.pallas import tpu as pltpu
from jax.sharding import PartitionSpec as P

TILE = 8
EQ = 6
LANES = 128
STEPS = 16
HIGHEST = lax.Precision.HIGHEST
NT = (((1,), (1,)), ((), ()))
PN, PD0, G0, LSF, LSL, UP, DOWN = range(7)
FIRST_VISC, LAST_VISC, LAST_STEP = 42, 43, 44
MAP_ROWS = 48


def call(kernel, outs, *args, scratch=(), cost=0, far=(), far_out=(), copies=0):
    shapes = [jax.ShapeDtypeStruct(shape, jnp.float32) for shape in outs]

    def spec(is_far):
        return pl.BlockSpec(memory_space=pltpu.HBM if is_far else pltpu.VMEM)

    return pl.pallas_call(
        kernel,
        out_shape=shapes,
        in_specs=[spec(i in far) for i in range(len(args))],
        out_specs=[spec(i in far_out) for i in range(len(outs))],
        scratch_shapes=[pltpu.VMEM(shape, kind) for shape, kind in scratch]
        + ([pltpu.SemaphoreType.DMA((copies,))] if copies else []),
        compiler_params=pltpu.CompilerParams(vmem_limit_bytes=16 << 20),
        cost_estimate=pl.CostEstimate(flops=cost, bytes_accessed=cost, transcendentals=0),
    )(*args)


def sub_iota(shape=(8, LANES)):
    return lax.broadcasted_iota(jnp.int32, shape, 0)


def up_entry(factor, offset):
    row = sub_iota()
    for reach in (1, 2, 4):
        inside = row >= reach
        offset = jnp.where(inside, factor * pltpu.roll(offset, reach, 0) + offset, offset)
        factor = jnp.where(inside, factor * pltpu.roll(factor, reach, 0), factor)
    return jnp.where(row >= 1, pltpu.roll(offset, 1, 0), 0.0), jnp.where(row >= 1, pltpu.roll(factor, 1, 0), 1.0)


def down_entry(factor, offset):
    row = sub_iota()
    for reach in (1, 2, 4):
        inside = row < 8 - reach
        offset = jnp.where(inside, factor * pltpu.roll(offset, 8 - reach, 0) + offset, offset)
        factor = jnp.where(inside, factor * pltpu.roll(factor, 8 - reach, 0), factor)
    return jnp.where(row < 7, pltpu.roll(offset, 7, 0), 0.0), jnp.where(row < 7, pltpu.roll(factor, 7, 0), 1.0)


def pack_kernel(
    cells, held, sides, small, state_ref, owner_ref, tile_ref, offset_ref, height_ref, force_ref, width_ref,
    *refs,
):
    cells_s, cells_g = cells
    small_in, refs = refs[:small], refs[small:]
    out_s, out_g, refs = refs[:2], refs[2 : 2 + sides], refs[2 + sides :]
    pay_ref, small_out, refs = refs[0], refs[1 : 1 + small], refs[1 + small :]
    owner, tile, offset, height, force, width = refs[:6]
    edges, sem = refs[6:-1], refs[-1]
    odd_s = lax.rem(lax.axis_index("stream"), 2)
    odd_g = lax.rem(lax.axis_index("girth"), 2)
    copies = []

    def start(source, target):
        copy = pltpu.make_async_copy(source, target, sem.at[len(copies)])
        copy.start()
        copies.append(copy)

    for side in range(sides):
        low = odd_g if side == 0 else 1 - odd_g
        at = pl.multiple_of((cells_g - 8) * (1 - low), 8)
        start(state_ref.at[:, :, pl.ds(at, 8), :], edges[side])
    for pair in zip(
        (owner_ref, tile_ref, offset_ref, height_ref, force_ref, width_ref),
        (owner, tile, offset, height, force, width),
    ):
        start(*pair)
    slab = 2 * cells_g
    for side, out_ref in enumerate(out_s):
        low = odd_s if side == 0 else 1 - odd_s
        at = (cells_s - 2) * (1 - low)
        for q in range(EQ):
            for r in range(2):
                base = q * slab + r * cells_g
                start(state_ref.at[q, at + r], out_ref.at[base : base + cells_g])
    for pair in zip(small_in, small_out):
        start(*pair)
    for copy in copies[sides : sides + 6]:
        copy.wait()
    tiles_g = cells_g // TILE
    number = tile[...].astype(jnp.float32)
    tile_s = jnp.floor(number * (1.0 / tiles_g))
    tile_g = number - tile_s * tiles_g
    wide = width[...]
    amplitude = 1.0 / (wide * wide * wide * math.pi**1.5)
    pay_ref[...] = jnp.zeros_like(pay_ref)
    pay_ref[0:1, :held] = tile_s * TILE + offset[0:1]
    pay_ref[1:2, :held] = tile_g * TILE + offset[1:2]
    pay_ref[2:3, :held] = height[...]
    pay_ref[3:4, :held] = 1.0 / (wide * wide)
    pay_ref[4:7, :held] = force[...] * amplitude
    pay_ref[7:8, :held] = owner[...].astype(jnp.float32)
    ends = [(ref, EQ * slab) for ref in out_s] + [(ref, 2 * EQ * cells_s) for ref in out_g]
    for out_ref, rows in ends:
        if out_ref.shape[0] > rows:
            out_ref[rows:, :] = pay_ref[...]
    for side, out_ref in enumerate(out_g):
        copies[side].wait()
        low = odd_g if side == 0 else 1 - odd_g
        flat = edges[side].reshape(EQ * cells_s * 8, LANES)
        for r in range(2):
            for q in range(EQ):
                out_ref[(r * EQ + q) * cells_s : (r * EQ + q + 1) * cells_s, :] = flat[
                    pl.ds(q * cells_s * 8 + 6 * (1 - low) + r, cells_s, stride=8), :
                ]
    for copy in copies[sides + 6 :]:
        copy.wait()


def coef_kernel(
    cells, state_ref, advect_ref, dtau_ref, visc_ref, speed_ref, left_ref, right_ref, source_ref,
    r0_ref, adv_ref, lb_ref, rb_ref, fu_ref, gu_ref, fd_ref, gd_ref, dru_ref, rd_ref, gf_ref, pd_ref,
    crow_ref, spd_ref, turned, speeds,
):
    cells_s, cells_g = cells
    columns = cells_s * cells_g
    tiles = columns // 8
    crow_ref[LAST_STEP + 1 :] = jnp.zeros((MAP_ROWS - LAST_STEP - 1, LANES), jnp.float32)
    spd_ref[...] = jnp.zeros_like(spd_ref)
    for m in range(EQ):
        speeds[m] = jnp.broadcast_to(speed_ref[0:1, m : m + 1], (8, LANES))
        spd_ref[m : m + 1] = jnp.broadcast_to(speed_ref[0:1, m : m + 1], (1, LANES))
        for q in range(EQ):
            lb_ref[m * EQ + q] = jnp.broadcast_to(left_ref[m : m + 1, q : q + 1], (8, LANES))
            rb_ref[m * EQ + q] = jnp.broadcast_to(right_ref[m : m + 1, q : q + 1], (8, LANES))
    on = sub_iota((cells_g, cells_g)) == lax.broadcasted_iota(jnp.int32, (cells_g, cells_g), 1)
    for d in range(2):
        for s in range(cells_s):
            line = jnp.broadcast_to(advect_ref[d, s : s + 1, :], (cells_g, cells_g))
            line = jnp.sum(jnp.where(on, line, 0.0), axis=1, keepdims=True)
            adv_ref[d, s * cells_g : (s + 1) * cells_g, :] = jnp.broadcast_to(line, (cells_g, LANES))
    girth = sub_iota((cells_g, LANES))
    lane = lax.broadcasted_iota(jnp.int32, (cells_g, LANES), 1)
    for s in range(cells_s):
        rows = slice(s * cells_g, (s + 1) * cells_g)
        speed_s, speed_g, visc = adv_ref[0, rows], adv_ref[1, rows], visc_ref[rows]
        state = [state_ref[q * columns + s * cells_g : q * columns + (s + 1) * cells_g] for q in range(EQ)]
        near_up, near_down = 0.125 - speed_s * (2.0 / 3.0), 0.125 + speed_s * (2.0 / 3.0)
        far_up, far_down = speed_s * (1.0 / 12.0) - 0.03125, -0.03125 - speed_s * (1.0 / 12.0)
        right1 = jnp.where(girth < cells_g - 1, 0.125 - speed_g * (2.0 / 3.0), 0.0)
        left1 = jnp.where(girth >= 1, 0.125 + speed_g * (2.0 / 3.0), 0.0)
        right2 = jnp.where(girth < cells_g - 2, speed_g * (1.0 / 12.0) - 0.03125, 0.0)
        left2 = jnp.where(girth >= 2, -0.03125 - speed_g * (1.0 / 12.0), 0.0)
        above = jnp.where(lane < LANES - 1, visc, 0.0)
        below = jnp.where(lane >= 1, visc, 0.0)
        centre = -0.375 - 2.0 * visc
        for q in range(EQ):
            here = state[q]
            total = centre * here
            for shift, weight in ((1, near_up), (-1, near_down), (2, far_up), (-2, far_down)):
                if 0 <= s + shift < cells_s:
                    at = q * columns + (s + shift) * cells_g
                    total = total + weight * state_ref[at : at + cells_g]
            total = total + right1 * pltpu.roll(here, cells_g - 1, 0) + left1 * pltpu.roll(here, 1, 0)
            total = total + right2 * pltpu.roll(here, cells_g - 2, 0) + left2 * pltpu.roll(here, 2, 0)
            total = total + above * pltpu.roll(here, LANES - 1, 1) + below * pltpu.roll(here, 1, 1)
            for f in range(EQ):
                total = total + jnp.broadcast_to(source_ref[q : q + 1, f : f + 1], (cells_g, LANES)) * state[f]
            r0_ref[q * columns + s * cells_g : q * columns + (s + 1) * cells_g] = total
    sub, lanes = sub_iota(), lax.broadcasted_iota(jnp.int32, (8, LANES), 1)
    ends = ((sub == 0) & (lanes == 0)) | ((sub == 1) & (lanes == LANES - 1))
    ends = jnp.where(ends, 1.0, 0.0)
    edge = [
        lax.dot_general(
            ends, state_ref[q * columns : (q + 1) * columns], NT, precision=HIGHEST,
            preferred_element_type=jnp.float32,
        )
        for q in range(EQ)
    ]
    for m in range(EQ):
        mixed = lb_ref[m * EQ] * edge[0]
        for q in range(1, EQ):
            mixed = mixed + lb_ref[m * EQ + q] * edge[q]
        crow_ref[LSF * EQ + m : LSF * EQ + m + 1] = mixed[0:1]
        crow_ref[LSL * EQ + m : LSL * EQ + m + 1] = mixed[1:2]
    turned[0] = jnp.transpose(dtau_ref[...])
    turned[1] = jnp.transpose(visc_ref[...])
    crow_ref[FIRST_VISC : FIRST_VISC + 1] = turned[1, 0:1]
    crow_ref[LAST_VISC : LAST_VISC + 1] = turned[1, LANES - 1 : LANES]
    crow_ref[LAST_STEP : LAST_STEP + 1] = turned[0, LANES - 1 : LANES]

    def mode(m, carry):
        ahead = jnp.maximum(speeds[m], 0.0)
        back = jnp.maximum(-speeds[m], 0.0)
        step = [turned[0, pl.ds(j, 8, stride=STEPS), :] for j in range(STEPS)]
        visc = [turned[1, pl.ds(j, 8, stride=STEPS), :] for j in range(STEPS)]
        product, ups = None, []
        for j in range(STEPS):
            a = step[j] * (ahead + visc[j])
            ru = 1.0 / (1.0 + a)
            fu = a * ru
            product = fu if product is None else fu * product
            fu_ref[m, j], gu_ref[m, j], dru_ref[m, j] = fu, product, step[j] * ru
            ups.append(product)
        _, outer = up_entry(product, jnp.zeros_like(product))
        ups = [p * outer for p in ups]
        product, value, downs, values = None, None, [None] * STEPS, [None] * STEPS
        for j in reversed(range(STEPS)):
            b = step[j] * (back + visc[j])
            rd = 1.0 / (1.0 + b)
            fd = b * rd
            source = ups[j] * rd
            product = fd if product is None else fd * product
            value = source if value is None else fd * value + source
            fd_ref[m, j], gd_ref[m, j], rd_ref[m, j] = fd, product, rd
            downs[j], values[j] = product, value
        entry, outer = down_entry(product, value)
        for j in range(STEPS):
            gf_ref[m, j] = values[j] + downs[j] * entry
            pd_ref[m, j] = downs[j] * outer
        rows = (
            (PN, ups[-1][7:8]),
            (PD0, (downs[0] * outer)[0:1]),
            (G0, (values[0] + downs[0] * entry)[0:1]),
        )
        for kind, row in rows:
            crow_ref[pl.ds(kind * EQ + m, 1), :] = row
        return carry

    lax.fori_loop(0, EQ, mode, 0)


def bundle_kernel(cells, pay_ref, a_ref, b_ref, g_ref, crow_ref, out_ref):
    cells_s, cells_g = cells
    at_s, at_g = EQ * 2 * cells_g, EQ * 2 * cells_s
    total = pay_ref[...] + pltpu.roll(a_ref[at_s : at_s + 8], 8, 1)
    out_ref[...] = total + pltpu.roll(b_ref[at_s : at_s + 8], 16, 1) + pltpu.roll(g_ref[at_g : at_g + 8], 24, 1)


def halo_kernel(cells, counts, sides, a_ref, b_ref, *refs):
    cells_s, cells_g = cells
    count_s, count_g = counts
    columns = cells_s * cells_g
    g_refs, (r0_ref, adv_ref, lb_ref, turned, res_ref) = refs[:sides], refs[sides:]
    at_s, at_g = lax.axis_index("stream"), lax.axis_index("girth")
    odd_s, odd_g = lax.rem(at_s, 2) == 1, lax.rem(at_g, 2) == 1
    low_s = jnp.where(at_s > 0, 1.0, 0.0)
    high_s = jnp.where(at_s < count_s - 1, 1.0, 0.0)
    low_g = jnp.where(at_g > 0, 1.0, 0.0)
    high_g = jnp.where(at_g < count_g - 1, 1.0, 0.0)
    speed = [adv_ref[0, s * cells_g : (s + 1) * cells_g] for s in range(cells_s)]
    sub = sub_iota()
    zero = jnp.zeros((8, LANES), jnp.float32)
    turn = []
    for s in range(cells_s):
        lead = adv_ref[1, s * cells_g : s * cells_g + 8]
        tail = adv_ref[1, (s + 1) * cells_g - 8 : (s + 1) * cells_g]
        near, far = low_g * (0.125 + lead * (2.0 / 3.0)), low_g * (-0.03125 - lead * (1.0 / 12.0))
        near_low = jnp.where(sub == 0, near, jnp.where(sub == 1, far, zero))
        far_low = jnp.where(sub == 0, far, zero)
        near, far = high_g * (0.125 - tail * (2.0 / 3.0)), high_g * (tail * (1.0 / 12.0) - 0.03125)
        near_high = jnp.where(sub == 7, near, jnp.where(sub == 6, far, zero))
        far_high = jnp.where(sub == 7, far, zero)
        turn.append((near_low, far_low, near_high, far_high))
    wide = cells_g
    for q in range(EQ):
        slab = slice(q * 2 * wide, (q + 1) * 2 * wide)
        slab_a, slab_b = a_ref[slab], b_ref[slab]
        low, high = jnp.where(odd_s, slab_a, slab_b), jnp.where(odd_s, slab_b, slab_a)
        for s in range(cells_s):
            rows = slice(q * columns + s * wide, q * columns + (s + 1) * wide)
            total = r0_ref[rows]
            if s == 0:
                total = total + low_s * (0.125 + speed[s] * (2.0 / 3.0)) * low[wide:]
                total = total + low_s * (-0.03125 - speed[s] * (1.0 / 12.0)) * low[:wide]
            if s == 1:
                total = total + low_s * (-0.03125 - speed[s] * (1.0 / 12.0)) * low[wide:]
            if s == cells_s - 2:
                total = total + high_s * (speed[s] * (1.0 / 12.0) - 0.03125) * high[:wide]
            if s == cells_s - 1:
                total = total + high_s * (0.125 - speed[s] * (2.0 / 3.0)) * high[:wide]
                total = total + high_s * (speed[s] * (1.0 / 12.0) - 0.03125) * high[wide:]
            near_low, far_low, near_high, far_high = turn[s]
            at = (q * cells_s + s, (EQ + q) * cells_s + s)
            part = [jnp.broadcast_to(g_refs[0][i : i + 1], (8, LANES)) for i in at]
            part_low = part_high = part
            if sides > 1:
                other = [jnp.broadcast_to(g_refs[1][i : i + 1], (8, LANES)) for i in at]
                part_low = [jnp.where(odd_g, x, y) for x, y in zip(part, other)]
                part_high = [jnp.where(odd_g, y, x) for x, y in zip(part, other)]
            lead, tail = slice(rows.start, rows.start + 8), slice(rows.stop - 8, rows.stop)
            if wide > 16:
                res_ref[rows] = total
            res_ref[lead] = total[:8] + near_low * part_low[1] + far_low * part_low[0]
            res_ref[tail] = total[wide - 8 :] + near_high * part_high[0] + far_high * part_high[1]
    tiles = columns // 8
    for m in range(EQ):
        total = None
        for q in range(EQ):
            part = lb_ref[m * EQ + q][None] * res_ref[q * columns : (q + 1) * columns].reshape(tiles, 8, LANES)
            total = part if total is None else total + part
        turned[m] = jnp.transpose(total.reshape(columns, LANES))


def sweep_kernel(
    cells, count_g, shared, turned, lb_ref, fu_ref, gu_ref, fd_ref, gd_ref, dru_ref, rd_ref, crow_ref, *refs
):
    cells_s, cells_g = cells
    columns = cells_s * cells_g
    elems = refs[:-3]
    h_ref, map_ref, field_ref = refs[-3:]
    at_s, at_g, at_w = (lax.axis_index(name) for name in ("stream", "girth", "wall"))
    mine = (at_s * count_g + at_g).astype(jnp.float32)
    base_s = sub_iota((cells_s, LANES)).astype(jnp.float32) + 0.5
    base_g = sub_iota((cells_g, LANES)).astype(jnp.float32) + 0.5
    first = sub_iota() * STEPS + at_w * LANES
    base_w = jnp.concatenate([first + j for j in range(STEPS)], axis=0).astype(jnp.float32) + 0.5

    def spread(pay):
        sharp = -pay[3:4]
        prof_s = jnp.exp(sharp * (base_s - pay[0:1]) ** 2)
        prof_g = jnp.exp(sharp * (base_g - pay[1:2]) ** 2)
        prof_w = jnp.exp(sharp * (base_w - pay[2:3]) ** 2)
        push = jnp.where(pay[7:8] == mine, pay[4:7], 0.0)
        plane = jnp.concatenate([prof_g * prof_s[s : s + 1] for s in range(cells_s)], axis=0)
        weights = jnp.concatenate([plane * push[c : c + 1] for c in range(3)], axis=0)
        return lax.dot_general(prof_w, weights, NT, precision=HIGHEST, preferred_element_type=jnp.float32)

    if shared:
        field_ref[...] = spread(elems[0][...] + pltpu.roll(elems[1][...], 32, 1))
    else:
        field_ref[...] = jnp.zeros_like(field_ref)

        def chunk(i, carry):
            field_ref[...] += spread(elems[0][i])
            return carry

        lax.fori_loop(0, elems[0].shape[0], chunk, 0)
    map_ref[...] = crow_ref[...]
    for m in range(EQ):
        value, values = None, []
        for j in range(STEPS):
            source = turned[m, pl.ds(j, 8, stride=STEPS), :]
            for c in range(3):
                source = source + lb_ref[m * EQ + 1 + c] * field_ref[8 * j : 8 * j + 8, c * columns : (c + 1) * columns]
            source = source * dru_ref[m, j]
            value = source if value is None else fu_ref[m, j] * value + source
            values.append(value)
        entry, _ = up_entry(gu_ref[m, STEPS - 1], value)
        values = [v + gu_ref[m, j] * entry for j, v in enumerate(values)]
        map_ref[UP * EQ + m : UP * EQ + m + 1] = values[-1][7:8]
        value = None
        for j in reversed(range(STEPS)):
            source = values[j] * rd_ref[m, j]
            value = source if value is None else fd_ref[m, j] * value + source
            values[j] = value
        entry, _ = down_entry(gd_ref[m, 0], value)
        for j in range(STEPS):
            values[j] = values[j] + gd_ref[m, j] * entry
            h_ref[m, j] = values[j]
        map_ref[DOWN * EQ + m : DOWN * EQ + m + 1] = values[0][0:1]


def close_kernel(count, *refs):
    maps = refs[:count]
    h_ref, gf_ref, pd_ref, rb_ref, spd_ref, out_ref, all_ref, modal, turned, ready, sem = refs[count:]
    here = lax.axis_index("wall")
    for r, ref in enumerate(maps):
        all_ref[lax.rem(here + count - r, count)] = ref[...]

    def get(j, kind):
        return all_ref[j, kind * EQ : (kind + 1) * EQ]

    ahead = jnp.maximum(spd_ref[:EQ], 0.0)
    back = jnp.maximum(-spd_ref[:EQ], 0.0)
    first = [all_ref[j, FIRST_VISC : FIRST_VISC + 1] for j in range(count)]
    last = [all_ref[j, LAST_VISC : LAST_VISC + 1] for j in range(count)]
    step = [all_ref[j, LAST_STEP : LAST_STEP + 1] for j in range(count)]
    share = [1.0 / (1.0 + step[j] * (ahead + last[j])) for j in range(count)]
    zero = jnp.zeros((EQ, LANES), jnp.float32)
    entry, entries, mine_up = zero, [], zero
    for j in range(count):
        if j > 0:
            entry = entry + first[j] / (ahead + first[j]) * get(j - 1, LSL)
        entries.append(entry)
        mine_up = jnp.where(here == j, entry, mine_up)
        entry = get(j, PN) * entry + get(j, UP)
        if j < count - 1:
            entry = entry + share[j] * step[j] * last[j] * get(j + 1, LSF)
    above, mine_down = zero, zero
    for j in reversed(range(count)):
        if j < count - 1:
            above = above + share[j] * last[j] / (back + last[j]) * get(j + 1, LSF)
        mine_down = jnp.where(here == j, above, mine_down)
        above = get(j, PD0) * above + get(j, G0) * entries[j] + get(j, DOWN)
    for m in range(EQ):
        up = jnp.broadcast_to(mine_up[m : m + 1], (8, LANES))
        down = jnp.broadcast_to(mine_down[m : m + 1], (8, LANES))
        for j in range(STEPS):
            modal[m, j] = h_ref[m, j] + gf_ref[m, j] * up + pd_ref[m, j] * down
    copies = []
    for q in range(EQ):
        weight = [rb_ref[q * EQ + m] for m in range(EQ)]
        for j in range(STEPS):
            total = weight[0] * modal[0, j]
            for m in range(1, EQ):
                total = total + weight[m] * modal[m, j]
            turned[q, pl.ds(j, 8, stride=STEPS), :] = total
        ready[q] = jnp.transpose(turned[q])
        copy = pltpu.make_async_copy(ready.at[q], out_ref.at[q], sem.at[q])
        copy.start()
        copies.append(copy)
    for copy in copies:
        copy.wait()


def swaps(count, side):
    if side == 0:
        return [(i, i ^ 1) for i in range(count)]
    return [(i, (i + (1 if i % 2 else -1)) % count) for i in range(count)]


def local(
    state,
    advect,
    dtau,
    viscosity,
    mode_speed,
    left_modes,
    right_modes,
    source_jac,
    elem_owner,
    elem_tile,
    elem_offset,
    elem_height,
    elem_force,
    elem_width,
):
    f32 = jnp.float32
    cells = (state.shape[1], state.shape[2])
    cells_s, cells_g = cells
    columns = cells_s * cells_g
    count_s, count_g, count_w = (lax.axis_size(name) for name in ("stream", "girth", "wall"))
    held = elem_owner.shape[0]
    shared = count_s == 4 and count_g == 2 and held <= 8
    sides = 1 if count_g == 2 else 2
    extra = 8 if shared else 0
    small = (advect, mode_speed.reshape(1, EQ), left_modes, right_modes, source_jac)
    outs = [(EQ * 2 * cells_g + extra, LANES)] * 2
    outs += [(EQ * 2 * cells_s + extra, LANES)] * sides + [(8, LANES)] + [part.shape for part in small]
    packed = call(
        functools.partial(pack_kernel, cells, held, sides, len(small)),
        outs,
        state,
        elem_owner.T,
        elem_tile.reshape(1, held),
        elem_offset.T,
        elem_height.reshape(1, held),
        elem_force.T,
        elem_width.reshape(1, held),
        *small,
        scratch=[((1, held), jnp.int32), ((1, held), jnp.int32), ((2, held), f32), ((1, held), f32)]
        + [((3, held), f32), ((1, held), f32)]
        + [((EQ, cells_s, 8, LANES), f32)] * sides,
        far=range(7 + len(small)),
        copies=sides + 6 + 4 * EQ + len(small),
    )
    pay, small = packed[2 + sides], packed[3 + sides :]
    halo_a = lax.ppermute(packed[0], "stream", swaps(count_s, 0))
    halo_b = lax.ppermute(packed[1], "stream", swaps(count_s, 1))
    halo_g = [lax.ppermute(packed[2 + i], "girth", swaps(count_g, i)) for i in range(sides)]
    wide = (EQ, STEPS, 8, LANES)
    r0, adv, lb, rb, fu, gu, fd, gd, dru, rd, gf, pd, crow, spd = call(
        functools.partial(coef_kernel, cells),
        [(EQ * columns, LANES), (2, columns, LANES), (EQ * EQ, 8, LANES), (EQ * EQ, 8, LANES)]
        + [wide] * 8
        + [(MAP_ROWS, LANES), (8, LANES)],
        state.reshape(EQ * columns, LANES),
        small[0],
        dtau.reshape(columns, LANES),
        viscosity.reshape(columns, LANES),
        *small[1:],
        scratch=[((2, LANES, columns), f32), ((EQ, 8, LANES), f32)],
        cost=4 << 20,
    )
    if shared:
        (bundle,) = call(
            functools.partial(bundle_kernel, cells), [(8, LANES)], pay, halo_a, halo_b, halo_g[0], crow
        )
        across = [(i, i ^ 5) for i in range(8)]
        elems = (bundle, lax.ppermute(bundle, ("stream", "girth"), across))
    else:
        elems = (lax.all_gather(pay, ("stream", "girth")),)
    (turned,) = call(
        functools.partial(halo_kernel, cells, (count_s, count_g), sides),
        [(EQ, LANES, columns)],
        halo_a, halo_b, *halo_g, r0, adv, lb,
        scratch=[((EQ * columns, LANES), f32)],
        cost=1 << 20,
    )
    h, block_map = call(
        functools.partial(sweep_kernel, cells, count_g, shared),
        [wide, (MAP_ROWS, LANES)],
        turned, lb, fu, gu, fd, gd, dru, rd, crow, *elems,
        scratch=[((LANES, 3 * columns), f32)],
        cost=1 << 20,
    )
    maps = [block_map]
    for r in range(1, count_w):
        maps.append(lax.ppermute(block_map, "wall", [(i, (i + r) % count_w) for i in range(count_w)]))
    (out,) = call(
        functools.partial(close_kernel, count_w),
        [(EQ, columns, LANES)],
        *maps, h, gf, pd, rb, spd,
        scratch=[((count_w, MAP_ROWS, LANES), f32), (wide, f32), ((EQ, LANES, columns), f32)]
        + [((EQ, columns, LANES), f32)],
        cost=1 << 20,
        far_out=(0,),
        copies=EQ,
    )
    return out.reshape(state.shape)


def solution(mesh):
    in_specs = (
        P(None, "stream", "girth", "wall"),
        P(None, "stream", "girth"),
        P("stream", "girth", "wall"),
        P("stream", "girth", "wall"),
        P(),
        P(),
        P(),
        P(),
        P(("stream", "girth"), None),
        P(("stream", "girth")),
        P(("stream", "girth"), None),
        P(("stream", "girth")),
        P(("stream", "girth"), None),
        P(("stream", "girth")),
    )
    out_specs = P(None, "stream", "girth", "wall")
    return jax.shard_map(local, mesh=mesh, in_specs=in_specs, out_specs=out_specs, check_vma=False)
```

```python
import functools
import math

import jax
import jax.numpy as jnp
from jax import lax
from jax.experimental import pallas as pl
from jax.experimental.pallas import tpu as pltpu
from jax.sharding import PartitionSpec as P

TILE = 8
EQ = 6
LANES = 128
STEPS = 16
HIGHEST = lax.Precision.HIGHEST
NT = (((1,), (1,)), ((), ()))
PN, PD0, G0, LSF, LSL, UP, DOWN = range(7)
FIRST_VISC, LAST_VISC, LAST_STEP = 42, 43, 44
MAP_ROWS = 48


def call(kernel, outs, *args, scratch=(), cost=0, far=(), far_out=(), copies=0):
    shapes = [jax.ShapeDtypeStruct(shape, jnp.float32) for shape in outs]

    def spec(is_far):
        return pl.BlockSpec(memory_space=pltpu.HBM if is_far else pltpu.VMEM)

    args = [pltpu.with_memory_space_constraint(part, pltpu.HBM) if i in far else part for i, part in enumerate(args)]
    return pl.pallas_call(
        kernel,
        out_shape=shapes,
        in_specs=[spec(i in far) for i in range(len(args))],
        out_specs=[spec(i in far_out) for i in range(len(outs))],
        scratch_shapes=[pltpu.VMEM(shape, kind) for shape, kind in scratch]
        + ([pltpu.SemaphoreType.DMA((copies,))] if copies else []),
        compiler_params=pltpu.CompilerParams(vmem_limit_bytes=16 << 20),
        cost_estimate=pl.CostEstimate(flops=cost, bytes_accessed=cost, transcendentals=0),
    )(*args)


def sub_iota(shape=(8, LANES)):
    return lax.broadcasted_iota(jnp.int32, shape, 0)


def up_entry(factor, offset):
    row = sub_iota()
    for reach in (1, 2, 4):
        inside = row >= reach
        offset = jnp.where(inside, factor * pltpu.roll(offset, reach, 0) + offset, offset)
        factor = jnp.where(inside, factor * pltpu.roll(factor, reach, 0), factor)
    return jnp.where(row >= 1, pltpu.roll(offset, 1, 0), 0.0), jnp.where(row >= 1, pltpu.roll(factor, 1, 0), 1.0)


def down_entry(factor, offset):
    row = sub_iota()
    for reach in (1, 2, 4):
        inside = row < 8 - reach
        offset = jnp.where(inside, factor * pltpu.roll(offset, 8 - reach, 0) + offset, offset)
        factor = jnp.where(inside, factor * pltpu.roll(factor, 8 - reach, 0), factor)
    return jnp.where(row < 7, pltpu.roll(offset, 7, 0), 0.0), jnp.where(row < 7, pltpu.roll(factor, 7, 0), 1.0)


def pack_kernel(
    cells, held, sides, small, state_ref, owner_ref, tile_ref, offset_ref, height_ref, force_ref, width_ref,
    *refs,
):
    cells_s, cells_g = cells
    small_in, refs = refs[:small], refs[small:]
    out_s, out_g, refs = refs[:2], refs[2 : 2 + sides], refs[2 + sides :]
    pay_ref, small_out, refs = refs[0], refs[1 : 1 + small], refs[1 + small :]
    owner, tile, offset, height, force, width = refs[:6]
    edges, sem = refs[6:-1], refs[-1]
    odd_s = lax.rem(lax.axis_index("stream"), 2)
    odd_g = lax.rem(lax.axis_index("girth"), 2)
    copies = []

    def start(source, target):
        copy = pltpu.make_async_copy(source, target, sem.at[len(copies)])
        copy.start()
        copies.append(copy)

    for side in range(sides):
        low = odd_g if side == 0 else 1 - odd_g
        at = pl.multiple_of((cells_g - 8) * (1 - low), 8)
        start(state_ref.at[:, :, pl.ds(at, 8), :], edges[side])
    for pair in zip(
        (owner_ref, tile_ref, offset_ref, height_ref, force_ref, width_ref),
        (owner, tile, offset, height, force, width),
    ):
        start(*pair)
    slab = 2 * cells_g
    for side, out_ref in enumerate(out_s):
        low = odd_s if side == 0 else 1 - odd_s
        at = (cells_s - 2) * (1 - low)
        for q in range(EQ):
            for r in range(2):
                base = q * slab + r * cells_g
                start(state_ref.at[q, at + r], out_ref.at[base : base + cells_g])
    for pair in zip(small_in, small_out):
        start(*pair)
    for copy in copies[sides : sides + 6]:
        copy.wait()
    tiles_g = cells_g // TILE
    number = tile[...].astype(jnp.float32)
    tile_s = jnp.floor(number * (1.0 / tiles_g))
    tile_g = number - tile_s * tiles_g
    wide = width[...]
    amplitude = 1.0 / (wide * wide * wide * math.pi**1.5)
    pay_ref[...] = jnp.zeros_like(pay_ref)
    pay_ref[0:1, :held] = tile_s * TILE + offset[0:1]
    pay_ref[1:2, :held] = tile_g * TILE + offset[1:2]
    pay_ref[2:3, :held] = height[...]
    pay_ref[3:4, :held] = 1.0 / (wide * wide)
    pay_ref[4:7, :held] = force[...] * amplitude
    pay_ref[7:8, :held] = owner[...].astype(jnp.float32)
    ends = [(ref, EQ * slab) for ref in out_s] + [(ref, 2 * EQ * cells_s) for ref in out_g]
    for out_ref, rows in ends:
        if out_ref.shape[0] > rows:
            out_ref[rows:, :] = pay_ref[...]
    for side, out_ref in enumerate(out_g):
        copies[side].wait()
        low = odd_g if side == 0 else 1 - odd_g
        flat = edges[side].reshape(EQ * cells_s * 8, LANES)
        for r in range(2):
            for q in range(EQ):
                out_ref[(r * EQ + q) * cells_s : (r * EQ + q + 1) * cells_s, :] = flat[
                    pl.ds(q * cells_s * 8 + 6 * (1 - low) + r, cells_s, stride=8), :
                ]
    for copy in copies[sides + 6 :]:
        copy.wait()


def coef_kernel(
    cells, state_ref, advect_ref, dtau_ref, visc_ref, speed_ref, left_ref, right_ref, source_ref,
    r0_ref, adv_ref, lb_ref, rb_ref, fu_ref, gu_ref, fd_ref, gd_ref, dru_ref, rd_ref, gf_ref, pd_ref,
    crow_ref, spd_ref, turned, speeds,
):
    cells_s, cells_g = cells
    columns = cells_s * cells_g
    tiles = columns // 8
    crow_ref[LAST_STEP + 1 :] = jnp.zeros((MAP_ROWS - LAST_STEP - 1, LANES), jnp.float32)
    spd_ref[...] = jnp.zeros_like(spd_ref)
    for m in range(EQ):
        speeds[m] = jnp.broadcast_to(speed_ref[0:1, m : m + 1], (8, LANES))
        spd_ref[m : m + 1] = jnp.broadcast_to(speed_ref[0:1, m : m + 1], (1, LANES))
        for q in range(EQ):
            lb_ref[m * EQ + q] = jnp.broadcast_to(left_ref[m : m + 1, q : q + 1], (8, LANES))
            rb_ref[m * EQ + q] = jnp.broadcast_to(right_ref[m : m + 1, q : q + 1], (8, LANES))
    on = sub_iota((cells_g, cells_g)) == lax.broadcasted_iota(jnp.int32, (cells_g, cells_g), 1)
    for d in range(2):
        for s in range(cells_s):
            line = jnp.broadcast_to(advect_ref[d, s : s + 1, :], (cells_g, cells_g))
            line = jnp.sum(jnp.where(on, line, 0.0), axis=1, keepdims=True)
            adv_ref[d, s * cells_g : (s + 1) * cells_g, :] = jnp.broadcast_to(line, (cells_g, LANES))
    girth = sub_iota((cells_g, LANES))
    lane = lax.broadcasted_iota(jnp.int32, (cells_g, LANES), 1)
    for s in range(cells_s):
        rows = slice(s * cells_g, (s + 1) * cells_g)
        speed_s, speed_g, visc = adv_ref[0, rows], adv_ref[1, rows], visc_ref[rows]
        state = [state_ref[q * columns + s * cells_g : q * columns + (s + 1) * cells_g] for q in range(EQ)]
        near_up, near_down = 0.125 - speed_s * (2.0 / 3.0), 0.125 + speed_s * (2.0 / 3.0)
        far_up, far_down = speed_s * (1.0 / 12.0) - 0.03125, -0.03125 - speed_s * (1.0 / 12.0)
        right1 = jnp.where(girth < cells_g - 1, 0.125 - speed_g * (2.0 / 3.0), 0.0)
        left1 = jnp.where(girth >= 1, 0.125 + speed_g * (2.0 / 3.0), 0.0)
        right2 = jnp.where(girth < cells_g - 2, speed_g * (1.0 / 12.0) - 0.03125, 0.0)
        left2 = jnp.where(girth >= 2, -0.03125 - speed_g * (1.0 / 12.0), 0.0)
        above = jnp.where(lane < LANES - 1, visc, 0.0)
        below = jnp.where(lane >= 1, visc, 0.0)
        centre = -0.375 - 2.0 * visc
        for q in range(EQ):
            here = state[q]
            total = centre * here
            for shift, weight in ((1, near_up), (-1, near_down), (2, far_up), (-2, far_down)):
                if 0 <= s + shift < cells_s:
                    at = q * columns + (s + shift) * cells_g
                    total = total + weight * state_ref[at : at + cells_g]
            total = total + right1 * pltpu.roll(here, cells_g - 1, 0) + left1 * pltpu.roll(here, 1, 0)
            total = total + right2 * pltpu.roll(here, cells_g - 2, 0) + left2 * pltpu.roll(here, 2, 0)
            total = total + above * pltpu.roll(here, LANES - 1, 1) + below * pltpu.roll(here, 1, 1)
            for f in range(EQ):
                total = total + jnp.broadcast_to(source_ref[q : q + 1, f : f + 1], (cells_g, LANES)) * state[f]
            r0_ref[q * columns + s * cells_g : q * columns + (s + 1) * cells_g] = total
    sub, lanes = sub_iota(), lax.broadcasted_iota(jnp.int32, (8, LANES), 1)
    ends = ((sub == 0) & (lanes == 0)) | ((sub == 1) & (lanes == LANES - 1))
    ends = jnp.where(ends, 1.0, 0.0)
    edge = [
        lax.dot_general(
            ends, state_ref[q * columns : (q + 1) * columns], NT, precision=HIGHEST,
            preferred_element_type=jnp.float32,
        )
        for q in range(EQ)
    ]
    for m in range(EQ):
        mixed = lb_ref[m * EQ] * edge[0]
        for q in range(1, EQ):
            mixed = mixed + lb_ref[m * EQ + q] * edge[q]
        crow_ref[LSF * EQ + m : LSF * EQ + m + 1] = mixed[0:1]
        crow_ref[LSL * EQ + m : LSL * EQ + m + 1] = mixed[1:2]
    turned[0] = jnp.transpose(dtau_ref[...])
    turned[1] = jnp.transpose(visc_ref[...])
    crow_ref[FIRST_VISC : FIRST_VISC + 1] = turned[1, 0:1]
    crow_ref[LAST_VISC : LAST_VISC + 1] = turned[1, LANES - 1 : LANES]
    crow_ref[LAST_STEP : LAST_STEP + 1] = turned[0, LANES - 1 : LANES]

    def mode(m, carry):
        ahead = jnp.maximum(speeds[m], 0.0)
        back = jnp.maximum(-speeds[m], 0.0)
        step = [turned[0, pl.ds(j, 8, stride=STEPS), :] for j in range(STEPS)]
        visc = [turned[1, pl.ds(j, 8, stride=STEPS), :] for j in range(STEPS)]
        product, ups = None, []
        for j in range(STEPS):
            a = step[j] * (ahead + visc[j])
            ru = 1.0 / (1.0 + a)
            fu = a * ru
            product = fu if product is None else fu * product
            fu_ref[m, j], gu_ref[m, j], dru_ref[m, j] = fu, product, step[j] * ru
            ups.append(product)
        _, outer = up_entry(product, jnp.zeros_like(product))
        ups = [p * outer for p in ups]
        product, value, downs, values = None, None, [None] * STEPS, [None] * STEPS
        for j in reversed(range(STEPS)):
            b = step[j] * (back + visc[j])
            rd = 1.0 / (1.0 + b)
            fd = b * rd
            source = ups[j] * rd
            product = fd if product is None else fd * product
            value = source if value is None else fd * value + source
            fd_ref[m, j], gd_ref[m, j], rd_ref[m, j] = fd, product, rd
            downs[j], values[j] = product, value
        entry, outer = down_entry(product, value)
        for j in range(STEPS):
            gf_ref[m, j] = values[j] + downs[j] * entry
            pd_ref[m, j] = downs[j] * outer
        rows = (
            (PN, ups[-1][7:8]),
            (PD0, (downs[0] * outer)[0:1]),
            (G0, (values[0] + downs[0] * entry)[0:1]),
        )
        for kind, row in rows:
            crow_ref[pl.ds(kind * EQ + m, 1), :] = row
        return carry

    lax.fori_loop(0, EQ, mode, 0)


def bundle_kernel(cells, pay_ref, a_ref, b_ref, g_ref, one_ref, two_ref, crow_ref, out_ref, kept_ref):
    cells_s, cells_g = cells
    at_s, at_g = EQ * 2 * cells_g, EQ * 2 * cells_s
    far = one_ref[...] + pltpu.roll(two_ref[...], 8, 1)
    out_ref[...] = far
    kept = pay_ref[...] + pltpu.roll(a_ref[at_s : at_s + 8], 8, 1) + pltpu.roll(b_ref[at_s : at_s + 8], 16, 1)
    kept_ref[...] = kept + pltpu.roll(g_ref[at_g : at_g + 8], 24, 1) + pltpu.roll(far, 32, 1)


def halo_kernel(cells, counts, sides, a_ref, b_ref, *refs):
    cells_s, cells_g = cells
    count_s, count_g = counts
    columns = cells_s * cells_g
    g_refs, (r0_ref, adv_ref, lb_ref, turned, res_ref) = refs[:sides], refs[sides:]
    at_s, at_g = lax.axis_index("stream"), lax.axis_index("girth")
    odd_s, odd_g = lax.rem(at_s, 2) == 1, lax.rem(at_g, 2) == 1
    low_s = jnp.where(at_s > 0, 1.0, 0.0)
    high_s = jnp.where(at_s < count_s - 1, 1.0, 0.0)
    low_g = jnp.where(at_g > 0, 1.0, 0.0)
    high_g = jnp.where(at_g < count_g - 1, 1.0, 0.0)
    speed = [adv_ref[0, s * cells_g : (s + 1) * cells_g] for s in range(cells_s)]
    sub = sub_iota()
    zero = jnp.zeros((8, LANES), jnp.float32)
    turn = []
    for s in range(cells_s):
        lead = adv_ref[1, s * cells_g : s * cells_g + 8]
        tail = adv_ref[1, (s + 1) * cells_g - 8 : (s + 1) * cells_g]
        near, far = low_g * (0.125 + lead * (2.0 / 3.0)), low_g * (-0.03125 - lead * (1.0 / 12.0))
        near_low = jnp.where(sub == 0, near, jnp.where(sub == 1, far, zero))
        far_low = jnp.where(sub == 0, far, zero)
        near, far = high_g * (0.125 - tail * (2.0 / 3.0)), high_g * (tail * (1.0 / 12.0) - 0.03125)
        near_high = jnp.where(sub == 7, near, jnp.where(sub == 6, far, zero))
        far_high = jnp.where(sub == 7, far, zero)
        turn.append((near_low, far_low, near_high, far_high))
    wide = cells_g
    for q in range(EQ):
        slab = slice(q * 2 * wide, (q + 1) * 2 * wide)
        slab_a, slab_b = a_ref[slab], b_ref[slab]
        low, high = jnp.where(odd_s, slab_a, slab_b), jnp.where(odd_s, slab_b, slab_a)
        for s in range(cells_s):
            rows = slice(q * columns + s * wide, q * columns + (s + 1) * wide)
            total = r0_ref[rows]
            if s == 0:
                total = total + low_s * (0.125 + speed[s] * (2.0 / 3.0)) * low[wide:]
                total = total + low_s * (-0.03125 - speed[s] * (1.0 / 12.0)) * low[:wide]
            if s == 1:
                total = total + low_s * (-0.03125 - speed[s] * (1.0 / 12.0)) * low[wide:]
            if s == cells_s - 2:
                total = total + high_s * (speed[s] * (1.0 / 12.0) - 0.03125) * high[:wide]
            if s == cells_s - 1:
                total = total + high_s * (0.125 - speed[s] * (2.0 / 3.0)) * high[:wide]
                total = total + high_s * (speed[s] * (1.0 / 12.0) - 0.03125) * high[wide:]
            near_low, far_low, near_high, far_high = turn[s]
            at = (q * cells_s + s, (EQ + q) * cells_s + s)
            part = [jnp.broadcast_to(g_refs[0][i : i + 1], (8, LANES)) for i in at]
            part_low = part_high = part
            if sides > 1:
                other = [jnp.broadcast_to(g_refs[1][i : i + 1], (8, LANES)) for i in at]
                part_low = [jnp.where(odd_g, x, y) for x, y in zip(part, other)]
                part_high = [jnp.where(odd_g, y, x) for x, y in zip(part, other)]
            lead, tail = slice(rows.start, rows.start + 8), slice(rows.stop - 8, rows.stop)
            if wide > 16:
                res_ref[rows] = total
            res_ref[lead] = total[:8] + near_low * part_low[1] + far_low * part_low[0]
            res_ref[tail] = total[wide - 8 :] + near_high * part_high[0] + far_high * part_high[1]
    tiles = columns // 8
    for m in range(EQ):
        total = None
        for q in range(EQ):
            part = lb_ref[m * EQ + q][None] * res_ref[q * columns : (q + 1) * columns].reshape(tiles, 8, LANES)
            total = part if total is None else total + part
        turned[m] = jnp.transpose(total.reshape(columns, LANES))


def sweep_kernel(
    cells, count_g, shared, turned, lb_ref, fu_ref, gu_ref, fd_ref, gd_ref, dru_ref, rd_ref, crow_ref, *refs
):
    cells_s, cells_g = cells
    columns = cells_s * cells_g
    elems = refs[:-3]
    h_ref, map_ref, field_ref = refs[-3:]
    at_s, at_g, at_w = (lax.axis_index(name) for name in ("stream", "girth", "wall"))
    mine = (at_s * count_g + at_g).astype(jnp.float32)
    base_s = sub_iota((cells_s, LANES)).astype(jnp.float32) + 0.5
    base_g = sub_iota((cells_g, LANES)).astype(jnp.float32) + 0.5
    first = sub_iota() * STEPS + at_w * LANES
    base_w = jnp.concatenate([first + j for j in range(STEPS)], axis=0).astype(jnp.float32) + 0.5

    def spread(pay):
        sharp = -pay[3:4]
        prof_s = jnp.exp(sharp * (base_s - pay[0:1]) ** 2)
        prof_g = jnp.exp(sharp * (base_g - pay[1:2]) ** 2)
        prof_w = jnp.exp(sharp * (base_w - pay[2:3]) ** 2)
        push = jnp.where(pay[7:8] == mine, pay[4:7], 0.0)
        plane = jnp.concatenate([prof_g * prof_s[s : s + 1] for s in range(cells_s)], axis=0)
        weights = jnp.concatenate([plane * push[c : c + 1] for c in range(3)], axis=0)
        return lax.dot_general(prof_w, weights, NT, precision=HIGHEST, preferred_element_type=jnp.float32)

    if shared:
        field_ref[...] = spread(elems[0][...] + pltpu.roll(elems[1][...], 48, 1))
    else:
        field_ref[...] = jnp.zeros_like(field_ref)

        def chunk(i, carry):
            field_ref[...] += spread(elems[0][i])
            return carry

        lax.fori_loop(0, elems[0].shape[0], chunk, 0)
    map_ref[...] = crow_ref[...]
    for m in range(EQ):
        value, values = None, []
        for j in range(STEPS):
            source = turned[m, pl.ds(j, 8, stride=STEPS), :]
            for c in range(3):
                source = source + lb_ref[m * EQ + 1 + c] * field_ref[8 * j : 8 * j + 8, c * columns : (c + 1) * columns]
            source = source * dru_ref[m, j]
            value = source if value is None else fu_ref[m, j] * value + source
            values.append(value)
        entry, _ = up_entry(gu_ref[m, STEPS - 1], value)
        values = [v + gu_ref[m, j] * entry for j, v in enumerate(values)]
        map_ref[UP * EQ + m : UP * EQ + m + 1] = values[-1][7:8]
        value = None
        for j in reversed(range(STEPS)):
            source = values[j] * rd_ref[m, j]
            value = source if value is None else fd_ref[m, j] * value + source
            values[j] = value
        entry, _ = down_entry(gd_ref[m, 0], value)
        for j in range(STEPS):
            values[j] = values[j] + gd_ref[m, j] * entry
            h_ref[m, j] = values[j]
        map_ref[DOWN * EQ + m : DOWN * EQ + m + 1] = values[0][0:1]


def close_kernel(count, *refs):
    maps = refs[:count]
    h_ref, gf_ref, pd_ref, rb_ref, spd_ref, out_ref, all_ref, modal, turned, ready, sem = refs[count:]
    here = lax.axis_index("wall")
    for r, ref in enumerate(maps):
        all_ref[source(here, r, count)] = ref[...]

    def get(j, kind):
        return all_ref[j, kind * EQ : (kind + 1) * EQ]

    ahead = jnp.maximum(spd_ref[:EQ], 0.0)
    back = jnp.maximum(-spd_ref[:EQ], 0.0)
    first = [all_ref[j, FIRST_VISC : FIRST_VISC + 1] for j in range(count)]
    last = [all_ref[j, LAST_VISC : LAST_VISC + 1] for j in range(count)]
    step = [all_ref[j, LAST_STEP : LAST_STEP + 1] for j in range(count)]
    share = [1.0 / (1.0 + step[j] * (ahead + last[j])) for j in range(count)]
    zero = jnp.zeros((EQ, LANES), jnp.float32)
    entry, entries, mine_up = zero, [], zero
    for j in range(count):
        if j > 0:
            entry = entry + first[j] / (ahead + first[j]) * get(j - 1, LSL)
        entries.append(entry)
        mine_up = jnp.where(here == j, entry, mine_up)
        entry = get(j, PN) * entry + get(j, UP)
        if j < count - 1:
            entry = entry + share[j] * step[j] * last[j] * get(j + 1, LSF)
    above, mine_down = zero, zero
    for j in reversed(range(count)):
        if j < count - 1:
            above = above + share[j] * last[j] / (back + last[j]) * get(j + 1, LSF)
        mine_down = jnp.where(here == j, above, mine_down)
        above = get(j, PD0) * above + get(j, G0) * entries[j] + get(j, DOWN)
    for m in range(EQ):
        up = jnp.broadcast_to(mine_up[m : m + 1], (8, LANES))
        down = jnp.broadcast_to(mine_down[m : m + 1], (8, LANES))
        for j in range(STEPS):
            modal[m, j] = h_ref[m, j] + gf_ref[m, j] * up + pd_ref[m, j] * down
    copies = []
    for q in range(EQ):
        weight = [rb_ref[q * EQ + m] for m in range(EQ)]
        for j in range(STEPS):
            total = weight[0] * modal[0, j]
            for m in range(1, EQ):
                total = total + weight[m] * modal[m, j]
            turned[q, pl.ds(j, 8, stride=STEPS), :] = total
        ready[q] = jnp.transpose(turned[q])
        copy = pltpu.make_async_copy(ready.at[q], out_ref.at[q], sem.at[q])
        copy.start()
        copies.append(copy)
    for copy in copies:
        copy.wait()


def source(here, r, count):
    if count & (count - 1) == 0:
        return here ^ r
    return (here + count - r) % count


def blocks(count_s, count_g, count_w, moves):
    pairs = []
    for s in range(count_s):
        for g in range(count_g):
            for w in range(count_w):
                at_s, at_g = moves[w % 2]
                target = ((s ^ at_s) * count_g + (g ^ at_g)) * count_w + w
                pairs.append(((s * count_g + g) * count_w + w, target))
    return pairs


def swaps(count, side):
    if side == 0:
        return [(i, i ^ 1) for i in range(count)]
    return [(i, (i + (1 if i % 2 else -1)) % count) for i in range(count)]


def local(
    state,
    advect,
    dtau,
    viscosity,
    mode_speed,
    left_modes,
    right_modes,
    source_jac,
    elem_owner,
    elem_tile,
    elem_offset,
    elem_height,
    elem_force,
    elem_width,
):
    f32 = jnp.float32
    cells = (state.shape[1], state.shape[2])
    cells_s, cells_g = cells
    columns = cells_s * cells_g
    count_s, count_g, count_w = (lax.axis_size(name) for name in ("stream", "girth", "wall"))
    held = elem_owner.shape[0]
    shared = count_s == 4 and count_g == 2 and count_w % 2 == 0 and held <= 8
    sides = 1 if count_g == 2 else 2
    extra = 8 if shared else 0
    small = (advect, mode_speed.reshape(1, EQ), left_modes, right_modes, source_jac)
    outs = [(EQ * 2 * cells_g + extra, LANES)] * 2
    outs += [(EQ * 2 * cells_s + extra, LANES)] * sides + [(8, LANES)] + [part.shape for part in small]
    packed = call(
        functools.partial(pack_kernel, cells, held, sides, len(small)),
        outs,
        state,
        elem_owner.T,
        elem_tile.reshape(1, held),
        elem_offset.T,
        elem_height.reshape(1, held),
        elem_force.T,
        elem_width.reshape(1, held),
        *small,
        scratch=[((1, held), jnp.int32), ((1, held), jnp.int32), ((2, held), f32), ((1, held), f32)]
        + [((3, held), f32), ((1, held), f32)]
        + [((EQ, cells_s, 8, LANES), f32)] * sides,
        far=range(7 + len(small)),
        copies=sides + 6 + 4 * EQ + len(small),
    )
    pay, small = packed[2 + sides], packed[3 + sides :]
    halo_a = lax.ppermute(packed[0], "stream", swaps(count_s, 0))
    halo_b = lax.ppermute(packed[1], "stream", swaps(count_s, 1))
    halo_g = [lax.ppermute(packed[2 + i], "girth", swaps(count_g, i)) for i in range(sides)]
    if shared:
        every = ("stream", "girth", "wall")
        far = [
            lax.ppermute(pay, every, blocks(count_s, count_g, count_w, moves))
            for moves in (((2, 0), (2, 1)), ((1, 1), (3, 1)))
        ]
    wide = (EQ, STEPS, 8, LANES)
    r0, adv, lb, rb, fu, gu, fd, gd, dru, rd, gf, pd, crow, spd = call(
        functools.partial(coef_kernel, cells),
        [(EQ * columns, LANES), (2, columns, LANES), (EQ * EQ, 8, LANES), (EQ * EQ, 8, LANES)]
        + [wide] * 8
        + [(MAP_ROWS, LANES), (8, LANES)],
        state.reshape(EQ * columns, LANES),
        small[0],
        dtau.reshape(columns, LANES),
        viscosity.reshape(columns, LANES),
        *small[1:],
        scratch=[((2, LANES, columns), f32), ((EQ, 8, LANES), f32)],
        cost=4 << 20,
    )
    if shared:
        bundle, kept = call(
            functools.partial(bundle_kernel, cells),
            [(8, LANES)] * 2,
            pay, halo_a, halo_b, halo_g[0], *far, crow,
        )
        elems = (kept, lax.ppermute(bundle, "wall", [(i, i ^ 1) for i in range(count_w)]))
    else:
        elems = (lax.all_gather(pay, ("stream", "girth")),)
    (turned,) = call(
        functools.partial(halo_kernel, cells, (count_s, count_g), sides),
        [(EQ, LANES, columns)],
        halo_a, halo_b, *halo_g, r0, adv, lb,
        scratch=[((EQ * columns, LANES), f32)],
        cost=1 << 20,
    )
    h, block_map = call(
        functools.partial(sweep_kernel, cells, count_g, shared),
        [wide, (MAP_ROWS, LANES)],
        turned, lb, fu, gu, fd, gd, dru, rd, crow, *elems,
        scratch=[((LANES, 3 * columns), f32)],
        cost=1 << 20,
    )
    maps = [block_map]
    for r in range(1, count_w):
        pairs = [(int(source(i, r, count_w)), i) for i in range(count_w)]
        maps.append(lax.ppermute(block_map, "wall", pairs))
    (out,) = call(
        functools.partial(close_kernel, count_w),
        [(EQ, columns, LANES)],
        *maps, h, gf, pd, rb, spd,
        scratch=[((count_w, MAP_ROWS, LANES), f32), (wide, f32), ((EQ, LANES, columns), f32)]
        + [((EQ, columns, LANES), f32)],
        cost=1 << 20,
        far_out=(0,),
        copies=EQ,
    )
    return out.reshape(state.shape)


def solution(mesh):
    in_specs = (
        P(None, "stream", "girth", "wall"),
        P(None, "stream", "girth"),
        P("stream", "girth", "wall"),
        P("stream", "girth", "wall"),
        P(),
        P(),
        P(),
        P(),
        P(("stream", "girth"), None),
        P(("stream", "girth")),
        P(("stream", "girth"), None),
        P(("stream", "girth")),
        P(("stream", "girth"), None),
        P(("stream", "girth")),
    )
    out_specs = P(None, "stream", "girth", "wall")
    return jax.shard_map(local, mesh=mesh, in_specs=in_specs, out_specs=out_specs, check_vma=False)
```

```python
import functools
import math

import jax
import jax.numpy as jnp
from jax import lax
from jax.experimental import pallas as pl
from jax.experimental.pallas import tpu as pltpu
from jax.sharding import PartitionSpec as P

TILE = 8
EQ = 6
LANES = 128
STEPS = 16
HIGHEST = lax.Precision.HIGHEST
NT = (((1,), (1,)), ((), ()))
PN, PD0, G0, LSF, LSL, UP, DOWN = range(7)
FIRST_VISC, LAST_VISC, LAST_STEP = 42, 43, 44
MAP_ROWS = 48
AHEAD = 7


def call(kernel, outs, *args, scratch=(), cost=0, far=(), far_out=(), copies=0):
    shapes = [jax.ShapeDtypeStruct(shape, jnp.float32) for shape in outs]

    def spec(is_far):
        return pl.BlockSpec(memory_space=pltpu.HBM if is_far else pltpu.VMEM)

    args = [pltpu.with_memory_space_constraint(part, pltpu.HBM) if i in far else part for i, part in enumerate(args)]
    return pl.pallas_call(
        kernel,
        out_shape=shapes,
        in_specs=[spec(i in far) for i in range(len(args))],
        out_specs=[spec(i in far_out) for i in range(len(outs))],
        scratch_shapes=[pltpu.VMEM(shape, kind) for shape, kind in scratch]
        + ([pltpu.SemaphoreType.DMA((copies,))] if copies else []),
        compiler_params=pltpu.CompilerParams(vmem_limit_bytes=16 << 20),
        cost_estimate=pl.CostEstimate(flops=cost, bytes_accessed=cost, transcendentals=0),
    )(*args)


def sub_iota(shape=(8, LANES)):
    return lax.broadcasted_iota(jnp.int32, shape, 0)


def up_entry(factor, offset):
    row = sub_iota()
    for reach in (1, 2, 4):
        inside = row >= reach
        offset = jnp.where(inside, factor * pltpu.roll(offset, reach, 0) + offset, offset)
        factor = jnp.where(inside, factor * pltpu.roll(factor, reach, 0), factor)
    return jnp.where(row >= 1, pltpu.roll(offset, 1, 0), 0.0), jnp.where(row >= 1, pltpu.roll(factor, 1, 0), 1.0)


def down_entry(factor, offset):
    row = sub_iota()
    for reach in (1, 2, 4):
        inside = row < 8 - reach
        offset = jnp.where(inside, factor * pltpu.roll(offset, 8 - reach, 0) + offset, offset)
        factor = jnp.where(inside, factor * pltpu.roll(factor, 8 - reach, 0), factor)
    return jnp.where(row < 7, pltpu.roll(offset, 7, 0), 0.0), jnp.where(row < 7, pltpu.roll(factor, 7, 0), 1.0)


def pack_kernel(
    cells, held, sides, state_ref, owner_ref, tile_ref, offset_ref, height_ref, force_ref, width_ref,
    *refs,
):
    cells_s, cells_g = cells
    ahead, refs = refs[:AHEAD], refs[AHEAD:]
    out_s, out_g, refs = refs[:2], refs[2 : 2 + sides], refs[2 + sides :]
    pay_ref, fetched, refs = refs[0], refs[1 : 1 + AHEAD], refs[1 + AHEAD :]
    owner, tile, offset, height, force, width, sem = refs
    odd_s = lax.rem(lax.axis_index("stream"), 2)
    odd_g = lax.rem(lax.axis_index("girth"), 2)
    copies = []

    def start(source, target):
        copy = pltpu.make_async_copy(source, target, sem.at[len(copies)])
        copy.start()
        copies.append(copy)

    for pair in zip(
        (owner_ref, tile_ref, offset_ref, height_ref, force_ref, width_ref),
        (owner, tile, offset, height, force, width),
    ):
        start(*pair)
    slab = 2 * cells_g
    for side, out_ref in enumerate(out_s):
        low = odd_s if side == 0 else 1 - odd_s
        at = (cells_s - 2) * (1 - low)
        start(state_ref.at[:, pl.ds(at, 2)], out_ref.at[: EQ * slab].reshape(EQ, 2, cells_g, LANES))
    for side in range(sides):
        low = odd_g if side == 0 else 1 - odd_g
        at = (cells_g - 2) * (1 - low)
        rows = out_g[side].at[: 2 * EQ * cells_s]
        start(state_ref.at[:, :, pl.ds(at, 2), :], rows.reshape(EQ, cells_s, 2, LANES))
    for pair in zip(ahead, fetched):
        start(*pair)
    for copy in copies[:6]:
        copy.wait()
    tiles_g = cells_g // TILE
    number = tile[...].astype(jnp.float32)
    tile_s = jnp.floor(number * (1.0 / tiles_g))
    tile_g = number - tile_s * tiles_g
    wide = width[...]
    amplitude = 1.0 / (wide * wide * wide * math.pi**1.5)
    pay_ref[...] = jnp.zeros_like(pay_ref)
    pay_ref[0:1, :held] = tile_s * TILE + offset[0:1]
    pay_ref[1:2, :held] = tile_g * TILE + offset[1:2]
    pay_ref[2:3, :held] = height[...]
    pay_ref[3:4, :held] = 1.0 / (wide * wide)
    pay_ref[4:7, :held] = force[...] * amplitude
    pay_ref[7:8, :held] = owner[...].astype(jnp.float32)
    ends = [(ref, EQ * slab) for ref in out_s] + [(ref, 2 * EQ * cells_s) for ref in out_g]
    for out_ref, rows in ends:
        if out_ref.shape[0] > rows:
            out_ref[rows:, :] = pay_ref[...]
    for copy in copies[6:]:
        copy.wait()


def coef_kernel(cells, *refs):
    cells_s, cells_g = cells
    columns = cells_s * cells_g
    dtau_ref, visc_ref, speed_ref, left_ref, right_ref, source_ref, advect_ref, state_ref = refs[:8]
    (
        r0_ref, adv_ref, lb_ref, rb_ref, fu_ref, gu_ref, fd_ref, gd_ref, dru_ref, rd_ref, gf_ref, pd_ref,
        crow_ref, spd_ref, turned, speeds,
    ) = refs[8:]
    crow_ref[LAST_STEP + 1 :] = jnp.zeros((MAP_ROWS - LAST_STEP - 1, LANES), jnp.float32)
    spd_ref[...] = jnp.zeros_like(spd_ref)
    for m in range(EQ):
        speeds[m] = jnp.broadcast_to(speed_ref[0:1, m : m + 1], (8, LANES))
        spd_ref[m : m + 1] = jnp.broadcast_to(speed_ref[0:1, m : m + 1], (1, LANES))
        for q in range(EQ):
            lb_ref[m * EQ + q] = jnp.broadcast_to(left_ref[m : m + 1, q : q + 1], (8, LANES))
            rb_ref[m * EQ + q] = jnp.broadcast_to(right_ref[m : m + 1, q : q + 1], (8, LANES))
    on = sub_iota((cells_g, cells_g)) == lax.broadcasted_iota(jnp.int32, (cells_g, cells_g), 1)
    for d in range(2):
        for s in range(cells_s):
            line = jnp.broadcast_to(advect_ref[d, s : s + 1, :], (cells_g, cells_g))
            line = jnp.sum(jnp.where(on, line, 0.0), axis=1, keepdims=True)
            adv_ref[d, s * cells_g : (s + 1) * cells_g, :] = jnp.broadcast_to(line, (cells_g, LANES))
    turned[0] = jnp.transpose(dtau_ref[...])
    turned[1] = jnp.transpose(visc_ref[...])
    crow_ref[FIRST_VISC : FIRST_VISC + 1] = turned[1, 0:1]
    crow_ref[LAST_VISC : LAST_VISC + 1] = turned[1, LANES - 1 : LANES]
    crow_ref[LAST_STEP : LAST_STEP + 1] = turned[0, LANES - 1 : LANES]

    def mode(m, carry):
        ahead = jnp.maximum(speeds[m], 0.0)
        back = jnp.maximum(-speeds[m], 0.0)
        step = [turned[0, pl.ds(j, 8, stride=STEPS), :] for j in range(STEPS)]
        visc = [turned[1, pl.ds(j, 8, stride=STEPS), :] for j in range(STEPS)]
        product, ups = None, []
        for j in range(STEPS):
            a = step[j] * (ahead + visc[j])
            ru = 1.0 / (1.0 + a)
            fu = a * ru
            product = fu if product is None else fu * product
            fu_ref[m, j], gu_ref[m, j], dru_ref[m, j] = fu, product, step[j] * ru
            ups.append(product)
        _, outer = up_entry(product, jnp.zeros_like(product))
        ups = [p * outer for p in ups]
        product, value, downs, values = None, None, [None] * STEPS, [None] * STEPS
        for j in reversed(range(STEPS)):
            b = step[j] * (back + visc[j])
            rd = 1.0 / (1.0 + b)
            fd = b * rd
            source = ups[j] * rd
            product = fd if product is None else fd * product
            value = source if value is None else fd * value + source
            fd_ref[m, j], gd_ref[m, j], rd_ref[m, j] = fd, product, rd
            downs[j], values[j] = product, value
        entry, outer = down_entry(product, value)
        for j in range(STEPS):
            gf_ref[m, j] = values[j] + downs[j] * entry
            pd_ref[m, j] = downs[j] * outer
        rows = (
            (PN, ups[-1][7:8]),
            (PD0, (downs[0] * outer)[0:1]),
            (G0, (values[0] + downs[0] * entry)[0:1]),
        )
        for kind, row in rows:
            crow_ref[pl.ds(kind * EQ + m, 1), :] = row
        return carry

    lax.fori_loop(0, EQ, mode, 0)
    girth = sub_iota((cells_g, LANES))
    lane = lax.broadcasted_iota(jnp.int32, (cells_g, LANES), 1)
    for s in range(cells_s):
        rows = slice(s * cells_g, (s + 1) * cells_g)
        speed_s, speed_g, visc = adv_ref[0, rows], adv_ref[1, rows], visc_ref[rows]
        state = [state_ref[q * columns + s * cells_g : q * columns + (s + 1) * cells_g] for q in range(EQ)]
        near_up, near_down = 0.125 - speed_s * (2.0 / 3.0), 0.125 + speed_s * (2.0 / 3.0)
        far_up, far_down = speed_s * (1.0 / 12.0) - 0.03125, -0.03125 - speed_s * (1.0 / 12.0)
        right1 = jnp.where(girth < cells_g - 1, 0.125 - speed_g * (2.0 / 3.0), 0.0)
        left1 = jnp.where(girth >= 1, 0.125 + speed_g * (2.0 / 3.0), 0.0)
        right2 = jnp.where(girth < cells_g - 2, speed_g * (1.0 / 12.0) - 0.03125, 0.0)
        left2 = jnp.where(girth >= 2, -0.03125 - speed_g * (1.0 / 12.0), 0.0)
        above = jnp.where(lane < LANES - 1, visc, 0.0)
        below = jnp.where(lane >= 1, visc, 0.0)
        centre = -0.375 - 2.0 * visc
        for q in range(EQ):
            here = state[q]
            total = centre * here
            for shift, weight in ((1, near_up), (-1, near_down), (2, far_up), (-2, far_down)):
                if 0 <= s + shift < cells_s:
                    at = q * columns + (s + shift) * cells_g
                    total = total + weight * state_ref[at : at + cells_g]
            total = total + right1 * pltpu.roll(here, cells_g - 1, 0) + left1 * pltpu.roll(here, 1, 0)
            total = total + right2 * pltpu.roll(here, cells_g - 2, 0) + left2 * pltpu.roll(here, 2, 0)
            total = total + above * pltpu.roll(here, LANES - 1, 1) + below * pltpu.roll(here, 1, 1)
            for f in range(EQ):
                total = total + jnp.broadcast_to(source_ref[q : q + 1, f : f + 1], (cells_g, LANES)) * state[f]
            r0_ref[q * columns + s * cells_g : q * columns + (s + 1) * cells_g] = total
    sub, lanes = sub_iota(), lax.broadcasted_iota(jnp.int32, (8, LANES), 1)
    ends = ((sub == 0) & (lanes == 0)) | ((sub == 1) & (lanes == LANES - 1))
    ends = jnp.where(ends, 1.0, 0.0)
    edge = [
        lax.dot_general(
            ends, state_ref[q * columns : (q + 1) * columns], NT, precision=HIGHEST,
            preferred_element_type=jnp.float32,
        )
        for q in range(EQ)
    ]
    for m in range(EQ):
        mixed = lb_ref[m * EQ] * edge[0]
        for q in range(1, EQ):
            mixed = mixed + lb_ref[m * EQ + q] * edge[q]
        crow_ref[LSF * EQ + m : LSF * EQ + m + 1] = mixed[0:1]
        crow_ref[LSL * EQ + m : LSL * EQ + m + 1] = mixed[1:2]


def pair_kernel(one_ref, two_ref, crow_ref, out_ref):
    out_ref[...] = one_ref[...] + pltpu.roll(two_ref[...], 8, 1)


def halo_kernel(cells, counts, sides, a_ref, b_ref, *refs):
    cells_s, cells_g = cells
    count_s, count_g = counts
    columns = cells_s * cells_g
    g_refs, (r0_ref, adv_ref, lb_ref), refs = refs[:sides], refs[sides : sides + 3], refs[sides + 3 :]
    turned, res_ref = refs[-2:]
    if len(refs) > 2:
        pay_ref, pair_ref, kept_ref = refs[0], refs[1], refs[-3]
        rows = slice(EQ * 2 * cells_g, EQ * 2 * cells_g + 8)
        kept = pay_ref[...] + pltpu.roll(pair_ref[...], 32, 1)
        kept = kept + pltpu.roll(a_ref[rows], 8, 1) + pltpu.roll(b_ref[rows], 16, 1)
        rows = slice(EQ * 2 * cells_s, EQ * 2 * cells_s + 8)
        kept_ref[...] = kept + pltpu.roll(g_refs[0][rows], 24, 1)
    at_s, at_g = lax.axis_index("stream"), lax.axis_index("girth")
    odd_s, odd_g = lax.rem(at_s, 2) == 1, lax.rem(at_g, 2) == 1
    low_s = jnp.where(at_s > 0, 1.0, 0.0)
    high_s = jnp.where(at_s < count_s - 1, 1.0, 0.0)
    low_g = jnp.where(at_g > 0, 1.0, 0.0)
    high_g = jnp.where(at_g < count_g - 1, 1.0, 0.0)
    speed = [adv_ref[0, s * cells_g : (s + 1) * cells_g] for s in range(cells_s)]
    sub = sub_iota()
    zero = jnp.zeros((8, LANES), jnp.float32)
    turn = []
    for s in range(cells_s):
        lead = adv_ref[1, s * cells_g : s * cells_g + 8]
        tail = adv_ref[1, (s + 1) * cells_g - 8 : (s + 1) * cells_g]
        near, far = low_g * (0.125 + lead * (2.0 / 3.0)), low_g * (-0.03125 - lead * (1.0 / 12.0))
        near_low = jnp.where(sub == 0, near, jnp.where(sub == 1, far, zero))
        far_low = jnp.where(sub == 0, far, zero)
        near, far = high_g * (0.125 - tail * (2.0 / 3.0)), high_g * (tail * (1.0 / 12.0) - 0.03125)
        near_high = jnp.where(sub == 7, near, jnp.where(sub == 6, far, zero))
        far_high = jnp.where(sub == 7, far, zero)
        turn.append((near_low, far_low, near_high, far_high))
    wide = cells_g
    for q in range(EQ):
        slab = slice(q * 2 * wide, (q + 1) * 2 * wide)
        slab_a, slab_b = a_ref[slab], b_ref[slab]
        low, high = jnp.where(odd_s, slab_a, slab_b), jnp.where(odd_s, slab_b, slab_a)
        for s in range(cells_s):
            rows = slice(q * columns + s * wide, q * columns + (s + 1) * wide)
            total = r0_ref[rows]
            if s == 0:
                total = total + low_s * (0.125 + speed[s] * (2.0 / 3.0)) * low[wide:]
                total = total + low_s * (-0.03125 - speed[s] * (1.0 / 12.0)) * low[:wide]
            if s == 1:
                total = total + low_s * (-0.03125 - speed[s] * (1.0 / 12.0)) * low[wide:]
            if s == cells_s - 2:
                total = total + high_s * (speed[s] * (1.0 / 12.0) - 0.03125) * high[:wide]
            if s == cells_s - 1:
                total = total + high_s * (0.125 - speed[s] * (2.0 / 3.0)) * high[:wide]
                total = total + high_s * (speed[s] * (1.0 / 12.0) - 0.03125) * high[wide:]
            near_low, far_low, near_high, far_high = turn[s]
            at = (2 * (q * cells_s + s), 2 * (q * cells_s + s) + 1)
            part = [jnp.broadcast_to(g_refs[0][i : i + 1], (8, LANES)) for i in at]
            part_low = part_high = part
            if sides > 1:
                other = [jnp.broadcast_to(g_refs[1][i : i + 1], (8, LANES)) for i in at]
                part_low = [jnp.where(odd_g, x, y) for x, y in zip(part, other)]
                part_high = [jnp.where(odd_g, y, x) for x, y in zip(part, other)]
            lead, tail = slice(rows.start, rows.start + 8), slice(rows.stop - 8, rows.stop)
            if wide > 16:
                res_ref[rows] = total
            res_ref[lead] = total[:8] + near_low * part_low[1] + far_low * part_low[0]
            res_ref[tail] = total[wide - 8 :] + near_high * part_high[0] + far_high * part_high[1]
    tiles = columns // 8
    for m in range(EQ):
        total = None
        for q in range(EQ):
            part = lb_ref[m * EQ + q][None] * res_ref[q * columns : (q + 1) * columns].reshape(tiles, 8, LANES)
            total = part if total is None else total + part
        turned[m] = jnp.transpose(total.reshape(columns, LANES))


def sweep_kernel(
    cells, count_g, shared, turned, lb_ref, fu_ref, gu_ref, fd_ref, gd_ref, dru_ref, rd_ref, crow_ref, *refs
):
    cells_s, cells_g = cells
    columns = cells_s * cells_g
    elems = refs[:-3]
    h_ref, map_ref, field_ref = refs[-3:]
    at_s, at_g, at_w = (lax.axis_index(name) for name in ("stream", "girth", "wall"))
    mine = (at_s * count_g + at_g).astype(jnp.float32)
    base_s = sub_iota((cells_s, LANES)).astype(jnp.float32) + 0.5
    base_g = sub_iota((cells_g, LANES)).astype(jnp.float32) + 0.5
    first = sub_iota() * STEPS + at_w * LANES
    base_w = jnp.concatenate([first + j for j in range(STEPS)], axis=0).astype(jnp.float32) + 0.5

    def spread(pay):
        sharp = -pay[3:4]
        prof_s = jnp.exp(sharp * (base_s - pay[0:1]) ** 2)
        prof_g = jnp.exp(sharp * (base_g - pay[1:2]) ** 2)
        prof_w = jnp.exp(sharp * (base_w - pay[2:3]) ** 2)
        push = jnp.where(pay[7:8] == mine, pay[4:7], 0.0)
        plane = jnp.concatenate([prof_g * prof_s[s : s + 1] for s in range(cells_s)], axis=0)
        weights = jnp.concatenate([plane * push[c : c + 1] for c in range(3)], axis=0)
        return lax.dot_general(prof_w, weights, NT, precision=HIGHEST, preferred_element_type=jnp.float32)

    if shared:
        field_ref[...] = spread(elems[0][...] + pltpu.roll(elems[1][...], 48, 1))
    else:
        field_ref[...] = jnp.zeros_like(field_ref)

        def chunk(i, carry):
            field_ref[...] += spread(elems[0][i])
            return carry

        lax.fori_loop(0, elems[0].shape[0], chunk, 0)
    map_ref[...] = crow_ref[...]
    for m in range(EQ):
        value, values = None, []
        for j in range(STEPS):
            source = turned[m, pl.ds(j, 8, stride=STEPS), :]
            for c in range(3):
                source = source + lb_ref[m * EQ + 1 + c] * field_ref[8 * j : 8 * j + 8, c * columns : (c + 1) * columns]
            source = source * dru_ref[m, j]
            value = source if value is None else fu_ref[m, j] * value + source
            values.append(value)
        entry, _ = up_entry(gu_ref[m, STEPS - 1], value)
        values = [v + gu_ref[m, j] * entry for j, v in enumerate(values)]
        map_ref[UP * EQ + m : UP * EQ + m + 1] = values[-1][7:8]
        value = None
        for j in reversed(range(STEPS)):
            source = values[j] * rd_ref[m, j]
            value = source if value is None else fd_ref[m, j] * value + source
            values[j] = value
        entry, _ = down_entry(gd_ref[m, 0], value)
        for j in range(STEPS):
            values[j] = values[j] + gd_ref[m, j] * entry
            h_ref[m, j] = values[j]
        map_ref[DOWN * EQ + m : DOWN * EQ + m + 1] = values[0][0:1]


def close_kernel(count, *refs):
    maps = refs[:count]
    h_ref, gf_ref, pd_ref, rb_ref, spd_ref, out_ref, all_ref, modal, turned, ready, sem = refs[count:]
    here = lax.axis_index("wall")
    for r, ref in enumerate(maps):
        all_ref[source(here, r, count)] = ref[...]

    def get(j, kind):
        return all_ref[j, kind * EQ : (kind + 1) * EQ]

    ahead = jnp.maximum(spd_ref[:EQ], 0.0)
    back = jnp.maximum(-spd_ref[:EQ], 0.0)
    first = [all_ref[j, FIRST_VISC : FIRST_VISC + 1] for j in range(count)]
    last = [all_ref[j, LAST_VISC : LAST_VISC + 1] for j in range(count)]
    step = [all_ref[j, LAST_STEP : LAST_STEP + 1] for j in range(count)]
    share = [1.0 / (1.0 + step[j] * (ahead + last[j])) for j in range(count)]
    zero = jnp.zeros((EQ, LANES), jnp.float32)
    entry, entries, mine_up = zero, [], zero
    for j in range(count):
        if j > 0:
            entry = entry + first[j] / (ahead + first[j]) * get(j - 1, LSL)
        entries.append(entry)
        mine_up = jnp.where(here == j, entry, mine_up)
        entry = get(j, PN) * entry + get(j, UP)
        if j < count - 1:
            entry = entry + share[j] * step[j] * last[j] * get(j + 1, LSF)
    above, mine_down = zero, zero
    for j in reversed(range(count)):
        if j < count - 1:
            above = above + share[j] * last[j] / (back + last[j]) * get(j + 1, LSF)
        mine_down = jnp.where(here == j, above, mine_down)
        above = get(j, PD0) * above + get(j, G0) * entries[j] + get(j, DOWN)
    for m in range(EQ):
        up = jnp.broadcast_to(mine_up[m : m + 1], (8, LANES))
        down = jnp.broadcast_to(mine_down[m : m + 1], (8, LANES))
        for j in range(STEPS):
            modal[m, j] = h_ref[m, j] + gf_ref[m, j] * up + pd_ref[m, j] * down
    copies = []
    for k in range(3):
        for q in (2 * k, 2 * k + 1):
            weight = [rb_ref[q * EQ + m] for m in range(EQ)]
            for j in range(STEPS):
                total = weight[0] * modal[0, j]
                for m in range(1, EQ):
                    total = total + weight[m] * modal[m, j]
                turned[q, pl.ds(j, 8, stride=STEPS), :] = total
            ready[q] = jnp.transpose(turned[q])
        part = slice(2 * k, 2 * k + 2)
        copy = pltpu.make_async_copy(ready.at[part], out_ref.at[part], sem.at[k])
        copy.start()
        copies.append(copy)
    for copy in copies:
        copy.wait()


def source(here, r, count):
    if count & (count - 1) == 0:
        return here ^ r
    return (here + count - r) % count


def blocks(count_s, count_g, count_w, moves):
    pairs = []
    for s in range(count_s):
        for g in range(count_g):
            for w in range(count_w):
                at_s, at_g = moves[w % 2]
                target = ((s ^ at_s) * count_g + (g ^ at_g)) * count_w + w
                pairs.append(((s * count_g + g) * count_w + w, target))
    return pairs


def swaps(count, side):
    if side == 0:
        return [(i, i ^ 1) for i in range(count)]
    return [(i, (i + (1 if i % 2 else -1)) % count) for i in range(count)]


def local(
    state,
    advect,
    dtau,
    viscosity,
    mode_speed,
    left_modes,
    right_modes,
    source_jac,
    elem_owner,
    elem_tile,
    elem_offset,
    elem_height,
    elem_force,
    elem_width,
):
    f32 = jnp.float32
    cells = (state.shape[1], state.shape[2])
    cells_s, cells_g = cells
    columns = cells_s * cells_g
    count_s, count_g, count_w = (lax.axis_size(name) for name in ("stream", "girth", "wall"))
    held = elem_owner.shape[0]
    shared = count_s == 4 and count_g == 2 and count_w % 2 == 0 and held <= 8
    sides = 1 if count_g == 2 else 2
    extra = 8 if shared else 0
    ahead = (
        dtau.reshape(columns, LANES),
        viscosity.reshape(columns, LANES),
        mode_speed.reshape(1, EQ),
        left_modes,
        right_modes,
        source_jac,
        advect,
    )
    outs = [(EQ * 2 * cells_g + extra, LANES)] * 2
    outs += [(EQ * 2 * cells_s + extra, LANES)] * sides + [(8, LANES)] + [part.shape for part in ahead]
    packed = call(
        functools.partial(pack_kernel, cells, held, sides),
        outs,
        state,
        elem_owner.T,
        elem_tile.reshape(1, held),
        elem_offset.T,
        elem_height.reshape(1, held),
        elem_force.T,
        elem_width.reshape(1, held),
        *ahead,
        scratch=[((1, held), jnp.int32), ((1, held), jnp.int32), ((2, held), f32), ((1, held), f32)]
        + [((3, held), f32), ((1, held), f32)],
        far=range(7 + AHEAD),
        copies=sides + 8 + AHEAD,
    )
    pay, ahead = packed[2 + sides], packed[3 + sides :]
    halo_a = lax.ppermute(packed[0], "stream", swaps(count_s, 0))
    halo_b = lax.ppermute(packed[1], "stream", swaps(count_s, 1))
    halo_g = [lax.ppermute(packed[2 + i], "girth", swaps(count_g, i)) for i in range(sides)]
    if shared:
        every = ("stream", "girth", "wall")
        far = [
            lax.ppermute(pay, every, blocks(count_s, count_g, count_w, moves))
            for moves in (((1, 1), (2, 1)), ((2, 0), (3, 1)))
        ]
    wide = (EQ, STEPS, 8, LANES)
    r0, adv, lb, rb, fu, gu, fd, gd, dru, rd, gf, pd, crow, spd = call(
        functools.partial(coef_kernel, cells),
        [(EQ * columns, LANES), (2, columns, LANES), (EQ * EQ, 8, LANES), (EQ * EQ, 8, LANES)]
        + [wide] * 8
        + [(MAP_ROWS, LANES), (8, LANES)],
        *ahead,
        state.reshape(EQ * columns, LANES),
        scratch=[((2, LANES, columns), f32), ((EQ, 8, LANES), f32)],
        cost=4 << 20,
    )
    if shared:
        (pair,) = call(pair_kernel, [(8, LANES)], *far, crow)
        other = lax.ppermute(pair, "wall", [(i, i ^ 1) for i in range(count_w)])
    *kept, turned = call(
        functools.partial(halo_kernel, cells, (count_s, count_g), sides),
        [(8, LANES)] * shared + [(EQ, LANES, columns)],
        halo_a, halo_b, *halo_g, r0, adv, lb, *((pay, pair) if shared else ()),
        scratch=[((EQ * columns, LANES), f32)],
        cost=1 << 20,
    )
    elems = (*kept, other) if shared else (lax.all_gather(pay, ("stream", "girth")),)
    h, block_map = call(
        functools.partial(sweep_kernel, cells, count_g, shared),
        [wide, (MAP_ROWS, LANES)],
        turned, lb, fu, gu, fd, gd, dru, rd, crow, *elems,
        scratch=[((LANES, 3 * columns), f32)],
        cost=1 << 20,
    )
    maps = [block_map]
    for r in range(1, count_w):
        pairs = [(int(source(i, r, count_w)), i) for i in range(count_w)]
        maps.append(lax.ppermute(block_map, "wall", pairs))
    (out,) = call(
        functools.partial(close_kernel, count_w),
        [(EQ, columns, LANES)],
        *maps, h, gf, pd, rb, spd,
        scratch=[((count_w, MAP_ROWS, LANES), f32), (wide, f32), ((EQ, LANES, columns), f32)]
        + [((EQ, columns, LANES), f32)],
        cost=1 << 20,
        far_out=(0,),
        copies=3,
    )
    return out.reshape(state.shape)


def solution(mesh):
    in_specs = (
        P(None, "stream", "girth", "wall"),
        P(None, "stream", "girth"),
        P("stream", "girth", "wall"),
        P("stream", "girth", "wall"),
        P(),
        P(),
        P(),
        P(),
        P(("stream", "girth"), None),
        P(("stream", "girth")),
        P(("stream", "girth"), None),
        P(("stream", "girth")),
        P(("stream", "girth"), None),
        P(("stream", "girth")),
    )
    out_specs = P(None, "stream", "girth", "wall")
    return jax.shard_map(local, mesh=mesh, in_specs=in_specs, out_specs=out_specs, check_vma=False)
```

```python
import functools
import math

import jax
import jax.numpy as jnp
from jax import lax
from jax.experimental import pallas as pl
from jax.experimental.pallas import tpu as pltpu
from jax.sharding import PartitionSpec as P

TILE = 8
EQ = 6
LANES = 128
STEPS = 16
HIGHEST = lax.Precision.HIGHEST
HIGH = lax.Precision.HIGH
NT = (((1,), (1,)), ((), ()))
PN, PD0, G0, LSF, LSL, UP, DOWN = range(7)
FIRST_VISC, LAST_VISC, LAST_STEP = 42, 43, 44
MAP_ROWS = 48
AHEAD = 7


def call(kernel, outs, *args, scratch=(), cost=0, far=(), far_out=(), copies=0):
    shapes = [jax.ShapeDtypeStruct(shape, jnp.float32) for shape in outs]

    def spec(is_far):
        return pl.BlockSpec(memory_space=pltpu.HBM if is_far else pltpu.VMEM)

    args = [pltpu.with_memory_space_constraint(part, pltpu.HBM) if i in far else part for i, part in enumerate(args)]
    return pl.pallas_call(
        kernel,
        out_shape=shapes,
        in_specs=[spec(i in far) for i in range(len(args))],
        out_specs=[spec(i in far_out) for i in range(len(outs))],
        scratch_shapes=[pltpu.VMEM(shape, kind) for shape, kind in scratch]
        + ([pltpu.SemaphoreType.DMA((copies,))] if copies else []),
        compiler_params=pltpu.CompilerParams(vmem_limit_bytes=16 << 20),
        cost_estimate=pl.CostEstimate(flops=cost, bytes_accessed=cost, transcendentals=0),
    )(*args)


def sub_iota(shape=(8, LANES)):
    return lax.broadcasted_iota(jnp.int32, shape, 0)


def up_entry(factor, offset):
    row = sub_iota()
    for reach in (1, 2, 4):
        inside = row >= reach
        offset = jnp.where(inside, factor * pltpu.roll(offset, reach, 0) + offset, offset)
        factor = jnp.where(inside, factor * pltpu.roll(factor, reach, 0), factor)
    return jnp.where(row >= 1, pltpu.roll(offset, 1, 0), 0.0), jnp.where(row >= 1, pltpu.roll(factor, 1, 0), 1.0)


def down_entry(factor, offset):
    row = sub_iota()
    for reach in (1, 2, 4):
        inside = row < 8 - reach
        offset = jnp.where(inside, factor * pltpu.roll(offset, 8 - reach, 0) + offset, offset)
        factor = jnp.where(inside, factor * pltpu.roll(factor, 8 - reach, 0), factor)
    return jnp.where(row < 7, pltpu.roll(offset, 7, 0), 0.0), jnp.where(row < 7, pltpu.roll(factor, 7, 0), 1.0)


def pack_kernel(
    cells, held, sides, state_ref, owner_ref, tile_ref, offset_ref, height_ref, force_ref, width_ref,
    *refs,
):
    cells_s, cells_g = cells
    ahead, refs = refs[:AHEAD], refs[AHEAD:]
    out_s, out_g, refs = refs[:2], refs[2 : 2 + sides], refs[2 + sides :]
    pay_ref, fetched, refs = refs[0], refs[1 : 1 + AHEAD], refs[1 + AHEAD :]
    owner, tile, offset, height, force, width, sem = refs
    odd_s = lax.rem(lax.axis_index("stream"), 2)
    odd_g = lax.rem(lax.axis_index("girth"), 2)
    copies = []

    def start(source, target):
        copy = pltpu.make_async_copy(source, target, sem.at[len(copies)])
        copy.start()
        copies.append(copy)

    for pair in zip(
        (owner_ref, tile_ref, offset_ref, height_ref, force_ref, width_ref),
        (owner, tile, offset, height, force, width),
    ):
        start(*pair)
    slab = 2 * cells_g
    for side, out_ref in enumerate(out_s):
        low = odd_s if side == 0 else 1 - odd_s
        at = (cells_s - 2) * (1 - low)
        start(state_ref.at[:, pl.ds(at, 2)], out_ref.at[: EQ * slab].reshape(EQ, 2, cells_g, LANES))
    for side in range(sides):
        low = odd_g if side == 0 else 1 - odd_g
        at = (cells_g - 2) * (1 - low)
        rows = out_g[side].at[: 2 * EQ * cells_s]
        start(state_ref.at[:, :, pl.ds(at, 2), :], rows.reshape(EQ, cells_s, 2, LANES))
    for pair in zip(ahead, fetched):
        start(*pair)
    for copy in copies[:6]:
        copy.wait()
    tiles_g = cells_g // TILE
    number = tile[...].astype(jnp.float32)
    tile_s = jnp.floor(number * (1.0 / tiles_g))
    tile_g = number - tile_s * tiles_g
    wide = width[...]
    amplitude = 1.0 / (wide * wide * wide * math.pi**1.5)
    pay_ref[...] = jnp.zeros_like(pay_ref)
    pay_ref[0:1, :held] = tile_s * TILE + offset[0:1]
    pay_ref[1:2, :held] = tile_g * TILE + offset[1:2]
    pay_ref[2:3, :held] = height[...]
    pay_ref[3:4, :held] = 1.0 / (wide * wide)
    pay_ref[4:7, :held] = force[...] * amplitude
    pay_ref[7:8, :held] = owner[...].astype(jnp.float32)
    ends = [(ref, EQ * slab) for ref in out_s] + [(ref, 2 * EQ * cells_s) for ref in out_g]
    for out_ref, rows in ends:
        if out_ref.shape[0] > rows:
            out_ref[rows:, :] = pay_ref[...]
    for copy in copies[6:]:
        copy.wait()


def coef_kernel(cells, *refs):
    cells_s, cells_g = cells
    columns = cells_s * cells_g
    dtau_ref, visc_ref, speed_ref, left_ref, right_ref, source_ref, advect_ref, state_ref = refs[:8]
    (
        r0_ref, adv_ref, lb_ref, rb_ref, fu_ref, gu_ref, fd_ref, gd_ref, dru_ref, rd_ref, gf_ref, pd_ref,
        crow_ref, spd_ref, turned, speeds,
    ) = refs[8:]
    crow_ref[LAST_STEP + 1 :] = jnp.zeros((MAP_ROWS - LAST_STEP - 1, LANES), jnp.float32)
    spd_ref[...] = jnp.zeros_like(spd_ref)
    for m in range(EQ):
        speeds[m] = jnp.broadcast_to(speed_ref[0:1, m : m + 1], (8, LANES))
        spd_ref[m : m + 1] = jnp.broadcast_to(speed_ref[0:1, m : m + 1], (1, LANES))
        for q in range(EQ):
            lb_ref[m * EQ + q] = jnp.broadcast_to(left_ref[m : m + 1, q : q + 1], (8, LANES))
            rb_ref[m * EQ + q] = jnp.broadcast_to(right_ref[m : m + 1, q : q + 1], (8, LANES))
    on = sub_iota((cells_g, cells_g)) == lax.broadcasted_iota(jnp.int32, (cells_g, cells_g), 1)
    for d in range(2):
        for s in range(cells_s):
            line = jnp.broadcast_to(advect_ref[d, s : s + 1, :], (cells_g, cells_g))
            line = jnp.sum(jnp.where(on, line, 0.0), axis=1, keepdims=True)
            adv_ref[d, s * cells_g : (s + 1) * cells_g, :] = jnp.broadcast_to(line, (cells_g, LANES))
    turned[0] = jnp.transpose(dtau_ref[...])
    turned[1] = jnp.transpose(visc_ref[...])
    crow_ref[FIRST_VISC : FIRST_VISC + 1] = turned[1, 0:1]
    crow_ref[LAST_VISC : LAST_VISC + 1] = turned[1, LANES - 1 : LANES]
    crow_ref[LAST_STEP : LAST_STEP + 1] = turned[0, LANES - 1 : LANES]

    def mode(m, carry):
        ahead = jnp.maximum(speeds[m], 0.0)
        back = jnp.maximum(-speeds[m], 0.0)
        step = [turned[0, pl.ds(j, 8, stride=STEPS), :] for j in range(STEPS)]
        visc = [turned[1, pl.ds(j, 8, stride=STEPS), :] for j in range(STEPS)]
        product, ups = None, []
        for j in range(STEPS):
            a = step[j] * (ahead + visc[j])
            ru = 1.0 / (1.0 + a)
            fu = a * ru
            product = fu if product is None else fu * product
            fu_ref[m, j], gu_ref[m, j], dru_ref[m, j] = fu, product, step[j] * ru
            ups.append(product)
        _, outer = up_entry(product, jnp.zeros_like(product))
        ups = [p * outer for p in ups]
        product, value, downs, values = None, None, [None] * STEPS, [None] * STEPS
        for j in reversed(range(STEPS)):
            b = step[j] * (back + visc[j])
            rd = 1.0 / (1.0 + b)
            fd = b * rd
            source = ups[j] * rd
            product = fd if product is None else fd * product
            value = source if value is None else fd * value + source
            fd_ref[m, j], gd_ref[m, j], rd_ref[m, j] = fd, product, rd
            downs[j], values[j] = product, value
        entry, outer = down_entry(product, value)
        for j in range(STEPS):
            gf_ref[m, j] = values[j] + downs[j] * entry
            pd_ref[m, j] = downs[j] * outer
        rows = (
            (PN, ups[-1][7:8]),
            (PD0, (downs[0] * outer)[0:1]),
            (G0, (values[0] + downs[0] * entry)[0:1]),
        )
        for kind, row in rows:
            crow_ref[pl.ds(kind * EQ + m, 1), :] = row
        return carry

    lax.fori_loop(0, EQ, mode, 0)
    girth = sub_iota((cells_g, LANES))
    lane = lax.broadcasted_iota(jnp.int32, (cells_g, LANES), 1)
    for s in range(cells_s):
        rows = slice(s * cells_g, (s + 1) * cells_g)
        speed_s, speed_g, visc = adv_ref[0, rows], adv_ref[1, rows], visc_ref[rows]
        state = [state_ref[q * columns + s * cells_g : q * columns + (s + 1) * cells_g] for q in range(EQ)]
        near_up, near_down = 0.125 - speed_s * (2.0 / 3.0), 0.125 + speed_s * (2.0 / 3.0)
        far_up, far_down = speed_s * (1.0 / 12.0) - 0.03125, -0.03125 - speed_s * (1.0 / 12.0)
        right1 = jnp.where(girth < cells_g - 1, 0.125 - speed_g * (2.0 / 3.0), 0.0)
        left1 = jnp.where(girth >= 1, 0.125 + speed_g * (2.0 / 3.0), 0.0)
        right2 = jnp.where(girth < cells_g - 2, speed_g * (1.0 / 12.0) - 0.03125, 0.0)
        left2 = jnp.where(girth >= 2, -0.03125 - speed_g * (1.0 / 12.0), 0.0)
        above = jnp.where(lane < LANES - 1, visc, 0.0)
        below = jnp.where(lane >= 1, visc, 0.0)
        centre = -0.375 - 2.0 * visc
        for q in range(EQ):
            here = state[q]
            total = centre * here
            for shift, weight in ((1, near_up), (-1, near_down), (2, far_up), (-2, far_down)):
                if 0 <= s + shift < cells_s:
                    at = q * columns + (s + shift) * cells_g
                    total = total + weight * state_ref[at : at + cells_g]
            total = total + right1 * pltpu.roll(here, cells_g - 1, 0) + left1 * pltpu.roll(here, 1, 0)
            total = total + right2 * pltpu.roll(here, cells_g - 2, 0) + left2 * pltpu.roll(here, 2, 0)
            total = total + above * pltpu.roll(here, LANES - 1, 1) + below * pltpu.roll(here, 1, 1)
            for f in range(EQ):
                total = total + jnp.broadcast_to(source_ref[q : q + 1, f : f + 1], (cells_g, LANES)) * state[f]
            r0_ref[q * columns + s * cells_g : q * columns + (s + 1) * cells_g] = total
    sub, lanes = sub_iota(), lax.broadcasted_iota(jnp.int32, (8, LANES), 1)
    ends = ((sub == 0) & (lanes == 0)) | ((sub == 1) & (lanes == LANES - 1))
    ends = jnp.where(ends, 1.0, 0.0)
    edge = [
        lax.dot_general(
            ends, state_ref[q * columns : (q + 1) * columns], NT, precision=HIGHEST,
            preferred_element_type=jnp.float32,
        )
        for q in range(EQ)
    ]
    for m in range(EQ):
        mixed = lb_ref[m * EQ] * edge[0]
        for q in range(1, EQ):
            mixed = mixed + lb_ref[m * EQ + q] * edge[q]
        crow_ref[LSF * EQ + m : LSF * EQ + m + 1] = mixed[0:1]
        crow_ref[LSL * EQ + m : LSL * EQ + m + 1] = mixed[1:2]


def pair_kernel(one_ref, two_ref, crow_ref, out_ref):
    out_ref[...] = one_ref[...] + pltpu.roll(two_ref[...], 8, 1)


def halo_kernel(cells, counts, sides, a_ref, b_ref, *refs):
    cells_s, cells_g = cells
    count_s, count_g = counts
    columns = cells_s * cells_g
    g_refs, (r0_ref, adv_ref, lb_ref), refs = refs[:sides], refs[sides : sides + 3], refs[sides + 3 :]
    turned, res_ref = refs[-2:]
    if len(refs) > 2:
        pay_ref, pair_ref, kept_ref = refs[0], refs[1], refs[-3]
        rows = slice(EQ * 2 * cells_g, EQ * 2 * cells_g + 8)
        kept = pay_ref[...] + pltpu.roll(pair_ref[...], 32, 1)
        kept = kept + pltpu.roll(a_ref[rows], 8, 1) + pltpu.roll(b_ref[rows], 16, 1)
        rows = slice(EQ * 2 * cells_s, EQ * 2 * cells_s + 8)
        kept_ref[...] = kept + pltpu.roll(g_refs[0][rows], 24, 1)
    at_s, at_g = lax.axis_index("stream"), lax.axis_index("girth")
    odd_s, odd_g = lax.rem(at_s, 2) == 1, lax.rem(at_g, 2) == 1
    low_s = jnp.where(at_s > 0, 1.0, 0.0)
    high_s = jnp.where(at_s < count_s - 1, 1.0, 0.0)
    low_g = jnp.where(at_g > 0, 1.0, 0.0)
    high_g = jnp.where(at_g < count_g - 1, 1.0, 0.0)
    speed = [adv_ref[0, s * cells_g : (s + 1) * cells_g] for s in range(cells_s)]
    sub = sub_iota()
    zero = jnp.zeros((8, LANES), jnp.float32)
    turn = []
    for s in range(cells_s):
        lead = adv_ref[1, s * cells_g : s * cells_g + 8]
        tail = adv_ref[1, (s + 1) * cells_g - 8 : (s + 1) * cells_g]
        near, far = low_g * (0.125 + lead * (2.0 / 3.0)), low_g * (-0.03125 - lead * (1.0 / 12.0))
        near_low = jnp.where(sub == 0, near, jnp.where(sub == 1, far, zero))
        far_low = jnp.where(sub == 0, far, zero)
        near, far = high_g * (0.125 - tail * (2.0 / 3.0)), high_g * (tail * (1.0 / 12.0) - 0.03125)
        near_high = jnp.where(sub == 7, near, jnp.where(sub == 6, far, zero))
        far_high = jnp.where(sub == 7, far, zero)
        turn.append((near_low, far_low, near_high, far_high))
    wide = cells_g
    for q in range(EQ):
        slab = slice(q * 2 * wide, (q + 1) * 2 * wide)
        slab_a, slab_b = a_ref[slab], b_ref[slab]
        low, high = jnp.where(odd_s, slab_a, slab_b), jnp.where(odd_s, slab_b, slab_a)
        for s in range(cells_s):
            rows = slice(q * columns + s * wide, q * columns + (s + 1) * wide)
            total = r0_ref[rows]
            if s == 0:
                total = total + low_s * (0.125 + speed[s] * (2.0 / 3.0)) * low[wide:]
                total = total + low_s * (-0.03125 - speed[s] * (1.0 / 12.0)) * low[:wide]
            if s == 1:
                total = total + low_s * (-0.03125 - speed[s] * (1.0 / 12.0)) * low[wide:]
            if s == cells_s - 2:
                total = total + high_s * (speed[s] * (1.0 / 12.0) - 0.03125) * high[:wide]
            if s == cells_s - 1:
                total = total + high_s * (0.125 - speed[s] * (2.0 / 3.0)) * high[:wide]
                total = total + high_s * (speed[s] * (1.0 / 12.0) - 0.03125) * high[wide:]
            near_low, far_low, near_high, far_high = turn[s]
            at = (2 * (q * cells_s + s), 2 * (q * cells_s + s) + 1)
            part = [jnp.broadcast_to(g_refs[0][i : i + 1], (8, LANES)) for i in at]
            part_low = part_high = part
            if sides > 1:
                other = [jnp.broadcast_to(g_refs[1][i : i + 1], (8, LANES)) for i in at]
                part_low = [jnp.where(odd_g, x, y) for x, y in zip(part, other)]
                part_high = [jnp.where(odd_g, y, x) for x, y in zip(part, other)]
            lead, tail = slice(rows.start, rows.start + 8), slice(rows.stop - 8, rows.stop)
            if wide > 16:
                res_ref[rows] = total
            res_ref[lead] = total[:8] + near_low * part_low[1] + far_low * part_low[0]
            res_ref[tail] = total[wide - 8 :] + near_high * part_high[0] + far_high * part_high[1]
    tiles = columns // 8
    for m in range(EQ):
        total = None
        for q in range(EQ):
            part = lb_ref[m * EQ + q][None] * res_ref[q * columns : (q + 1) * columns].reshape(tiles, 8, LANES)
            total = part if total is None else total + part
        turned[m] = jnp.transpose(total.reshape(columns, LANES))


def sweep_kernel(
    cells, count_g, shared, turned, lb_ref, fu_ref, gu_ref, fd_ref, gd_ref, dru_ref, rd_ref, crow_ref, *refs
):
    cells_s, cells_g = cells
    columns = cells_s * cells_g
    elems = refs[:-3]
    h_ref, map_ref, field_ref = refs[-3:]
    at_s, at_g, at_w = (lax.axis_index(name) for name in ("stream", "girth", "wall"))
    mine = (at_s * count_g + at_g).astype(jnp.float32)
    base_s = sub_iota((cells_s, LANES)).astype(jnp.float32) + 0.5
    base_g = sub_iota((cells_g, LANES)).astype(jnp.float32) + 0.5
    first = sub_iota() * STEPS + at_w * LANES
    base_w = jnp.concatenate([first + j for j in range(STEPS)], axis=0).astype(jnp.float32) + 0.5

    def spread(pay):
        sharp = -pay[3:4]
        prof_s = jnp.exp(sharp * (base_s - pay[0:1]) ** 2)
        prof_g = jnp.exp(sharp * (base_g - pay[1:2]) ** 2)
        prof_w = jnp.exp(sharp * (base_w - pay[2:3]) ** 2)
        push = jnp.where(pay[7:8] == mine, pay[4:7], 0.0)
        plane = jnp.concatenate([prof_g * prof_s[s : s + 1] for s in range(cells_s)], axis=0)
        weights = jnp.concatenate([plane * push[c : c + 1] for c in range(3)], axis=0)
        return lax.dot_general(prof_w, weights, NT, precision=HIGH, preferred_element_type=jnp.float32)

    if shared:
        field_ref[...] = spread(elems[0][...] + pltpu.roll(elems[1][...], 48, 1))
    else:
        field_ref[...] = jnp.zeros_like(field_ref)

        def chunk(i, carry):
            field_ref[...] += spread(elems[0][i])
            return carry

        lax.fori_loop(0, elems[0].shape[0], chunk, 0)
    map_ref[...] = crow_ref[...]
    for m in range(EQ):
        value, values = None, []
        for j in range(STEPS):
            source = turned[m, pl.ds(j, 8, stride=STEPS), :]
            for c in range(3):
                source = source + lb_ref[m * EQ + 1 + c] * field_ref[8 * j : 8 * j + 8, c * columns : (c + 1) * columns]
            source = source * dru_ref[m, j]
            value = source if value is None else fu_ref[m, j] * value + source
            values.append(value)
        entry, _ = up_entry(gu_ref[m, STEPS - 1], value)
        values = [v + gu_ref[m, j] * entry for j, v in enumerate(values)]
        map_ref[UP * EQ + m : UP * EQ + m + 1] = values[-1][7:8]
        value = None
        for j in reversed(range(STEPS)):
            source = values[j] * rd_ref[m, j]
            value = source if value is None else fd_ref[m, j] * value + source
            values[j] = value
        entry, _ = down_entry(gd_ref[m, 0], value)
        for j in range(STEPS):
            values[j] = values[j] + gd_ref[m, j] * entry
            h_ref[m, j] = values[j]
        map_ref[DOWN * EQ + m : DOWN * EQ + m + 1] = values[0][0:1]


def close_kernel(count, *refs):
    maps = refs[:count]
    h_ref, gf_ref, pd_ref, rb_ref, spd_ref, out_ref, all_ref, modal, turned, ready, sem = refs[count:]
    here = lax.axis_index("wall")
    for r, ref in enumerate(maps):
        all_ref[source(here, r, count)] = ref[...]

    def get(j, kind):
        return all_ref[j, kind * EQ : (kind + 1) * EQ]

    ahead = jnp.maximum(spd_ref[:EQ], 0.0)
    back = jnp.maximum(-spd_ref[:EQ], 0.0)
    first = [all_ref[j, FIRST_VISC : FIRST_VISC + 1] for j in range(count)]
    last = [all_ref[j, LAST_VISC : LAST_VISC + 1] for j in range(count)]
    step = [all_ref[j, LAST_STEP : LAST_STEP + 1] for j in range(count)]
    share = [1.0 / (1.0 + step[j] * (ahead + last[j])) for j in range(count)]
    zero = jnp.zeros((EQ, LANES), jnp.float32)
    entry, entries, mine_up = zero, [], zero
    for j in range(count):
        if j > 0:
            entry = entry + first[j] / (ahead + first[j]) * get(j - 1, LSL)
        entries.append(entry)
        mine_up = jnp.where(here == j, entry, mine_up)
        entry = get(j, PN) * entry + get(j, UP)
        if j < count - 1:
            entry = entry + share[j] * step[j] * last[j] * get(j + 1, LSF)
    above, mine_down = zero, zero
    for j in reversed(range(count)):
        if j < count - 1:
            above = above + share[j] * last[j] / (back + last[j]) * get(j + 1, LSF)
        mine_down = jnp.where(here == j, above, mine_down)
        above = get(j, PD0) * above + get(j, G0) * entries[j] + get(j, DOWN)
    for m in range(EQ):
        up = jnp.broadcast_to(mine_up[m : m + 1], (8, LANES))
        down = jnp.broadcast_to(mine_down[m : m + 1], (8, LANES))
        for j in range(STEPS):
            modal[m, j] = h_ref[m, j] + gf_ref[m, j] * up + pd_ref[m, j] * down
    copies = []
    for k in range(3):
        for q in (2 * k, 2 * k + 1):
            weight = [rb_ref[q * EQ + m] for m in range(EQ)]
            for j in range(STEPS):
                total = weight[0] * modal[0, j]
                for m in range(1, EQ):
                    total = total + weight[m] * modal[m, j]
                turned[q, pl.ds(j, 8, stride=STEPS), :] = total
            ready[q] = jnp.transpose(turned[q])
        part = slice(2 * k, 2 * k + 2)
        copy = pltpu.make_async_copy(ready.at[part], out_ref.at[part], sem.at[k])
        copy.start()
        copies.append(copy)
    for copy in copies:
        copy.wait()


def source(here, r, count):
    if count & (count - 1) == 0:
        return here ^ r
    return (here + count - r) % count


def blocks(count_s, count_g, count_w, moves):
    pairs = []
    for s in range(count_s):
        for g in range(count_g):
            for w in range(count_w):
                at_s, at_g = moves[w % 2]
                target = ((s ^ at_s) * count_g + (g ^ at_g)) * count_w + w
                pairs.append(((s * count_g + g) * count_w + w, target))
    return pairs


def swaps(count, side):
    if side == 0:
        return [(i, i ^ 1) for i in range(count)]
    return [(i, (i + (1 if i % 2 else -1)) % count) for i in range(count)]


def local(
    state,
    advect,
    dtau,
    viscosity,
    mode_speed,
    left_modes,
    right_modes,
    source_jac,
    elem_owner,
    elem_tile,
    elem_offset,
    elem_height,
    elem_force,
    elem_width,
):
    f32 = jnp.float32
    cells = (state.shape[1], state.shape[2])
    cells_s, cells_g = cells
    columns = cells_s * cells_g
    count_s, count_g, count_w = (lax.axis_size(name) for name in ("stream", "girth", "wall"))
    held = elem_owner.shape[0]
    shared = count_s == 4 and count_g == 2 and count_w % 2 == 0 and held <= 8
    sides = 1 if count_g == 2 else 2
    extra = 8 if shared else 0
    ahead = (
        dtau.reshape(columns, LANES),
        viscosity.reshape(columns, LANES),
        mode_speed.reshape(1, EQ),
        left_modes,
        right_modes,
        source_jac,
        advect,
    )
    outs = [(EQ * 2 * cells_g + extra, LANES)] * 2
    outs += [(EQ * 2 * cells_s + extra, LANES)] * sides + [(8, LANES)] + [part.shape for part in ahead]
    packed = call(
        functools.partial(pack_kernel, cells, held, sides),
        outs,
        state,
        elem_owner.T,
        elem_tile.reshape(1, held),
        elem_offset.T,
        elem_height.reshape(1, held),
        elem_force.T,
        elem_width.reshape(1, held),
        *ahead,
        scratch=[((1, held), jnp.int32), ((1, held), jnp.int32), ((2, held), f32), ((1, held), f32)]
        + [((3, held), f32), ((1, held), f32)],
        far=range(7 + AHEAD),
        copies=sides + 8 + AHEAD,
    )
    pay, ahead = packed[2 + sides], packed[3 + sides :]
    halo_a = lax.ppermute(packed[0], "stream", swaps(count_s, 0))
    halo_b = lax.ppermute(packed[1], "stream", swaps(count_s, 1))
    halo_g = [lax.ppermute(packed[2 + i], "girth", swaps(count_g, i)) for i in range(sides)]
    if shared:
        every = ("stream", "girth", "wall")
        far = [
            lax.ppermute(pay, every, blocks(count_s, count_g, count_w, moves))
            for moves in (((1, 1), (2, 1)), ((2, 0), (3, 1)))
        ]
    wide = (EQ, STEPS, 8, LANES)
    r0, adv, lb, rb, fu, gu, fd, gd, dru, rd, gf, pd, crow, spd = call(
        functools.partial(coef_kernel, cells),
        [(EQ * columns, LANES), (2, columns, LANES), (EQ * EQ, 8, LANES), (EQ * EQ, 8, LANES)]
        + [wide] * 8
        + [(MAP_ROWS, LANES), (8, LANES)],
        *ahead,
        state.reshape(EQ * columns, LANES),
        scratch=[((2, LANES, columns), f32), ((EQ, 8, LANES), f32)],
        cost=4 << 20,
    )
    if shared:
        (pair,) = call(pair_kernel, [(8, LANES)], *far, crow)
        other = lax.ppermute(pair, "wall", [(i, i ^ 1) for i in range(count_w)])
    *kept, turned = call(
        functools.partial(halo_kernel, cells, (count_s, count_g), sides),
        [(8, LANES)] * shared + [(EQ, LANES, columns)],
        halo_a, halo_b, *halo_g, r0, adv, lb, *((pay, pair) if shared else ()),
        scratch=[((EQ * columns, LANES), f32)],
        cost=1 << 20,
    )
    elems = (*kept, other) if shared else (lax.all_gather(pay, ("stream", "girth")),)
    h, block_map = call(
        functools.partial(sweep_kernel, cells, count_g, shared),
        [wide, (MAP_ROWS, LANES)],
        turned, lb, fu, gu, fd, gd, dru, rd, crow, *elems,
        scratch=[((LANES, 3 * columns), f32)],
        cost=1 << 20,
    )
    maps = [block_map]
    for r in range(1, count_w):
        pairs = [(int(source(i, r, count_w)), i) for i in range(count_w)]
        maps.append(lax.ppermute(block_map, "wall", pairs))
    (out,) = call(
        functools.partial(close_kernel, count_w),
        [(EQ, columns, LANES)],
        *maps, h, gf, pd, rb, spd,
        scratch=[((count_w, MAP_ROWS, LANES), f32), (wide, f32), ((EQ, LANES, columns), f32)]
        + [((EQ, columns, LANES), f32)],
        cost=1 << 20,
        far_out=(0,),
        copies=3,
    )
    return out.reshape(state.shape)


def solution(mesh):
    in_specs = (
        P(None, "stream", "girth", "wall"),
        P(None, "stream", "girth"),
        P("stream", "girth", "wall"),
        P("stream", "girth", "wall"),
        P(),
        P(),
        P(),
        P(),
        P(("stream", "girth"), None),
        P(("stream", "girth")),
        P(("stream", "girth"), None),
        P(("stream", "girth")),
        P(("stream", "girth"), None),
        P(("stream", "girth")),
    )
    out_specs = P(None, "stream", "girth", "wall")
    return jax.shard_map(local, mesh=mesh, in_specs=in_specs, out_specs=out_specs, check_vma=False)
```

```python
import functools
import math

import jax
import jax.numpy as jnp
from jax import lax
from jax.experimental import pallas as pl
from jax.experimental.pallas import tpu as pltpu
from jax.sharding import PartitionSpec as P

TILE = 8
EQ = 6
LANES = 128
STEPS = 16
HIGHEST = lax.Precision.HIGHEST
HIGH = lax.Precision.HIGH
NT = (((1,), (1,)), ((), ()))
PN, PD0, G0, LSF, LSL, UP, DOWN = range(7)
FIRST_VISC, LAST_VISC, LAST_STEP = 42, 43, 44
MAP_ROWS = 48
AHEAD = 7


def call(kernel, outs, *args, scratch=(), cost=0, far=(), far_out=(), copies=0):
    shapes = [jax.ShapeDtypeStruct(shape, jnp.float32) for shape in outs]

    def spec(is_far):
        return pl.BlockSpec(memory_space=pltpu.HBM if is_far else pltpu.VMEM)

    args = [pltpu.with_memory_space_constraint(part, pltpu.HBM) if i in far else part for i, part in enumerate(args)]
    return pl.pallas_call(
        kernel,
        out_shape=shapes,
        in_specs=[spec(i in far) for i in range(len(args))],
        out_specs=[spec(i in far_out) for i in range(len(outs))],
        scratch_shapes=[pltpu.VMEM(shape, kind) for shape, kind in scratch]
        + ([pltpu.SemaphoreType.DMA((copies,))] if copies else []),
        compiler_params=pltpu.CompilerParams(vmem_limit_bytes=16 << 20),
        cost_estimate=pl.CostEstimate(flops=cost, bytes_accessed=cost, transcendentals=0),
    )(*args)


def sub_iota(shape=(8, LANES)):
    return lax.broadcasted_iota(jnp.int32, shape, 0)


def up_entry(factor, offset):
    row = sub_iota()
    for reach in (1, 2, 4):
        inside = row >= reach
        offset = jnp.where(inside, factor * pltpu.roll(offset, reach, 0) + offset, offset)
        factor = jnp.where(inside, factor * pltpu.roll(factor, reach, 0), factor)
    return jnp.where(row >= 1, pltpu.roll(offset, 1, 0), 0.0), jnp.where(row >= 1, pltpu.roll(factor, 1, 0), 1.0)


def down_entry(factor, offset):
    row = sub_iota()
    for reach in (1, 2, 4):
        inside = row < 8 - reach
        offset = jnp.where(inside, factor * pltpu.roll(offset, 8 - reach, 0) + offset, offset)
        factor = jnp.where(inside, factor * pltpu.roll(factor, 8 - reach, 0), factor)
    return jnp.where(row < 7, pltpu.roll(offset, 7, 0), 0.0), jnp.where(row < 7, pltpu.roll(factor, 7, 0), 1.0)


def pack_kernel(
    cells, held, sides, state_ref, owner_ref, tile_ref, offset_ref, height_ref, force_ref, width_ref,
    *refs,
):
    cells_s, cells_g = cells
    ahead, refs = refs[:AHEAD], refs[AHEAD:]
    out_s, out_g, refs = refs[:2], refs[2 : 2 + sides], refs[2 + sides :]
    pay_ref, fetched, refs = refs[0], refs[1 : 1 + AHEAD], refs[1 + AHEAD :]
    owner, tile, offset, height, force, width, sem = refs
    odd_s = lax.rem(lax.axis_index("stream"), 2)
    odd_g = lax.rem(lax.axis_index("girth"), 2)
    copies = []

    def start(source, target):
        copy = pltpu.make_async_copy(source, target, sem.at[len(copies)])
        copy.start()
        copies.append(copy)

    for pair in zip(
        (owner_ref, tile_ref, offset_ref, height_ref, force_ref, width_ref),
        (owner, tile, offset, height, force, width),
    ):
        start(*pair)
    slab = 2 * cells_g
    for side, out_ref in enumerate(out_s):
        low = odd_s if side == 0 else 1 - odd_s
        at = (cells_s - 2) * (1 - low)
        start(state_ref.at[:, pl.ds(at, 2)], out_ref.at[: EQ * slab].reshape(EQ, 2, cells_g, LANES))
    for side in range(sides):
        low = odd_g if side == 0 else 1 - odd_g
        at = (cells_g - 2) * (1 - low)
        rows = out_g[side].at[: 2 * EQ * cells_s]
        start(state_ref.at[:, :, pl.ds(at, 2), :], rows.reshape(EQ, cells_s, 2, LANES))
    for pair in zip(ahead, fetched):
        start(*pair)
    for copy in copies[:6]:
        copy.wait()
    tiles_g = cells_g // TILE
    number = tile[...].astype(jnp.float32)
    tile_s = jnp.floor(number * (1.0 / tiles_g))
    tile_g = number - tile_s * tiles_g
    wide = width[...]
    amplitude = 1.0 / (wide * wide * wide * math.pi**1.5)
    pay_ref[...] = jnp.zeros_like(pay_ref)
    pay_ref[0:1, :held] = tile_s * TILE + offset[0:1]
    pay_ref[1:2, :held] = tile_g * TILE + offset[1:2]
    pay_ref[2:3, :held] = height[...]
    pay_ref[3:4, :held] = 1.0 / (wide * wide)
    pay_ref[4:7, :held] = force[...] * amplitude
    pay_ref[7:8, :held] = owner[...].astype(jnp.float32)
    ends = [(ref, EQ * slab) for ref in out_s] + [(ref, 2 * EQ * cells_s) for ref in out_g]
    for out_ref, rows in ends:
        if out_ref.shape[0] > rows:
            out_ref[rows:, :] = pay_ref[...]
    for copy in copies[6:]:
        copy.wait()


def coef_kernel(cells, *refs):
    cells_s, cells_g = cells
    columns = cells_s * cells_g
    dtau_ref, visc_ref, speed_ref, left_ref, right_ref, source_ref, advect_ref, state_ref = refs[:8]
    (
        r0_ref, adv_ref, lb_ref, rb_ref, fu_ref, gu_ref, fd_ref, gd_ref, dru_ref, rd_ref, gf_ref, pd_ref,
        crow_ref, spd_ref, turned, speeds,
    ) = refs[8:]
    crow_ref[LAST_STEP + 1 :] = jnp.zeros((MAP_ROWS - LAST_STEP - 1, LANES), jnp.float32)
    spd_ref[...] = jnp.zeros_like(spd_ref)
    for m in range(EQ):
        speeds[m] = jnp.broadcast_to(speed_ref[0:1, m : m + 1], (8, LANES))
        spd_ref[m : m + 1] = jnp.broadcast_to(speed_ref[0:1, m : m + 1], (1, LANES))
        for q in range(EQ):
            lb_ref[m * EQ + q] = jnp.broadcast_to(left_ref[m : m + 1, q : q + 1], (8, LANES))
            rb_ref[m * EQ + q] = jnp.broadcast_to(right_ref[m : m + 1, q : q + 1], (8, LANES))
    on = sub_iota((cells_g, cells_g)) == lax.broadcasted_iota(jnp.int32, (cells_g, cells_g), 1)
    for d in range(2):
        for s in range(cells_s):
            line = jnp.broadcast_to(advect_ref[d, s : s + 1, :], (cells_g, cells_g))
            line = jnp.sum(jnp.where(on, line, 0.0), axis=1, keepdims=True)
            adv_ref[d, s * cells_g : (s + 1) * cells_g, :] = jnp.broadcast_to(line, (cells_g, LANES))
    turned[0] = jnp.transpose(dtau_ref[...])
    turned[1] = jnp.transpose(visc_ref[...])
    crow_ref[FIRST_VISC : FIRST_VISC + 1] = turned[1, 0:1]
    crow_ref[LAST_VISC : LAST_VISC + 1] = turned[1, LANES - 1 : LANES]
    crow_ref[LAST_STEP : LAST_STEP + 1] = turned[0, LANES - 1 : LANES]

    def mode(m, carry):
        ahead = jnp.maximum(speeds[m], 0.0)
        back = jnp.maximum(-speeds[m], 0.0)
        step = [turned[0, pl.ds(j, 8, stride=STEPS), :] for j in range(STEPS)]
        visc = [turned[1, pl.ds(j, 8, stride=STEPS), :] for j in range(STEPS)]
        product, ups = None, []
        for j in range(STEPS):
            a = step[j] * (ahead + visc[j])
            ru = 1.0 / (1.0 + a)
            fu = a * ru
            product = fu if product is None else fu * product
            fu_ref[m, j], gu_ref[m, j], dru_ref[m, j] = fu, product, step[j] * ru
            ups.append(product)
        _, outer = up_entry(product, jnp.zeros_like(product))
        ups = [p * outer for p in ups]
        product, value, downs, values = None, None, [None] * STEPS, [None] * STEPS
        for j in reversed(range(STEPS)):
            b = step[j] * (back + visc[j])
            rd = 1.0 / (1.0 + b)
            fd = b * rd
            source = ups[j] * rd
            product = fd if product is None else fd * product
            value = source if value is None else fd * value + source
            fd_ref[m, j], gd_ref[m, j], rd_ref[m, j] = fd, product, rd
            downs[j], values[j] = product, value
        entry, outer = down_entry(product, value)
        for j in range(STEPS):
            gf_ref[m, j] = values[j] + downs[j] * entry
            pd_ref[m, j] = downs[j] * outer
        rows = (
            (PN, ups[-1][7:8]),
            (PD0, (downs[0] * outer)[0:1]),
            (G0, (values[0] + downs[0] * entry)[0:1]),
        )
        for kind, row in rows:
            crow_ref[pl.ds(kind * EQ + m, 1), :] = row
        return carry

    lax.fori_loop(0, EQ, mode, 0)
    girth = sub_iota((cells_g, LANES))
    lane = lax.broadcasted_iota(jnp.int32, (cells_g, LANES), 1)
    for s in range(cells_s):
        rows = slice(s * cells_g, (s + 1) * cells_g)
        speed_s, speed_g, visc = adv_ref[0, rows], adv_ref[1, rows], visc_ref[rows]
        state = [state_ref[q * columns + s * cells_g : q * columns + (s + 1) * cells_g] for q in range(EQ)]
        near_up, near_down = 0.125 - speed_s * (2.0 / 3.0), 0.125 + speed_s * (2.0 / 3.0)
        far_up, far_down = speed_s * (1.0 / 12.0) - 0.03125, -0.03125 - speed_s * (1.0 / 12.0)
        right1 = jnp.where(girth < cells_g - 1, 0.125 - speed_g * (2.0 / 3.0), 0.0)
        left1 = jnp.where(girth >= 1, 0.125 + speed_g * (2.0 / 3.0), 0.0)
        right2 = jnp.where(girth < cells_g - 2, speed_g * (1.0 / 12.0) - 0.03125, 0.0)
        left2 = jnp.where(girth >= 2, -0.03125 - speed_g * (1.0 / 12.0), 0.0)
        above = jnp.where(lane < LANES - 1, visc, 0.0)
        below = jnp.where(lane >= 1, visc, 0.0)
        centre = -0.375 - 2.0 * visc
        for q in range(EQ):
            here = state[q]
            total = centre * here
            for shift, weight in ((1, near_up), (-1, near_down), (2, far_up), (-2, far_down)):
                if 0 <= s + shift < cells_s:
                    at = q * columns + (s + shift) * cells_g
                    total = total + weight * state_ref[at : at + cells_g]
            total = total + right1 * pltpu.roll(here, cells_g - 1, 0) + left1 * pltpu.roll(here, 1, 0)
            total = total + right2 * pltpu.roll(here, cells_g - 2, 0) + left2 * pltpu.roll(here, 2, 0)
            total = total + above * pltpu.roll(here, LANES - 1, 1) + below * pltpu.roll(here, 1, 1)
            for f in range(EQ):
                total = total + jnp.broadcast_to(source_ref[q : q + 1, f : f + 1], (cells_g, LANES)) * state[f]
            r0_ref[q * columns + s * cells_g : q * columns + (s + 1) * cells_g] = total
    sub, lanes = sub_iota(), lax.broadcasted_iota(jnp.int32, (8, LANES), 1)
    ends = ((sub == 0) & (lanes == 0)) | ((sub == 1) & (lanes == LANES - 1))
    ends = jnp.where(ends, 1.0, 0.0)
    edge = [
        lax.dot_general(
            ends, state_ref[q * columns : (q + 1) * columns], NT, precision=HIGHEST,
            preferred_element_type=jnp.float32,
        )
        for q in range(EQ)
    ]
    for m in range(EQ):
        mixed = lb_ref[m * EQ] * edge[0]
        for q in range(1, EQ):
            mixed = mixed + lb_ref[m * EQ + q] * edge[q]
        crow_ref[LSF * EQ + m : LSF * EQ + m + 1] = mixed[0:1]
        crow_ref[LSL * EQ + m : LSL * EQ + m + 1] = mixed[1:2]


def pair_kernel(one_ref, two_ref, crow_ref, out_ref):
    out_ref[...] = one_ref[...] + pltpu.roll(two_ref[...], 8, 1)


def halo_kernel(cells, counts, sides, a_ref, b_ref, *refs):
    cells_s, cells_g = cells
    count_s, count_g = counts
    columns = cells_s * cells_g
    g_refs, (r0_ref, adv_ref, lb_ref), refs = refs[:sides], refs[sides : sides + 3], refs[sides + 3 :]
    turned, res_ref = refs[-2:]
    if len(refs) > 2:
        pay_ref, pair_ref, kept_ref = refs[0], refs[1], refs[-3]
        rows = slice(EQ * 2 * cells_g, EQ * 2 * cells_g + 8)
        kept = pay_ref[...] + pltpu.roll(pair_ref[...], 32, 1)
        kept = kept + pltpu.roll(a_ref[rows], 8, 1) + pltpu.roll(b_ref[rows], 16, 1)
        rows = slice(EQ * 2 * cells_s, EQ * 2 * cells_s + 8)
        kept_ref[...] = kept + pltpu.roll(g_refs[0][rows], 24, 1)
    at_s, at_g = lax.axis_index("stream"), lax.axis_index("girth")
    odd_s, odd_g = lax.rem(at_s, 2) == 1, lax.rem(at_g, 2) == 1
    low_s = jnp.where(at_s > 0, 1.0, 0.0)
    high_s = jnp.where(at_s < count_s - 1, 1.0, 0.0)
    low_g = jnp.where(at_g > 0, 1.0, 0.0)
    high_g = jnp.where(at_g < count_g - 1, 1.0, 0.0)
    speed = [adv_ref[0, s * cells_g : (s + 1) * cells_g] for s in range(cells_s)]
    sub = sub_iota()
    zero = jnp.zeros((8, LANES), jnp.float32)
    turn = []
    for s in range(cells_s):
        lead = adv_ref[1, s * cells_g : s * cells_g + 8]
        tail = adv_ref[1, (s + 1) * cells_g - 8 : (s + 1) * cells_g]
        near, far = low_g * (0.125 + lead * (2.0 / 3.0)), low_g * (-0.03125 - lead * (1.0 / 12.0))
        near_low = jnp.where(sub == 0, near, jnp.where(sub == 1, far, zero))
        far_low = jnp.where(sub == 0, far, zero)
        near, far = high_g * (0.125 - tail * (2.0 / 3.0)), high_g * (tail * (1.0 / 12.0) - 0.03125)
        near_high = jnp.where(sub == 7, near, jnp.where(sub == 6, far, zero))
        far_high = jnp.where(sub == 7, far, zero)
        turn.append((near_low, far_low, near_high, far_high))
    wide = cells_g
    for q in range(EQ):
        slab = slice(q * 2 * wide, (q + 1) * 2 * wide)
        slab_a, slab_b = a_ref[slab], b_ref[slab]
        low, high = jnp.where(odd_s, slab_a, slab_b), jnp.where(odd_s, slab_b, slab_a)
        for s in range(cells_s):
            rows = slice(q * columns + s * wide, q * columns + (s + 1) * wide)
            total = r0_ref[rows]
            if s == 0:
                total = total + low_s * (0.125 + speed[s] * (2.0 / 3.0)) * low[wide:]
                total = total + low_s * (-0.03125 - speed[s] * (1.0 / 12.0)) * low[:wide]
            if s == 1:
                total = total + low_s * (-0.03125 - speed[s] * (1.0 / 12.0)) * low[wide:]
            if s == cells_s - 2:
                total = total + high_s * (speed[s] * (1.0 / 12.0) - 0.03125) * high[:wide]
            if s == cells_s - 1:
                total = total + high_s * (0.125 - speed[s] * (2.0 / 3.0)) * high[:wide]
                total = total + high_s * (speed[s] * (1.0 / 12.0) - 0.03125) * high[wide:]
            near_low, far_low, near_high, far_high = turn[s]
            at = (2 * (q * cells_s + s), 2 * (q * cells_s + s) + 1)
            part = [jnp.broadcast_to(g_refs[0][i : i + 1], (8, LANES)) for i in at]
            part_low = part_high = part
            if sides > 1:
                other = [jnp.broadcast_to(g_refs[1][i : i + 1], (8, LANES)) for i in at]
                part_low = [jnp.where(odd_g, x, y) for x, y in zip(part, other)]
                part_high = [jnp.where(odd_g, y, x) for x, y in zip(part, other)]
            lead, tail = slice(rows.start, rows.start + 8), slice(rows.stop - 8, rows.stop)
            if wide > 16:
                res_ref[rows] = total
            res_ref[lead] = total[:8] + near_low * part_low[1] + far_low * part_low[0]
            res_ref[tail] = total[wide - 8 :] + near_high * part_high[0] + far_high * part_high[1]
    tiles = columns // 8
    for m in range(EQ):
        total = None
        for q in range(EQ):
            part = lb_ref[m * EQ + q][None] * res_ref[q * columns : (q + 1) * columns].reshape(tiles, 8, LANES)
            total = part if total is None else total + part
        turned[m] = jnp.transpose(total.reshape(columns, LANES))


def sweep_kernel(
    cells, count_g, shared, turned, lb_ref, fu_ref, gu_ref, fd_ref, gd_ref, dru_ref, rd_ref, crow_ref, *refs
):
    cells_s, cells_g = cells
    columns = cells_s * cells_g
    elems = refs[:-3]
    h_ref, map_ref, field_ref = refs[-3:]
    at_s, at_g, at_w = (lax.axis_index(name) for name in ("stream", "girth", "wall"))
    mine = (at_s * count_g + at_g).astype(jnp.float32)
    base_s = sub_iota((cells_s, LANES)).astype(jnp.float32) + 0.5
    base_g = sub_iota((cells_g, LANES)).astype(jnp.float32) + 0.5
    first = sub_iota() * STEPS + at_w * LANES
    base_w = jnp.concatenate([first + j for j in range(STEPS)], axis=0).astype(jnp.float32) + 0.5

    def spread(pay):
        sharp = -pay[3:4]
        prof_s = jnp.exp(sharp * (base_s - pay[0:1]) ** 2)
        prof_g = jnp.exp(sharp * (base_g - pay[1:2]) ** 2)
        prof_w = jnp.exp(sharp * (base_w - pay[2:3]) ** 2)
        push = jnp.where(pay[7:8] == mine, pay[4:7], 0.0)
        plane = jnp.concatenate([prof_g * prof_s[s : s + 1] for s in range(cells_s)], axis=0)
        weights = jnp.concatenate([plane * push[c : c + 1] for c in range(3)], axis=0)
        return lax.dot_general(prof_w, weights, NT, precision=HIGH, preferred_element_type=jnp.float32)

    if shared:
        field_ref[...] = spread(elems[0][...] + pltpu.roll(elems[1][...], 48, 1))
    else:
        field_ref[...] = jnp.zeros_like(field_ref)

        def chunk(i, carry):
            field_ref[...] += spread(elems[0][i])
            return carry

        lax.fori_loop(0, elems[0].shape[0], chunk, 0)
    map_ref[...] = crow_ref[...]
    for m in range(EQ):
        value, values = None, []
        for j in range(STEPS):
            source = turned[m, pl.ds(j, 8, stride=STEPS), :]
            for c in range(3):
                source = source + lb_ref[m * EQ + 1 + c] * field_ref[8 * j : 8 * j + 8, c * columns : (c + 1) * columns]
            source = source * dru_ref[m, j]
            value = source if value is None else fu_ref[m, j] * value + source
            values.append(value)
        entry, _ = up_entry(gu_ref[m, STEPS - 1], value)
        values = [v + gu_ref[m, j] * entry for j, v in enumerate(values)]
        map_ref[UP * EQ + m : UP * EQ + m + 1] = values[-1][7:8]
        value = None
        for j in reversed(range(STEPS)):
            source = values[j] * rd_ref[m, j]
            value = source if value is None else fd_ref[m, j] * value + source
            values[j] = value
        entry, _ = down_entry(gd_ref[m, 0], value)
        for j in range(STEPS):
            values[j] = values[j] + gd_ref[m, j] * entry
            h_ref[m, j] = values[j]
        map_ref[DOWN * EQ + m : DOWN * EQ + m + 1] = values[0][0:1]


def close_kernel(count, *refs):
    maps = refs[:count]
    h_ref, gf_ref, pd_ref, rb_ref, spd_ref, out_ref, all_ref, modal, turned, ready, sem = refs[count:]
    here = lax.axis_index("wall")
    for r, ref in zip((0, 3, 1, 2), maps):
        all_ref[source(here, r, count)] = ref[...]

    def get(j, kind):
        return all_ref[j, kind * EQ : (kind + 1) * EQ]

    ahead = jnp.maximum(spd_ref[:EQ], 0.0)
    back = jnp.maximum(-spd_ref[:EQ], 0.0)
    first = [all_ref[j, FIRST_VISC : FIRST_VISC + 1] for j in range(count)]
    last = [all_ref[j, LAST_VISC : LAST_VISC + 1] for j in range(count)]
    step = [all_ref[j, LAST_STEP : LAST_STEP + 1] for j in range(count)]
    share = [1.0 / (1.0 + step[j] * (ahead + last[j])) for j in range(count)]
    zero = jnp.zeros((EQ, LANES), jnp.float32)
    entry, entries, mine_up = zero, [], zero
    for j in range(count):
        if j > 0:
            entry = entry + first[j] / (ahead + first[j]) * get(j - 1, LSL)
        entries.append(entry)
        mine_up = jnp.where(here == j, entry, mine_up)
        entry = get(j, PN) * entry + get(j, UP)
        if j < count - 1:
            entry = entry + share[j] * step[j] * last[j] * get(j + 1, LSF)
    above, mine_down = zero, zero
    for j in reversed(range(count)):
        if j < count - 1:
            above = above + share[j] * last[j] / (back + last[j]) * get(j + 1, LSF)
        mine_down = jnp.where(here == j, above, mine_down)
        above = get(j, PD0) * above + get(j, G0) * entries[j] + get(j, DOWN)
    for m in range(EQ):
        up = jnp.broadcast_to(mine_up[m : m + 1], (8, LANES))
        down = jnp.broadcast_to(mine_down[m : m + 1], (8, LANES))
        for j in range(STEPS):
            modal[m, j] = h_ref[m, j] + gf_ref[m, j] * up + pd_ref[m, j] * down
    copies = []
    for k in range(3):
        for q in (2 * k, 2 * k + 1):
            weight = [rb_ref[q * EQ + m] for m in range(EQ)]
            for j in range(STEPS):
                total = weight[0] * modal[0, j]
                for m in range(1, EQ):
                    total = total + weight[m] * modal[m, j]
                turned[q, pl.ds(j, 8, stride=STEPS), :] = total
            ready[q] = jnp.transpose(turned[q])
        part = slice(2 * k, 2 * k + 2)
        copy = pltpu.make_async_copy(ready.at[part], out_ref.at[part], sem.at[k])
        copy.start()
        copies.append(copy)
    for copy in copies:
        copy.wait()


def source(here, r, count):
    if count & (count - 1) == 0:
        return here ^ r
    return (here + count - r) % count


def blocks(count_s, count_g, count_w, moves):
    pairs = []
    for s in range(count_s):
        for g in range(count_g):
            for w in range(count_w):
                at_s, at_g = moves[w % 2]
                target = ((s ^ at_s) * count_g + (g ^ at_g)) * count_w + w
                pairs.append(((s * count_g + g) * count_w + w, target))
    return pairs


def swaps(count, side):
    if side == 0:
        return [(i, i ^ 1) for i in range(count)]
    return [(i, (i + (1 if i % 2 else -1)) % count) for i in range(count)]


def local(
    state,
    advect,
    dtau,
    viscosity,
    mode_speed,
    left_modes,
    right_modes,
    source_jac,
    elem_owner,
    elem_tile,
    elem_offset,
    elem_height,
    elem_force,
    elem_width,
):
    f32 = jnp.float32
    cells = (state.shape[1], state.shape[2])
    cells_s, cells_g = cells
    columns = cells_s * cells_g
    count_s, count_g, count_w = (lax.axis_size(name) for name in ("stream", "girth", "wall"))
    held = elem_owner.shape[0]
    shared = count_s == 4 and count_g == 2 and count_w % 2 == 0 and held <= 8
    sides = 1 if count_g == 2 else 2
    extra = 8 if shared else 0
    ahead = (
        dtau.reshape(columns, LANES),
        viscosity.reshape(columns, LANES),
        mode_speed.reshape(1, EQ),
        left_modes,
        right_modes,
        source_jac,
        advect,
    )
    outs = [(EQ * 2 * cells_g + extra, LANES)] * 2
    outs += [(EQ * 2 * cells_s + extra, LANES)] * sides + [(8, LANES)] + [part.shape for part in ahead]
    packed = call(
        functools.partial(pack_kernel, cells, held, sides),
        outs,
        state,
        elem_owner.T,
        elem_tile.reshape(1, held),
        elem_offset.T,
        elem_height.reshape(1, held),
        elem_force.T,
        elem_width.reshape(1, held),
        *ahead,
        scratch=[((1, held), jnp.int32), ((1, held), jnp.int32), ((2, held), f32), ((1, held), f32)]
        + [((3, held), f32), ((1, held), f32)],
        far=range(7 + AHEAD),
        copies=sides + 8 + AHEAD,
    )
    pay, ahead = packed[2 + sides], packed[3 + sides :]
    halo_a = lax.ppermute(packed[0], "stream", swaps(count_s, 0))
    halo_b = lax.ppermute(packed[1], "stream", swaps(count_s, 1))
    halo_g = [lax.ppermute(packed[2 + i], "girth", swaps(count_g, i)) for i in range(sides)]
    if shared:
        every = ("stream", "girth", "wall")
        far = [
            lax.ppermute(pay, every, blocks(count_s, count_g, count_w, moves))
            for moves in (((1, 1), (2, 1)), ((2, 0), (3, 1)))
        ]
    wide = (EQ, STEPS, 8, LANES)
    r0, adv, lb, rb, fu, gu, fd, gd, dru, rd, gf, pd, crow, spd = call(
        functools.partial(coef_kernel, cells),
        [(EQ * columns, LANES), (2, columns, LANES), (EQ * EQ, 8, LANES), (EQ * EQ, 8, LANES)]
        + [wide] * 8
        + [(MAP_ROWS, LANES), (8, LANES)],
        *ahead,
        state.reshape(EQ * columns, LANES),
        scratch=[((2, LANES, columns), f32), ((EQ, 8, LANES), f32)],
        cost=4 << 20,
    )
    if shared:
        (pair,) = call(pair_kernel, [(8, LANES)], *far, crow)
        other = lax.ppermute(pair, "wall", [(i, i ^ 1) for i in range(count_w)])
    *kept, turned = call(
        functools.partial(halo_kernel, cells, (count_s, count_g), sides),
        [(8, LANES)] * shared + [(EQ, LANES, columns)],
        halo_a, halo_b, *halo_g, r0, adv, lb, *((pay, pair) if shared else ()),
        scratch=[((EQ * columns, LANES), f32)],
        cost=1 << 20,
    )
    elems = (*kept, other) if shared else (lax.all_gather(pay, ("stream", "girth")),)
    h, block_map = call(
        functools.partial(sweep_kernel, cells, count_g, shared),
        [wide, (MAP_ROWS, LANES)],
        turned, lb, fu, gu, fd, gd, dru, rd, crow, *elems,
        scratch=[((LANES, 3 * columns), f32)],
        cost=1 << 20,
    )
    maps = [block_map]
    for r in range(1, count_w):
        pairs = [(int(source(i, r, count_w)), i) for i in range(count_w)]
        maps.append(lax.ppermute(block_map, "wall", pairs))
    (out,) = call(
        functools.partial(close_kernel, count_w),
        [(EQ, columns, LANES)],
        *[maps[r] for r in (0, 3, 1, 2)], h, gf, pd, rb, spd,
        scratch=[((count_w, MAP_ROWS, LANES), f32), (wide, f32), ((EQ, LANES, columns), f32)]
        + [((EQ, columns, LANES), f32)],
        cost=1 << 20,
        far_out=(0,),
        copies=3,
    )
    return out.reshape(state.shape)


def solution(mesh):
    in_specs = (
        P(None, "stream", "girth", "wall"),
        P(None, "stream", "girth"),
        P("stream", "girth", "wall"),
        P("stream", "girth", "wall"),
        P(),
        P(),
        P(),
        P(),
        P(("stream", "girth"), None),
        P(("stream", "girth")),
        P(("stream", "girth"), None),
        P(("stream", "girth")),
        P(("stream", "girth"), None),
        P(("stream", "girth")),
    )
    out_specs = P(None, "stream", "girth", "wall")
    return jax.shard_map(local, mesh=mesh, in_specs=in_specs, out_specs=out_specs, check_vma=False)
```

```python
import functools
import math

import jax
import jax.numpy as jnp
from jax import lax
from jax.experimental import pallas as pl
from jax.experimental.pallas import tpu as pltpu
from jax.sharding import PartitionSpec as P

TILE = 8
EQ = 6
LANES = 128
STEPS = 16
HIGHEST = lax.Precision.HIGHEST
HIGH = lax.Precision.HIGH
NT = (((1,), (1,)), ((), ()))
PN, PD0, G0, LSF, LSL, UP, DOWN = range(7)
FIRST_VISC, LAST_VISC, LAST_STEP = 42, 43, 44
MAP_ROWS = 48
AHEAD = 7


def call(kernel, outs, *args, scratch=(), cost=0, far=(), far_out=(), copies=0):
    shapes = [jax.ShapeDtypeStruct(shape, jnp.float32) for shape in outs]

    def spec(is_far):
        return pl.BlockSpec(memory_space=pltpu.HBM if is_far else pltpu.VMEM)

    args = [pltpu.with_memory_space_constraint(part, pltpu.HBM) if i in far else part for i, part in enumerate(args)]
    return pl.pallas_call(
        kernel,
        out_shape=shapes,
        in_specs=[spec(i in far) for i in range(len(args))],
        out_specs=[spec(i in far_out) for i in range(len(outs))],
        scratch_shapes=[pltpu.VMEM(shape, kind) for shape, kind in scratch]
        + ([pltpu.SemaphoreType.DMA((copies,))] if copies else []),
        compiler_params=pltpu.CompilerParams(vmem_limit_bytes=16 << 20),
        cost_estimate=pl.CostEstimate(flops=cost, bytes_accessed=cost, transcendentals=0),
    )(*args)


def sub_iota(shape=(8, LANES)):
    return lax.broadcasted_iota(jnp.int32, shape, 0)


def up_entry(factor, offset):
    row = sub_iota()
    for reach in (1, 2, 4):
        inside = row >= reach
        offset = jnp.where(inside, factor * pltpu.roll(offset, reach, 0) + offset, offset)
        factor = jnp.where(inside, factor * pltpu.roll(factor, reach, 0), factor)
    return jnp.where(row >= 1, pltpu.roll(offset, 1, 0), 0.0), jnp.where(row >= 1, pltpu.roll(factor, 1, 0), 1.0)


def down_entry(factor, offset):
    row = sub_iota()
    for reach in (1, 2, 4):
        inside = row < 8 - reach
        offset = jnp.where(inside, factor * pltpu.roll(offset, 8 - reach, 0) + offset, offset)
        factor = jnp.where(inside, factor * pltpu.roll(factor, 8 - reach, 0), factor)
    return jnp.where(row < 7, pltpu.roll(offset, 7, 0), 0.0), jnp.where(row < 7, pltpu.roll(factor, 7, 0), 1.0)


def pack_kernel(
    cells, held, sides, state_ref, owner_ref, tile_ref, offset_ref, height_ref, force_ref, width_ref,
    *refs,
):
    cells_s, cells_g = cells
    ahead, refs = refs[:AHEAD], refs[AHEAD:]
    out_s, out_g, refs = refs[:2], refs[2 : 2 + sides], refs[2 + sides :]
    pay_ref, fetched, refs = refs[0], refs[1 : 1 + AHEAD], refs[1 + AHEAD :]
    owner, tile, offset, height, force, width, sem = refs
    odd_s = lax.rem(lax.axis_index("stream"), 2)
    odd_g = lax.rem(lax.axis_index("girth"), 2)
    copies = []

    def start(source, target):
        copy = pltpu.make_async_copy(source, target, sem.at[len(copies)])
        copy.start()
        copies.append(copy)

    for pair in zip(ahead, fetched):
        start(*pair)
    slab = 2 * cells_g
    for side, out_ref in enumerate(out_s):
        low = odd_s if side == 0 else 1 - odd_s
        at = (cells_s - 2) * (1 - low)
        start(state_ref.at[:, pl.ds(at, 2)], out_ref.at[: EQ * slab].reshape(EQ, 2, cells_g, LANES))
    for side in range(sides):
        low = odd_g if side == 0 else 1 - odd_g
        at = (cells_g - 2) * (1 - low)
        rows = out_g[side].at[: 2 * EQ * cells_s]
        start(state_ref.at[:, :, pl.ds(at, 2), :], rows.reshape(EQ, cells_s, 2, LANES))
    for pair in zip(
        (owner_ref, tile_ref, offset_ref, height_ref, force_ref, width_ref),
        (owner, tile, offset, height, force, width),
    ):
        start(*pair)
    for copy in copies[2 + sides + AHEAD :]:
        copy.wait()
    tiles_g = cells_g // TILE
    number = tile[...].astype(jnp.float32)
    tile_s = jnp.floor(number * (1.0 / tiles_g))
    tile_g = number - tile_s * tiles_g
    wide = width[...]
    amplitude = 1.0 / (wide * wide * wide * math.pi**1.5)
    pay_ref[...] = jnp.zeros_like(pay_ref)
    pay_ref[0:1, :held] = tile_s * TILE + offset[0:1]
    pay_ref[1:2, :held] = tile_g * TILE + offset[1:2]
    pay_ref[2:3, :held] = height[...]
    pay_ref[3:4, :held] = 1.0 / (wide * wide)
    pay_ref[4:7, :held] = force[...] * amplitude
    pay_ref[7:8, :held] = owner[...].astype(jnp.float32)
    ends = [(ref, EQ * slab) for ref in out_s] + [(ref, 2 * EQ * cells_s) for ref in out_g]
    for out_ref, rows in ends:
        if out_ref.shape[0] > rows:
            out_ref[rows:, :] = pay_ref[...]
    for copy in copies[: 2 + sides + AHEAD]:
        copy.wait()


def coef_kernel(cells, *refs):
    cells_s, cells_g = cells
    columns = cells_s * cells_g
    dtau_ref, visc_ref, speed_ref, left_ref, right_ref, source_ref, advect_ref, state_ref = refs[:8]
    (
        r0_ref, adv_ref, lb_ref, rb_ref, fu_ref, gu_ref, fd_ref, gd_ref, dru_ref, rd_ref, gf_ref, pd_ref,
        crow_ref, spd_ref, turned, speeds,
    ) = refs[8:]
    crow_ref[LAST_STEP + 1 :] = jnp.zeros((MAP_ROWS - LAST_STEP - 1, LANES), jnp.float32)
    spd_ref[...] = jnp.zeros_like(spd_ref)
    for m in range(EQ):
        speeds[m] = jnp.broadcast_to(speed_ref[0:1, m : m + 1], (8, LANES))
        spd_ref[m : m + 1] = jnp.broadcast_to(speed_ref[0:1, m : m + 1], (1, LANES))
        for q in range(EQ):
            lb_ref[m * EQ + q] = jnp.broadcast_to(left_ref[m : m + 1, q : q + 1], (8, LANES))
            rb_ref[m * EQ + q] = jnp.broadcast_to(right_ref[m : m + 1, q : q + 1], (8, LANES))
    on = sub_iota((cells_g, cells_g)) == lax.broadcasted_iota(jnp.int32, (cells_g, cells_g), 1)
    for d in range(2):
        for s in range(cells_s):
            line = jnp.broadcast_to(advect_ref[d, s : s + 1, :], (cells_g, cells_g))
            line = jnp.sum(jnp.where(on, line, 0.0), axis=1, keepdims=True)
            adv_ref[d, s * cells_g : (s + 1) * cells_g, :] = jnp.broadcast_to(line, (cells_g, LANES))
    turned[0] = jnp.transpose(dtau_ref[...])
    turned[1] = jnp.transpose(visc_ref[...])
    crow_ref[FIRST_VISC : FIRST_VISC + 1] = turned[1, 0:1]
    crow_ref[LAST_VISC : LAST_VISC + 1] = turned[1, LANES - 1 : LANES]
    crow_ref[LAST_STEP : LAST_STEP + 1] = turned[0, LANES - 1 : LANES]

    def mode(m, carry):
        ahead = jnp.maximum(speeds[m], 0.0)
        back = jnp.maximum(-speeds[m], 0.0)
        step = [turned[0, pl.ds(j, 8, stride=STEPS), :] for j in range(STEPS)]
        visc = [turned[1, pl.ds(j, 8, stride=STEPS), :] for j in range(STEPS)]
        product, ups = None, []
        for j in range(STEPS):
            a = step[j] * (ahead + visc[j])
            ru = 1.0 / (1.0 + a)
            fu = a * ru
            product = fu if product is None else fu * product
            fu_ref[m, j], gu_ref[m, j], dru_ref[m, j] = fu, product, step[j] * ru
            ups.append(product)
        _, outer = up_entry(product, jnp.zeros_like(product))
        ups = [p * outer for p in ups]
        product, value, downs, values = None, None, [None] * STEPS, [None] * STEPS
        for j in reversed(range(STEPS)):
            b = step[j] * (back + visc[j])
            rd = 1.0 / (1.0 + b)
            fd = b * rd
            source = ups[j] * rd
            product = fd if product is None else fd * product
            value = source if value is None else fd * value + source
            fd_ref[m, j], gd_ref[m, j], rd_ref[m, j] = fd, product, rd
            downs[j], values[j] = product, value
        entry, outer = down_entry(product, value)
        for j in range(STEPS):
            gf_ref[m, j] = values[j] + downs[j] * entry
            pd_ref[m, j] = downs[j] * outer
        rows = (
            (PN, ups[-1][7:8]),
            (PD0, (downs[0] * outer)[0:1]),
            (G0, (values[0] + downs[0] * entry)[0:1]),
        )
        for kind, row in rows:
            crow_ref[pl.ds(kind * EQ + m, 1), :] = row
        return carry

    lax.fori_loop(0, EQ, mode, 0)
    girth = sub_iota((cells_g, LANES))
    lane = lax.broadcasted_iota(jnp.int32, (cells_g, LANES), 1)
    for s in range(cells_s):
        rows = slice(s * cells_g, (s + 1) * cells_g)
        speed_s, speed_g, visc = adv_ref[0, rows], adv_ref[1, rows], visc_ref[rows]
        state = [state_ref[q * columns + s * cells_g : q * columns + (s + 1) * cells_g] for q in range(EQ)]
        near_up, near_down = 0.125 - speed_s * (2.0 / 3.0), 0.125 + speed_s * (2.0 / 3.0)
        far_up, far_down = speed_s * (1.0 / 12.0) - 0.03125, -0.03125 - speed_s * (1.0 / 12.0)
        right1 = jnp.where(girth < cells_g - 1, 0.125 - speed_g * (2.0 / 3.0), 0.0)
        left1 = jnp.where(girth >= 1, 0.125 + speed_g * (2.0 / 3.0), 0.0)
        right2 = jnp.where(girth < cells_g - 2, speed_g * (1.0 / 12.0) - 0.03125, 0.0)
        left2 = jnp.where(girth >= 2, -0.03125 - speed_g * (1.0 / 12.0), 0.0)
        above = jnp.where(lane < LANES - 1, visc, 0.0)
        below = jnp.where(lane >= 1, visc, 0.0)
        centre = -0.375 - 2.0 * visc
        for q in range(EQ):
            here = state[q]
            total = centre * here
            for shift, weight in ((1, near_up), (-1, near_down), (2, far_up), (-2, far_down)):
                if 0 <= s + shift < cells_s:
                    at = q * columns + (s + shift) * cells_g
                    total = total + weight * state_ref[at : at + cells_g]
            total = total + right1 * pltpu.roll(here, cells_g - 1, 0) + left1 * pltpu.roll(here, 1, 0)
            total = total + right2 * pltpu.roll(here, cells_g - 2, 0) + left2 * pltpu.roll(here, 2, 0)
            total = total + above * pltpu.roll(here, LANES - 1, 1) + below * pltpu.roll(here, 1, 1)
            for f in range(EQ):
                total = total + jnp.broadcast_to(source_ref[q : q + 1, f : f + 1], (cells_g, LANES)) * state[f]
            r0_ref[q * columns + s * cells_g : q * columns + (s + 1) * cells_g] = total
    sub, lanes = sub_iota(), lax.broadcasted_iota(jnp.int32, (8, LANES), 1)
    ends = ((sub == 0) & (lanes == 0)) | ((sub == 1) & (lanes == LANES - 1))
    ends = jnp.where(ends, 1.0, 0.0)
    edge = [
        lax.dot_general(
            ends, state_ref[q * columns : (q + 1) * columns], NT, precision=HIGHEST,
            preferred_element_type=jnp.float32,
        )
        for q in range(EQ)
    ]
    for m in range(EQ):
        mixed = lb_ref[m * EQ] * edge[0]
        for q in range(1, EQ):
            mixed = mixed + lb_ref[m * EQ + q] * edge[q]
        crow_ref[LSF * EQ + m : LSF * EQ + m + 1] = mixed[0:1]
        crow_ref[LSL * EQ + m : LSL * EQ + m + 1] = mixed[1:2]


def pair_kernel(one_ref, two_ref, crow_ref, out_ref):
    out_ref[...] = one_ref[...] + pltpu.roll(two_ref[...], 8, 1)


def halo_kernel(cells, counts, sides, a_ref, b_ref, *refs):
    cells_s, cells_g = cells
    count_s, count_g = counts
    columns = cells_s * cells_g
    g_refs, (r0_ref, adv_ref, lb_ref), refs = refs[:sides], refs[sides : sides + 3], refs[sides + 3 :]
    turned, res_ref = refs[-2:]
    if len(refs) > 2:
        pay_ref, pair_ref, kept_ref = refs[0], refs[1], refs[-3]
        rows = slice(EQ * 2 * cells_g, EQ * 2 * cells_g + 8)
        kept = pay_ref[...] + pltpu.roll(pair_ref[...], 32, 1)
        kept = kept + pltpu.roll(a_ref[rows], 8, 1) + pltpu.roll(b_ref[rows], 16, 1)
        rows = slice(EQ * 2 * cells_s, EQ * 2 * cells_s + 8)
        kept_ref[...] = kept + pltpu.roll(g_refs[0][rows], 24, 1)
    at_s, at_g = lax.axis_index("stream"), lax.axis_index("girth")
    odd_s, odd_g = lax.rem(at_s, 2) == 1, lax.rem(at_g, 2) == 1
    low_s = jnp.where(at_s > 0, 1.0, 0.0)
    high_s = jnp.where(at_s < count_s - 1, 1.0, 0.0)
    low_g = jnp.where(at_g > 0, 1.0, 0.0)
    high_g = jnp.where(at_g < count_g - 1, 1.0, 0.0)
    speed = [adv_ref[0, s * cells_g : (s + 1) * cells_g] for s in range(cells_s)]
    sub = sub_iota()
    zero = jnp.zeros((8, LANES), jnp.float32)
    turn = []
    for s in range(cells_s):
        lead = adv_ref[1, s * cells_g : s * cells_g + 8]
        tail = adv_ref[1, (s + 1) * cells_g - 8 : (s + 1) * cells_g]
        near, far = low_g * (0.125 + lead * (2.0 / 3.0)), low_g * (-0.03125 - lead * (1.0 / 12.0))
        near_low = jnp.where(sub == 0, near, jnp.where(sub == 1, far, zero))
        far_low = jnp.where(sub == 0, far, zero)
        near, far = high_g * (0.125 - tail * (2.0 / 3.0)), high_g * (tail * (1.0 / 12.0) - 0.03125)
        near_high = jnp.where(sub == 7, near, jnp.where(sub == 6, far, zero))
        far_high = jnp.where(sub == 7, far, zero)
        turn.append((near_low, far_low, near_high, far_high))
    wide = cells_g
    for q in range(EQ):
        slab = slice(q * 2 * wide, (q + 1) * 2 * wide)
        slab_a, slab_b = a_ref[slab], b_ref[slab]
        low, high = jnp.where(odd_s, slab_a, slab_b), jnp.where(odd_s, slab_b, slab_a)
        for s in range(cells_s):
            rows = slice(q * columns + s * wide, q * columns + (s + 1) * wide)
            total = r0_ref[rows]
            if s == 0:
                total = total + low_s * (0.125 + speed[s] * (2.0 / 3.0)) * low[wide:]
                total = total + low_s * (-0.03125 - speed[s] * (1.0 / 12.0)) * low[:wide]
            if s == 1:
                total = total + low_s * (-0.03125 - speed[s] * (1.0 / 12.0)) * low[wide:]
            if s == cells_s - 2:
                total = total + high_s * (speed[s] * (1.0 / 12.0) - 0.03125) * high[:wide]
            if s == cells_s - 1:
                total = total + high_s * (0.125 - speed[s] * (2.0 / 3.0)) * high[:wide]
                total = total + high_s * (speed[s] * (1.0 / 12.0) - 0.03125) * high[wide:]
            near_low, far_low, near_high, far_high = turn[s]
            at = (2 * (q * cells_s + s), 2 * (q * cells_s + s) + 1)
            part = [jnp.broadcast_to(g_refs[0][i : i + 1], (8, LANES)) for i in at]
            part_low = part_high = part
            if sides > 1:
                other = [jnp.broadcast_to(g_refs[1][i : i + 1], (8, LANES)) for i in at]
                part_low = [jnp.where(odd_g, x, y) for x, y in zip(part, other)]
                part_high = [jnp.where(odd_g, y, x) for x, y in zip(part, other)]
            lead, tail = slice(rows.start, rows.start + 8), slice(rows.stop - 8, rows.stop)
            if wide > 16:
                res_ref[rows] = total
            res_ref[lead] = total[:8] + near_low * part_low[1] + far_low * part_low[0]
            res_ref[tail] = total[wide - 8 :] + near_high * part_high[0] + far_high * part_high[1]
    tiles = columns // 8
    for m in range(EQ):
        total = None
        for q in range(EQ):
            part = lb_ref[m * EQ + q][None] * res_ref[q * columns : (q + 1) * columns].reshape(tiles, 8, LANES)
            total = part if total is None else total + part
        turned[m] = jnp.transpose(total.reshape(columns, LANES))


def sweep_kernel(
    cells, count_g, shared, turned, lb_ref, fu_ref, gu_ref, fd_ref, gd_ref, dru_ref, rd_ref, crow_ref, *refs
):
    cells_s, cells_g = cells
    columns = cells_s * cells_g
    elems = refs[:-3]
    h_ref, map_ref, field_ref = refs[-3:]
    at_s, at_g, at_w = (lax.axis_index(name) for name in ("stream", "girth", "wall"))
    mine = (at_s * count_g + at_g).astype(jnp.float32)
    base_s = sub_iota((cells_s, LANES)).astype(jnp.float32) + 0.5
    base_g = sub_iota((cells_g, LANES)).astype(jnp.float32) + 0.5
    first = sub_iota() * STEPS + at_w * LANES
    base_w = jnp.concatenate([first + j for j in range(STEPS)], axis=0).astype(jnp.float32) + 0.5

    def spread(pay):
        sharp = -pay[3:4]
        prof_s = jnp.exp(sharp * (base_s - pay[0:1]) ** 2)
        prof_g = jnp.exp(sharp * (base_g - pay[1:2]) ** 2)
        prof_w = jnp.exp(sharp * (base_w - pay[2:3]) ** 2)
        push = jnp.where(pay[7:8] == mine, pay[4:7], 0.0)
        plane = jnp.concatenate([prof_g * prof_s[s : s + 1] for s in range(cells_s)], axis=0)
        weights = jnp.concatenate([plane * push[c : c + 1] for c in range(3)], axis=0)
        return lax.dot_general(prof_w, weights, NT, precision=HIGH, preferred_element_type=jnp.float32)

    if shared:
        field_ref[...] = spread(elems[0][...] + pltpu.roll(elems[1][...], 48, 1))
    else:
        field_ref[...] = jnp.zeros_like(field_ref)

        def chunk(i, carry):
            field_ref[...] += spread(elems[0][i])
            return carry

        lax.fori_loop(0, elems[0].shape[0], chunk, 0)
    map_ref[...] = crow_ref[...]
    for m in range(EQ):
        value, values = None, []
        for j in range(STEPS):
            source = turned[m, pl.ds(j, 8, stride=STEPS), :]
            for c in range(3):
                source = source + lb_ref[m * EQ + 1 + c] * field_ref[8 * j : 8 * j + 8, c * columns : (c + 1) * columns]
            source = source * dru_ref[m, j]
            value = source if value is None else fu_ref[m, j] * value + source
            values.append(value)
        entry, _ = up_entry(gu_ref[m, STEPS - 1], value)
        values = [v + gu_ref[m, j] * entry for j, v in enumerate(values)]
        map_ref[UP * EQ + m : UP * EQ + m + 1] = values[-1][7:8]
        value = None
        for j in reversed(range(STEPS)):
            source = values[j] * rd_ref[m, j]
            value = source if value is None else fd_ref[m, j] * value + source
            values[j] = value
        entry, _ = down_entry(gd_ref[m, 0], value)
        for j in range(STEPS):
            values[j] = values[j] + gd_ref[m, j] * entry
            h_ref[m, j] = values[j]
        map_ref[DOWN * EQ + m : DOWN * EQ + m + 1] = values[0][0:1]


def close_kernel(count, *refs):
    maps = refs[:count]
    h_ref, gf_ref, pd_ref, rb_ref, spd_ref, out_ref, all_ref, modal, turned, ready, sem = refs[count:]
    here = lax.axis_index("wall")
    for r, ref in zip(rounds(count), maps):
        all_ref[source(here, r, count)] = ref[...]

    def get(j, kind):
        return all_ref[j, kind * EQ : (kind + 1) * EQ]

    ahead = jnp.maximum(spd_ref[:EQ], 0.0)
    back = jnp.maximum(-spd_ref[:EQ], 0.0)
    first = [all_ref[j, FIRST_VISC : FIRST_VISC + 1] for j in range(count)]
    last = [all_ref[j, LAST_VISC : LAST_VISC + 1] for j in range(count)]
    step = [all_ref[j, LAST_STEP : LAST_STEP + 1] for j in range(count)]
    share = [1.0 / (1.0 + step[j] * (ahead + last[j])) for j in range(count)]
    zero = jnp.zeros((EQ, LANES), jnp.float32)
    entry, entries, mine_up = zero, [], zero
    for j in range(count):
        if j > 0:
            entry = entry + first[j] / (ahead + first[j]) * get(j - 1, LSL)
        entries.append(entry)
        mine_up = jnp.where(here == j, entry, mine_up)
        entry = get(j, PN) * entry + get(j, UP)
        if j < count - 1:
            entry = entry + share[j] * step[j] * last[j] * get(j + 1, LSF)
    above, mine_down = zero, zero
    for j in reversed(range(count)):
        if j < count - 1:
            above = above + share[j] * last[j] / (back + last[j]) * get(j + 1, LSF)
        mine_down = jnp.where(here == j, above, mine_down)
        above = get(j, PD0) * above + get(j, G0) * entries[j] + get(j, DOWN)
    for m in range(EQ):
        up = jnp.broadcast_to(mine_up[m : m + 1], (8, LANES))
        down = jnp.broadcast_to(mine_down[m : m + 1], (8, LANES))
        for j in range(STEPS):
            modal[m, j] = h_ref[m, j] + gf_ref[m, j] * up + pd_ref[m, j] * down
    copies = []
    for k in range(3):
        for q in (2 * k, 2 * k + 1):
            weight = [rb_ref[q * EQ + m] for m in range(EQ)]
            for j in range(STEPS):
                total = weight[0] * modal[0, j]
                for m in range(1, EQ):
                    total = total + weight[m] * modal[m, j]
                turned[q, pl.ds(j, 8, stride=STEPS), :] = total
            ready[q] = jnp.transpose(turned[q])
        part = slice(2 * k, 2 * k + 2)
        copy = pltpu.make_async_copy(ready.at[part], out_ref.at[part], sem.at[k])
        copy.start()
        copies.append(copy)
    for copy in copies:
        copy.wait()


def rounds(count):
    return sorted(range(count), key=lambda r: (r != 0, r != count - 1, r))


def source(here, r, count):
    if count & (count - 1) == 0:
        return here ^ r
    return (here + count - r) % count


def blocks(count_s, count_g, count_w, moves):
    pairs = []
    for s in range(count_s):
        for g in range(count_g):
            for w in range(count_w):
                at_s, at_g = moves[w % 2]
                target = ((s ^ at_s) * count_g + (g ^ at_g)) * count_w + w
                pairs.append(((s * count_g + g) * count_w + w, target))
    return pairs


def swaps(count, side):
    if side == 0:
        return [(i, i ^ 1) for i in range(count)]
    return [(i, (i + (1 if i % 2 else -1)) % count) for i in range(count)]


def local(
    state,
    advect,
    dtau,
    viscosity,
    mode_speed,
    left_modes,
    right_modes,
    source_jac,
    elem_owner,
    elem_tile,
    elem_offset,
    elem_height,
    elem_force,
    elem_width,
):
    f32 = jnp.float32
    cells = (state.shape[1], state.shape[2])
    cells_s, cells_g = cells
    columns = cells_s * cells_g
    count_s, count_g, count_w = (lax.axis_size(name) for name in ("stream", "girth", "wall"))
    held = elem_owner.shape[0]
    shared = count_s == 4 and count_g == 2 and count_w % 2 == 0 and held <= 8
    sides = 1 if count_g == 2 else 2
    extra = 8 if shared else 0
    ahead = (
        dtau.reshape(columns, LANES),
        viscosity.reshape(columns, LANES),
        mode_speed.reshape(1, EQ),
        left_modes,
        right_modes,
        source_jac,
        advect,
    )
    outs = [(EQ * 2 * cells_g + extra, LANES)] * 2
    outs += [(EQ * 2 * cells_s + extra, LANES)] * sides + [(8, LANES)] + [part.shape for part in ahead]
    packed = call(
        functools.partial(pack_kernel, cells, held, sides),
        outs,
        state,
        elem_owner.T,
        elem_tile.reshape(1, held),
        elem_offset.T,
        elem_height.reshape(1, held),
        elem_force.T,
        elem_width.reshape(1, held),
        *ahead,
        scratch=[((1, held), jnp.int32), ((1, held), jnp.int32), ((2, held), f32), ((1, held), f32)]
        + [((3, held), f32), ((1, held), f32)],
        far=range(7 + AHEAD),
        copies=sides + 8 + AHEAD,
    )
    pay, ahead = packed[2 + sides], packed[3 + sides :]
    halo_a = lax.ppermute(packed[0], "stream", swaps(count_s, 0))
    halo_b = lax.ppermute(packed[1], "stream", swaps(count_s, 1))
    halo_g = [lax.ppermute(packed[2 + i], "girth", swaps(count_g, i)) for i in range(sides)]
    if shared:
        every = ("stream", "girth", "wall")
        far = [
            lax.ppermute(pay, every, blocks(count_s, count_g, count_w, moves))
            for moves in (((1, 1), (2, 1)), ((2, 0), (3, 1)))
        ]
    wide = (EQ, STEPS, 8, LANES)
    r0, adv, lb, rb, fu, gu, fd, gd, dru, rd, gf, pd, crow, spd = call(
        functools.partial(coef_kernel, cells),
        [(EQ * columns, LANES), (2, columns, LANES), (EQ * EQ, 8, LANES), (EQ * EQ, 8, LANES)]
        + [wide] * 8
        + [(MAP_ROWS, LANES), (8, LANES)],
        *ahead,
        state.reshape(EQ * columns, LANES),
        scratch=[((2, LANES, columns), f32), ((EQ, 8, LANES), f32)],
        cost=4 << 20,
    )
    if shared:
        (pair,) = call(pair_kernel, [(8, LANES)], *far, crow)
        other = lax.ppermute(pair, "wall", [(i, i ^ 1) for i in range(count_w)])
    *kept, turned = call(
        functools.partial(halo_kernel, cells, (count_s, count_g), sides),
        [(8, LANES)] * shared + [(EQ, LANES, columns)],
        halo_a, halo_b, *halo_g, r0, adv, lb, *((pay, pair) if shared else ()),
        scratch=[((EQ * columns, LANES), f32)],
        cost=1 << 20,
    )
    elems = (*kept, other) if shared else (lax.all_gather(pay, ("stream", "girth")),)
    h, block_map = call(
        functools.partial(sweep_kernel, cells, count_g, shared),
        [wide, (MAP_ROWS, LANES)],
        turned, lb, fu, gu, fd, gd, dru, rd, crow, *elems,
        scratch=[((LANES, 3 * columns), f32)],
        cost=1 << 20,
    )
    maps = [block_map]
    for r in range(1, count_w):
        pairs = [(int(source(i, r, count_w)), i) for i in range(count_w)]
        maps.append(lax.ppermute(block_map, "wall", pairs))
    (out,) = call(
        functools.partial(close_kernel, count_w),
        [(EQ, columns, LANES)],
        *[maps[r] for r in rounds(count_w)], h, gf, pd, rb, spd,
        scratch=[((count_w, MAP_ROWS, LANES), f32), (wide, f32), ((EQ, LANES, columns), f32)]
        + [((EQ, columns, LANES), f32)],
        cost=1 << 20,
        far_out=(0,),
        copies=3,
    )
    return out.reshape(state.shape)


def solution(mesh):
    in_specs = (
        P(None, "stream", "girth", "wall"),
        P(None, "stream", "girth"),
        P("stream", "girth", "wall"),
        P("stream", "girth", "wall"),
        P(),
        P(),
        P(),
        P(),
        P(("stream", "girth"), None),
        P(("stream", "girth")),
        P(("stream", "girth"), None),
        P(("stream", "girth")),
        P(("stream", "girth"), None),
        P(("stream", "girth")),
    )
    out_specs = P(None, "stream", "girth", "wall")
    return jax.shard_map(local, mesh=mesh, in_specs=in_specs, out_specs=out_specs, check_vma=False)
```

```python
import functools
import math

import jax
import jax.numpy as jnp
from jax import lax
from jax.experimental import pallas as pl
from jax.experimental.pallas import tpu as pltpu
from jax.sharding import PartitionSpec as P

TILE = 8
EQ = 6
LANES = 128
STEPS = 16
HIGHEST = lax.Precision.HIGHEST
HIGH = lax.Precision.HIGH
NT = (((1,), (1,)), ((), ()))
PN, PD0, G0, LSF, LSL, UP, DOWN = range(7)
FIRST_VISC, LAST_VISC, LAST_STEP = 42, 43, 44
MAP_ROWS = 48
AHEAD = 7


def call(kernel, outs, *args, scratch=(), cost=0, far=(), far_out=(), copies=0):
    shapes = [jax.ShapeDtypeStruct(shape, jnp.float32) for shape in outs]

    def spec(is_far):
        return pl.BlockSpec(memory_space=pltpu.HBM if is_far else pltpu.VMEM)

    args = [pltpu.with_memory_space_constraint(part, pltpu.HBM) if i in far else part for i, part in enumerate(args)]
    return pl.pallas_call(
        kernel,
        out_shape=shapes,
        in_specs=[spec(i in far) for i in range(len(args))],
        out_specs=[spec(i in far_out) for i in range(len(outs))],
        scratch_shapes=[pltpu.VMEM(shape, kind) for shape, kind in scratch]
        + ([pltpu.SemaphoreType.DMA((copies,))] if copies else []),
        compiler_params=pltpu.CompilerParams(vmem_limit_bytes=16 << 20),
        cost_estimate=pl.CostEstimate(flops=cost, bytes_accessed=cost, transcendentals=0),
    )(*args)


def sub_iota(shape=(8, LANES)):
    return lax.broadcasted_iota(jnp.int32, shape, 0)


def up_entry(factor, offset):
    row = sub_iota()
    for reach in (1, 2, 4):
        inside = row >= reach
        offset = jnp.where(inside, factor * pltpu.roll(offset, reach, 0) + offset, offset)
        factor = jnp.where(inside, factor * pltpu.roll(factor, reach, 0), factor)
    return jnp.where(row >= 1, pltpu.roll(offset, 1, 0), 0.0), jnp.where(row >= 1, pltpu.roll(factor, 1, 0), 1.0)


def down_entry(factor, offset):
    row = sub_iota()
    for reach in (1, 2, 4):
        inside = row < 8 - reach
        offset = jnp.where(inside, factor * pltpu.roll(offset, 8 - reach, 0) + offset, offset)
        factor = jnp.where(inside, factor * pltpu.roll(factor, 8 - reach, 0), factor)
    return jnp.where(row < 7, pltpu.roll(offset, 7, 0), 0.0), jnp.where(row < 7, pltpu.roll(factor, 7, 0), 1.0)


def pack_kernel(
    cells, held, sides, state_ref, owner_ref, tile_ref, offset_ref, height_ref, force_ref, width_ref,
    *refs,
):
    cells_s, cells_g = cells
    ahead, refs = refs[:AHEAD], refs[AHEAD:]
    out_s, out_g, refs = refs[:2], refs[2 : 2 + sides], refs[2 + sides :]
    pay_ref, fetched, refs = refs[0], refs[1 : 1 + AHEAD], refs[1 + AHEAD :]
    owner, tile, offset, height, force, width, sem = refs
    odd_s = lax.rem(lax.axis_index("stream"), 2)
    odd_g = lax.rem(lax.axis_index("girth"), 2)
    copies = []

    def start(source, target):
        copy = pltpu.make_async_copy(source, target, sem.at[len(copies)])
        copy.start()
        copies.append(copy)

    for pair in zip(ahead, fetched):
        start(*pair)
    slab = 2 * cells_g
    for side, out_ref in enumerate(out_s):
        low = odd_s if side == 0 else 1 - odd_s
        at = (cells_s - 2) * (1 - low)
        start(state_ref.at[:, pl.ds(at, 2)], out_ref.at[: EQ * slab].reshape(EQ, 2, cells_g, LANES))
    for side in range(sides):
        low = odd_g if side == 0 else 1 - odd_g
        at = (cells_g - 2) * (1 - low)
        rows = out_g[side].at[: 2 * EQ * cells_s]
        start(state_ref.at[:, :, pl.ds(at, 2), :], rows.reshape(EQ, cells_s, 2, LANES))
    for pair in zip(
        (owner_ref, tile_ref, offset_ref, height_ref, force_ref, width_ref),
        (owner, tile, offset, height, force, width),
    ):
        start(*pair)
    for copy in copies[2 + sides + AHEAD :]:
        copy.wait()
    tiles_g = cells_g // TILE
    number = tile[...].astype(jnp.float32)
    tile_s = jnp.floor(number * (1.0 / tiles_g))
    tile_g = number - tile_s * tiles_g
    wide = width[...]
    amplitude = 1.0 / (wide * wide * wide * math.pi**1.5)
    pay_ref[...] = jnp.zeros_like(pay_ref)
    pay_ref[0:1, :held] = tile_s * TILE + offset[0:1]
    pay_ref[1:2, :held] = tile_g * TILE + offset[1:2]
    pay_ref[2:3, :held] = height[...]
    pay_ref[3:4, :held] = 1.0 / (wide * wide)
    pay_ref[4:7, :held] = force[...] * amplitude
    pay_ref[7:8, :held] = owner[...].astype(jnp.float32)
    ends = [(ref, EQ * slab) for ref in out_s] + [(ref, 2 * EQ * cells_s) for ref in out_g]
    for out_ref, rows in ends:
        if out_ref.shape[0] > rows:
            out_ref[rows:, :] = pay_ref[...]
    for copy in copies[: 2 + sides + AHEAD]:
        copy.wait()


def coef_kernel(cells, *refs):
    cells_s, cells_g = cells
    columns = cells_s * cells_g
    dtau_ref, visc_ref, speed_ref, left_ref, right_ref, source_ref, advect_ref, state_ref = refs[:8]
    (
        r0_ref, adv_ref, lb_ref, rb_ref, fu_ref, gu_ref, fd_ref, gd_ref, dru_ref, rd_ref, gf_ref, pd_ref,
        crow_ref, spd_ref, turned, speeds,
    ) = refs[8:]
    crow_ref[LAST_STEP + 1 :] = jnp.zeros((MAP_ROWS - LAST_STEP - 1, LANES), jnp.float32)
    spd_ref[...] = jnp.zeros_like(spd_ref)
    for m in range(EQ):
        speeds[m] = jnp.broadcast_to(speed_ref[0:1, m : m + 1], (8, LANES))
        spd_ref[m : m + 1] = jnp.broadcast_to(speed_ref[0:1, m : m + 1], (1, LANES))
        for q in range(EQ):
            lb_ref[m * EQ + q] = jnp.broadcast_to(left_ref[m : m + 1, q : q + 1], (8, LANES))
            rb_ref[m * EQ + q] = jnp.broadcast_to(right_ref[m : m + 1, q : q + 1], (8, LANES))
    on = sub_iota((cells_g, cells_g)) == lax.broadcasted_iota(jnp.int32, (cells_g, cells_g), 1)
    for d in range(2):
        for s in range(cells_s):
            line = jnp.broadcast_to(advect_ref[d, s : s + 1, :], (cells_g, cells_g))
            line = jnp.sum(jnp.where(on, line, 0.0), axis=1, keepdims=True)
            adv_ref[d, s * cells_g : (s + 1) * cells_g, :] = jnp.broadcast_to(line, (cells_g, LANES))
    turned[0] = jnp.transpose(dtau_ref[...])
    turned[1] = jnp.transpose(visc_ref[...])
    crow_ref[FIRST_VISC : FIRST_VISC + 1] = turned[1, 0:1]
    crow_ref[LAST_VISC : LAST_VISC + 1] = turned[1, LANES - 1 : LANES]
    crow_ref[LAST_STEP : LAST_STEP + 1] = turned[0, LANES - 1 : LANES]

    def mode(m, carry):
        ahead = jnp.maximum(speeds[m], 0.0)
        back = jnp.maximum(-speeds[m], 0.0)
        step = [turned[0, pl.ds(j, 8, stride=STEPS), :] for j in range(STEPS)]
        visc = [turned[1, pl.ds(j, 8, stride=STEPS), :] for j in range(STEPS)]
        product, ups = None, []
        for j in range(STEPS):
            a = step[j] * (ahead + visc[j])
            ru = 1.0 / (1.0 + a)
            fu = a * ru
            product = fu if product is None else fu * product
            fu_ref[m, j], gu_ref[m, j], dru_ref[m, j] = fu, product, step[j] * ru
            ups.append(product)
        _, outer = up_entry(product, jnp.zeros_like(product))
        ups = [p * outer for p in ups]
        product, value, downs, values = None, None, [None] * STEPS, [None] * STEPS
        for j in reversed(range(STEPS)):
            b = step[j] * (back + visc[j])
            rd = 1.0 / (1.0 + b)
            fd = b * rd
            source = ups[j] * rd
            product = fd if product is None else fd * product
            value = source if value is None else fd * value + source
            fd_ref[m, j], gd_ref[m, j], rd_ref[m, j] = fd, product, rd
            downs[j], values[j] = product, value
        entry, outer = down_entry(product, value)
        for j in range(STEPS):
            gf_ref[m, j] = values[j] + downs[j] * entry
            pd_ref[m, j] = downs[j] * outer
        rows = (
            (PN, ups[-1][7:8]),
            (PD0, (downs[0] * outer)[0:1]),
            (G0, (values[0] + downs[0] * entry)[0:1]),
        )
        for kind, row in rows:
            crow_ref[pl.ds(kind * EQ + m, 1), :] = row
        return carry

    lax.fori_loop(0, EQ, mode, 0)
    girth = sub_iota((cells_g, LANES))
    lane = lax.broadcasted_iota(jnp.int32, (cells_g, LANES), 1)
    for s in range(cells_s):
        rows = slice(s * cells_g, (s + 1) * cells_g)
        speed_s, speed_g, visc = adv_ref[0, rows], adv_ref[1, rows], visc_ref[rows]
        state = [state_ref[q * columns + s * cells_g : q * columns + (s + 1) * cells_g] for q in range(EQ)]
        near_up, near_down = 0.125 - speed_s * (2.0 / 3.0), 0.125 + speed_s * (2.0 / 3.0)
        far_up, far_down = speed_s * (1.0 / 12.0) - 0.03125, -0.03125 - speed_s * (1.0 / 12.0)
        right1 = jnp.where(girth < cells_g - 1, 0.125 - speed_g * (2.0 / 3.0), 0.0)
        left1 = jnp.where(girth >= 1, 0.125 + speed_g * (2.0 / 3.0), 0.0)
        right2 = jnp.where(girth < cells_g - 2, speed_g * (1.0 / 12.0) - 0.03125, 0.0)
        left2 = jnp.where(girth >= 2, -0.03125 - speed_g * (1.0 / 12.0), 0.0)
        above = jnp.where(lane < LANES - 1, visc, 0.0)
        below = jnp.where(lane >= 1, visc, 0.0)
        centre = -0.375 - 2.0 * visc
        for q in range(EQ):
            here = state[q]
            total = centre * here
            for shift, weight in ((1, near_up), (-1, near_down), (2, far_up), (-2, far_down)):
                if 0 <= s + shift < cells_s:
                    at = q * columns + (s + shift) * cells_g
                    total = total + weight * state_ref[at : at + cells_g]
            total = total + right1 * pltpu.roll(here, cells_g - 1, 0) + left1 * pltpu.roll(here, 1, 0)
            total = total + right2 * pltpu.roll(here, cells_g - 2, 0) + left2 * pltpu.roll(here, 2, 0)
            total = total + above * pltpu.roll(here, LANES - 1, 1) + below * pltpu.roll(here, 1, 1)
            for f in range(EQ):
                total = total + jnp.broadcast_to(source_ref[q : q + 1, f : f + 1], (cells_g, LANES)) * state[f]
            r0_ref[q * columns + s * cells_g : q * columns + (s + 1) * cells_g] = total
    sub, lanes = sub_iota(), lax.broadcasted_iota(jnp.int32, (8, LANES), 1)
    ends = ((sub == 0) & (lanes == 0)) | ((sub == 1) & (lanes == LANES - 1))
    ends = jnp.where(ends, 1.0, 0.0)
    edge = [
        lax.dot_general(
            ends, state_ref[q * columns : (q + 1) * columns], NT, precision=HIGHEST,
            preferred_element_type=jnp.float32,
        )
        for q in range(EQ)
    ]
    for m in range(EQ):
        mixed = lb_ref[m * EQ] * edge[0]
        for q in range(1, EQ):
            mixed = mixed + lb_ref[m * EQ + q] * edge[q]
        crow_ref[LSF * EQ + m : LSF * EQ + m + 1] = mixed[0:1]
        crow_ref[LSL * EQ + m : LSL * EQ + m + 1] = mixed[1:2]


def pair_kernel(one_ref, two_ref, crow_ref, out_ref):
    out_ref[...] = one_ref[...] + pltpu.roll(two_ref[...], 8, 1)


def halo_kernel(cells, counts, sides, a_ref, b_ref, *refs):
    cells_s, cells_g = cells
    count_s, count_g = counts
    columns = cells_s * cells_g
    g_refs, (r0_ref, adv_ref, lb_ref), refs = refs[:sides], refs[sides : sides + 3], refs[sides + 3 :]
    turned, res_ref = refs[-2:]
    if len(refs) > 2:
        pay_ref, pair_ref, kept_ref = refs[0], refs[1], refs[-3]
        rows = slice(EQ * 2 * cells_g, EQ * 2 * cells_g + 8)
        kept = pay_ref[...] + pltpu.roll(pair_ref[...], 32, 1)
        kept = kept + pltpu.roll(a_ref[rows], 8, 1) + pltpu.roll(b_ref[rows], 16, 1)
        rows = slice(EQ * 2 * cells_s, EQ * 2 * cells_s + 8)
        kept_ref[...] = kept + pltpu.roll(g_refs[0][rows], 24, 1)
    at_s, at_g = lax.axis_index("stream"), lax.axis_index("girth")
    odd_s, odd_g = lax.rem(at_s, 2) == 1, lax.rem(at_g, 2) == 1
    low_s = jnp.where(at_s > 0, 1.0, 0.0)
    high_s = jnp.where(at_s < count_s - 1, 1.0, 0.0)
    low_g = jnp.where(at_g > 0, 1.0, 0.0)
    high_g = jnp.where(at_g < count_g - 1, 1.0, 0.0)
    speed = [adv_ref[0, s * cells_g : (s + 1) * cells_g] for s in range(cells_s)]
    sub = sub_iota()
    zero = jnp.zeros((8, LANES), jnp.float32)
    turn = []
    for s in range(cells_s):
        lead = adv_ref[1, s * cells_g : s * cells_g + 8]
        tail = adv_ref[1, (s + 1) * cells_g - 8 : (s + 1) * cells_g]
        near, far = low_g * (0.125 + lead * (2.0 / 3.0)), low_g * (-0.03125 - lead * (1.0 / 12.0))
        near_low = jnp.where(sub == 0, near, jnp.where(sub == 1, far, zero))
        far_low = jnp.where(sub == 0, far, zero)
        near, far = high_g * (0.125 - tail * (2.0 / 3.0)), high_g * (tail * (1.0 / 12.0) - 0.03125)
        near_high = jnp.where(sub == 7, near, jnp.where(sub == 6, far, zero))
        far_high = jnp.where(sub == 7, far, zero)
        turn.append((near_low, far_low, near_high, far_high))
    wide = cells_g
    for q in range(EQ):
        slab = slice(q * 2 * wide, (q + 1) * 2 * wide)
        slab_a, slab_b = a_ref[slab], b_ref[slab]
        low, high = jnp.where(odd_s, slab_a, slab_b), jnp.where(odd_s, slab_b, slab_a)
        for s in range(cells_s):
            rows = slice(q * columns + s * wide, q * columns + (s + 1) * wide)
            total = r0_ref[rows]
            if s == 0:
                total = total + low_s * (0.125 + speed[s] * (2.0 / 3.0)) * low[wide:]
                total = total + low_s * (-0.03125 - speed[s] * (1.0 / 12.0)) * low[:wide]
            if s == 1:
                total = total + low_s * (-0.03125 - speed[s] * (1.0 / 12.0)) * low[wide:]
            if s == cells_s - 2:
                total = total + high_s * (speed[s] * (1.0 / 12.0) - 0.03125) * high[:wide]
            if s == cells_s - 1:
                total = total + high_s * (0.125 - speed[s] * (2.0 / 3.0)) * high[:wide]
                total = total + high_s * (speed[s] * (1.0 / 12.0) - 0.03125) * high[wide:]
            near_low, far_low, near_high, far_high = turn[s]
            at = (2 * (q * cells_s + s), 2 * (q * cells_s + s) + 1)
            part = [jnp.broadcast_to(g_refs[0][i : i + 1], (8, LANES)) for i in at]
            part_low = part_high = part
            if sides > 1:
                other = [jnp.broadcast_to(g_refs[1][i : i + 1], (8, LANES)) for i in at]
                part_low = [jnp.where(odd_g, x, y) for x, y in zip(part, other)]
                part_high = [jnp.where(odd_g, y, x) for x, y in zip(part, other)]
            lead, tail = slice(rows.start, rows.start + 8), slice(rows.stop - 8, rows.stop)
            if wide > 16:
                res_ref[rows] = total
            res_ref[lead] = total[:8] + near_low * part_low[1] + far_low * part_low[0]
            res_ref[tail] = total[wide - 8 :] + near_high * part_high[0] + far_high * part_high[1]
    tiles = columns // 8
    for m in range(EQ):
        total = None
        for q in range(EQ):
            part = lb_ref[m * EQ + q][None] * res_ref[q * columns : (q + 1) * columns].reshape(tiles, 8, LANES)
            total = part if total is None else total + part
        turned[m] = jnp.transpose(total.reshape(columns, LANES))


def sweep_kernel(
    cells, count_g, shared, turned, lb_ref, fu_ref, gu_ref, fd_ref, gd_ref, dru_ref, rd_ref, crow_ref, *refs
):
    cells_s, cells_g = cells
    columns = cells_s * cells_g
    elems = refs[:-3]
    h_ref, map_ref, field_ref = refs[-3:]
    at_s, at_g, at_w = (lax.axis_index(name) for name in ("stream", "girth", "wall"))
    mine = (at_s * count_g + at_g).astype(jnp.float32)
    base_s = sub_iota((cells_s, LANES)).astype(jnp.float32) + 0.5
    base_g = sub_iota((cells_g, LANES)).astype(jnp.float32) + 0.5
    first = sub_iota() * STEPS + at_w * LANES
    base_w = jnp.concatenate([first + j for j in range(STEPS)], axis=0).astype(jnp.float32) + 0.5

    def spread(pay):
        sharp = -pay[3:4]
        prof_s = jnp.exp(sharp * (base_s - pay[0:1]) ** 2)
        prof_g = jnp.exp(sharp * (base_g - pay[1:2]) ** 2)
        prof_w = jnp.exp(sharp * (base_w - pay[2:3]) ** 2)
        push = jnp.where(pay[7:8] == mine, pay[4:7], 0.0)
        plane = jnp.concatenate([prof_g * prof_s[s : s + 1] for s in range(cells_s)], axis=0)
        weights = jnp.concatenate([plane * push[c : c + 1] for c in range(3)], axis=0)
        return lax.dot_general(prof_w, weights, NT, precision=HIGH, preferred_element_type=jnp.float32)

    if shared:
        field_ref[...] = spread(elems[0][...] + pltpu.roll(elems[1][...], 48, 1))
    else:
        field_ref[...] = jnp.zeros_like(field_ref)

        def chunk(i, carry):
            field_ref[...] += spread(elems[0][i])
            return carry

        lax.fori_loop(0, elems[0].shape[0], chunk, 0)
    map_ref[...] = crow_ref[...]
    for m in range(EQ):
        value, values = None, []
        for j in range(STEPS):
            source = turned[m, pl.ds(j, 8, stride=STEPS), :]
            for c in range(3):
                source = source + lb_ref[m * EQ + 1 + c] * field_ref[8 * j : 8 * j + 8, c * columns : (c + 1) * columns]
            source = source * dru_ref[m, j]
            value = source if value is None else fu_ref[m, j] * value + source
            values.append(value)
        entry, _ = up_entry(gu_ref[m, STEPS - 1], value)
        values = [v + gu_ref[m, j] * entry for j, v in enumerate(values)]
        map_ref[UP * EQ + m : UP * EQ + m + 1] = values[-1][7:8]
        value = None
        for j in reversed(range(STEPS)):
            source = values[j] * rd_ref[m, j]
            value = source if value is None else fd_ref[m, j] * value + source
            values[j] = value
        entry, _ = down_entry(gd_ref[m, 0], value)
        for j in range(STEPS):
            values[j] = values[j] + gd_ref[m, j] * entry
            h_ref[m, j] = values[j]
        map_ref[DOWN * EQ + m : DOWN * EQ + m + 1] = values[0][0:1]


def close_kernel(count, *refs):
    maps = refs[:count]
    h_ref, gf_ref, pd_ref, rb_ref, spd_ref, out_ref, all_ref, modal, turned, ready, sem = refs[count:]
    here = lax.axis_index("wall")
    for r, ref in zip(rounds(count), maps):
        all_ref[source(here, r, count)] = ref[...]

    def get(j, kind):
        return all_ref[j, kind * EQ : (kind + 1) * EQ]

    ahead = jnp.maximum(spd_ref[:EQ], 0.0)
    back = jnp.maximum(-spd_ref[:EQ], 0.0)
    first = [all_ref[j, FIRST_VISC : FIRST_VISC + 1] for j in range(count)]
    last = [all_ref[j, LAST_VISC : LAST_VISC + 1] for j in range(count)]
    step = [all_ref[j, LAST_STEP : LAST_STEP + 1] for j in range(count)]
    share = [1.0 / (1.0 + step[j] * (ahead + last[j])) for j in range(count)]
    zero = jnp.zeros((EQ, LANES), jnp.float32)
    entry, entries, mine_up = zero, [], zero
    for j in range(count):
        if j > 0:
            entry = entry + first[j] / (ahead + first[j]) * get(j - 1, LSL)
        entries.append(entry)
        mine_up = jnp.where(here == j, entry, mine_up)
        entry = get(j, PN) * entry + get(j, UP)
        if j < count - 1:
            entry = entry + share[j] * step[j] * last[j] * get(j + 1, LSF)
    above, mine_down = zero, zero
    for j in reversed(range(count)):
        if j < count - 1:
            above = above + share[j] * last[j] / (back + last[j]) * get(j + 1, LSF)
        mine_down = jnp.where(here == j, above, mine_down)
        above = get(j, PD0) * above + get(j, G0) * entries[j] + get(j, DOWN)
    for m in range(EQ):
        up = jnp.broadcast_to(mine_up[m : m + 1], (8, LANES))
        down = jnp.broadcast_to(mine_down[m : m + 1], (8, LANES))
        for j in range(STEPS):
            modal[m, j] = h_ref[m, j] + gf_ref[m, j] * up + pd_ref[m, j] * down
    copies = []
    for k, group in enumerate(((0,), (1, 2), (3, 4, 5))):
        for q in group:
            weight = [rb_ref[q * EQ + m] for m in range(EQ)]
            for j in range(STEPS):
                total = weight[0] * modal[0, j]
                for m in range(1, EQ):
                    total = total + weight[m] * modal[m, j]
                turned[q, pl.ds(j, 8, stride=STEPS), :] = total
            ready[q] = jnp.transpose(turned[q])
        part = slice(group[0], group[-1] + 1)
        copy = pltpu.make_async_copy(ready.at[part], out_ref.at[part], sem.at[k])
        copy.start()
        copies.append(copy)
    for copy in copies:
        copy.wait()


def rounds(count):
    return sorted(range(count), key=lambda r: (r != 0, r != count - 1, r))


def source(here, r, count):
    if count & (count - 1) == 0:
        return here ^ r
    return (here + count - r) % count


def blocks(count_s, count_g, count_w, moves):
    pairs = []
    for s in range(count_s):
        for g in range(count_g):
            for w in range(count_w):
                at_s, at_g = moves[w % 2]
                target = ((s ^ at_s) * count_g + (g ^ at_g)) * count_w + w
                pairs.append(((s * count_g + g) * count_w + w, target))
    return pairs


def swaps(count, side):
    if side == 0:
        return [(i, i ^ 1) for i in range(count)]
    return [(i, (i + (1 if i % 2 else -1)) % count) for i in range(count)]


def local(
    state,
    advect,
    dtau,
    viscosity,
    mode_speed,
    left_modes,
    right_modes,
    source_jac,
    elem_owner,
    elem_tile,
    elem_offset,
    elem_height,
    elem_force,
    elem_width,
):
    f32 = jnp.float32
    cells = (state.shape[1], state.shape[2])
    cells_s, cells_g = cells
    columns = cells_s * cells_g
    count_s, count_g, count_w = (lax.axis_size(name) for name in ("stream", "girth", "wall"))
    held = elem_owner.shape[0]
    shared = count_s == 4 and count_g == 2 and count_w % 2 == 0 and held <= 8
    sides = 1 if count_g == 2 else 2
    extra = 8 if shared else 0
    ahead = (
        dtau.reshape(columns, LANES),
        viscosity.reshape(columns, LANES),
        mode_speed.reshape(1, EQ),
        left_modes,
        right_modes,
        source_jac,
        advect,
    )
    outs = [(EQ * 2 * cells_g + extra, LANES)] * 2
    outs += [(EQ * 2 * cells_s + extra, LANES)] * sides + [(8, LANES)] + [part.shape for part in ahead]
    packed = call(
        functools.partial(pack_kernel, cells, held, sides),
        outs,
        state,
        elem_owner.T,
        elem_tile.reshape(1, held),
        elem_offset.T,
        elem_height.reshape(1, held),
        elem_force.T,
        elem_width.reshape(1, held),
        *ahead,
        scratch=[((1, held), jnp.int32), ((1, held), jnp.int32), ((2, held), f32), ((1, held), f32)]
        + [((3, held), f32), ((1, held), f32)],
        far=range(7 + AHEAD),
        copies=sides + 8 + AHEAD,
    )
    pay, ahead = packed[2 + sides], packed[3 + sides :]
    halo_a = lax.ppermute(packed[0], "stream", swaps(count_s, 0))
    halo_b = lax.ppermute(packed[1], "stream", swaps(count_s, 1))
    halo_g = [lax.ppermute(packed[2 + i], "girth", swaps(count_g, i)) for i in range(sides)]
    if shared:
        every = ("stream", "girth", "wall")
        far = [
            lax.ppermute(pay, every, blocks(count_s, count_g, count_w, moves))
            for moves in (((1, 1), (2, 1)), ((2, 0), (3, 1)))
        ]
    wide = (EQ, STEPS, 8, LANES)
    r0, adv, lb, rb, fu, gu, fd, gd, dru, rd, gf, pd, crow, spd = call(
        functools.partial(coef_kernel, cells),
        [(EQ * columns, LANES), (2, columns, LANES), (EQ * EQ, 8, LANES), (EQ * EQ, 8, LANES)]
        + [wide] * 8
        + [(MAP_ROWS, LANES), (8, LANES)],
        *ahead,
        state.reshape(EQ * columns, LANES),
        scratch=[((2, LANES, columns), f32), ((EQ, 8, LANES), f32)],
        cost=4 << 20,
    )
    if shared:
        (pair,) = call(pair_kernel, [(8, LANES)], *far, crow)
        other = lax.ppermute(pair, "wall", [(i, i ^ 1) for i in range(count_w)])
    *kept, turned = call(
        functools.partial(halo_kernel, cells, (count_s, count_g), sides),
        [(8, LANES)] * shared + [(EQ, LANES, columns)],
        halo_a, halo_b, *halo_g, r0, adv, lb, *((pay, pair) if shared else ()),
        scratch=[((EQ * columns, LANES), f32)],
        cost=1 << 20,
    )
    elems = (*kept, other) if shared else (lax.all_gather(pay, ("stream", "girth")),)
    h, block_map = call(
        functools.partial(sweep_kernel, cells, count_g, shared),
        [wide, (MAP_ROWS, LANES)],
        turned, lb, fu, gu, fd, gd, dru, rd, crow, *elems,
        scratch=[((LANES, 3 * columns), f32)],
        cost=1 << 20,
    )
    maps = [block_map]
    for r in range(1, count_w):
        pairs = [(int(source(i, r, count_w)), i) for i in range(count_w)]
        maps.append(lax.ppermute(block_map, "wall", pairs))
    (out,) = call(
        functools.partial(close_kernel, count_w),
        [(EQ, columns, LANES)],
        *[maps[r] for r in rounds(count_w)], h, gf, pd, rb, spd,
        scratch=[((count_w, MAP_ROWS, LANES), f32), (wide, f32), ((EQ, LANES, columns), f32)]
        + [((EQ, columns, LANES), f32)],
        cost=1 << 20,
        far_out=(0,),
        copies=3,
    )
    return out.reshape(state.shape)


def solution(mesh):
    in_specs = (
        P(None, "stream", "girth", "wall"),
        P(None, "stream", "girth"),
        P("stream", "girth", "wall"),
        P("stream", "girth", "wall"),
        P(),
        P(),
        P(),
        P(),
        P(("stream", "girth"), None),
        P(("stream", "girth")),
        P(("stream", "girth"), None),
        P(("stream", "girth")),
        P(("stream", "girth"), None),
        P(("stream", "girth")),
    )
    out_specs = P(None, "stream", "girth", "wall")
    return jax.shard_map(local, mesh=mesh, in_specs=in_specs, out_specs=out_specs, check_vma=False)
```
